512 devices in a mesh: box: 128 (over z, y, core), col: 4 (over x).
Axes of the slice: x: 4, y: 8, z: 8, core: 2. Of those that a mesh axis runs over, the one named last changes fastest.
Arguments:
- basis: float32 [4, 2, 64, 65536], P(None, None, 'col', 'box'), may hold values from -1000 to 1000
- offsets: float32 [3, 65536], P(None, 'box'), may hold values from -0.5 to 0.5
- weights: float32 [65536], P('box'), may hold values from 0.03 to 0.3
- interp: float32 [512, 32, 128], P('box'), may hold values from 0 to 1
- skeleton: int32 [512, 32], P('box'), may hold values from 0 to 127, as said below
- near_boxes: int32 [512, 27], P('box'), may hold values from 0 to 511, as said below
- near_count: int32 [512], P('box'), may hold values from 3 to 27, as said below
Outputs:
- new_block: float32 [2, 64, 65536], P(None, 'col', 'box')
- coupling: float32 [4, 64, 64], replicated
- factor: float32 [64, 64], replicated
The draws below stay inside these ranges and needn't reach their ends.
Inputs may be any that keep to these rules, and one draw needn't show every extreme that they name: `skeleton`: each row holds 32 different points of the box. `near_boxes`: entry 0 of box b's row is b itself, entry 1 is b + 4 and entry 2 is b - 4, both clipped to the boxes; every entry lies within 4 boxes of b. Box b's near field is the first near_count[b] entries of its row of near_boxes.
All inputs are finite; a program needn't handle non-finite values.
Results may differ from the reference program's by a relative error of at most 0.0003.
Values sent between devices are 32-bit elements; how exact they have to be, the bound alone decides.
No kernel may reach another device: no remote copies, remote signals or barrier semaphores. Data moves between devices by JAX's collectives and lax.ppermute only.
A program may use at most 64 MiB of HBM per device.

```python
import math
import jax
import jax.numpy as jnp
from jax import lax

BOX_DEV = 4
P_SIZE = 128
K = 32
NEAR = 27
NC = 64
NPREV = 4
NB = 512
N = 65536


def draw_basis(key, part):
    key_list = jax.random.split(jax.random.fold_in(key, 101), 4)
    shared = jax.random.normal(key_list[0], (1, 2, NC, N), jnp.float32)
    private = jax.random.normal(key_list[1], (NPREV, 2, NC, N), jnp.float32)
    position = 1.0 - (jnp.arange(N, dtype=jnp.int32) // P_SIZE).astype(jnp.float32) / max(NB - 1, 1)
    row_scale = 1.0 + 2.0 * position
    column_scale = 10.0 ** (0.5 * jax.random.uniform(key_list[3], (1, 1, NC, 1), jnp.float32))
    mixing = 0.6
    level = 1.0
    values = (mixing * shared + math.sqrt(1.0 - mixing * mixing) * private + level) * row_scale * column_scale
    return values.astype(jnp.float32)


def draw_skeleton(key, part):
    key_list = jax.random.split(jax.random.fold_in(key, 202), NB)
    orders = jax.vmap(lambda one_key: jax.random.permutation(one_key, P_SIZE))(key_list)
    return orders[:, :K].astype(jnp.int32)


def draw_near_boxes(key, part):
    own_box = jnp.arange(NB, dtype=jnp.int32)[:, None]
    offset = jax.random.randint(jax.random.fold_in(key, 303), (NB, NEAR), -BOX_DEV, BOX_DEV + 1, dtype=jnp.int32)
    slot_index = jnp.arange(NEAR, dtype=jnp.int32)[None, :]
    offset = jnp.where(slot_index == 0, 0, offset)
    offset = jnp.where(slot_index == 1, BOX_DEV, offset)
    offset = jnp.where(slot_index == 2, -BOX_DEV, offset)
    return jnp.clip(own_box + offset, 0, NB - 1).astype(jnp.int32)


def draw_near_count(key, part):
    spread_levels = NEAR - 3
    draw_level = jax.random.randint(jax.random.fold_in(key, 404), (NB,), 0, spread_levels + 1, dtype=jnp.int32)
    near_total = 3 + draw_level * draw_level * draw_level // max(spread_levels * spread_levels, 1)
    return jnp.where(jnp.arange(NB, dtype=jnp.int32) == 0, NEAR, near_total).astype(jnp.int32)


def steps_of(own_key, extent, shards, low, high):
    def one(dim, parts):
        heights = jax.random.uniform(jax.random.fold_in(jax.random.fold_in(own_key, 6), dim), (parts,), jnp.float32, low / len(shards), high / len(shards))
        return jnp.repeat(jnp.exp(heights), extent[dim] // parts).reshape((-1,) + (1,) * (len(extent) - dim - 1))

    factor_of = one(*shards[0])
    for cut in shards[1:]:
        factor_of = factor_of * one(*cut)
    return factor_of


def setup_inputs(seed: int = 0) -> dict:
    streams_of = jax.random.split(jax.random.key(seed), 8)
    return {
        "basis": draw_basis(jax.random.fold_in(streams_of[7], 71), 0),
        "offsets": jnp.clip(jax.random.uniform(streams_of[1], (3, N), jnp.float32, -0.5, 0.5) * steps_of(streams_of[1], (3, N), ((1, 128),), -0.4, 0.0), -0.5, 0.5),
        "weights": jnp.clip(jnp.exp(math.log(0.3) - 2.3025852 * jax.random.uniform(streams_of[2], (N,), jnp.float32) ** steps_of(streams_of[2], (N,), ((0, 128),), -0.2, 0.2)), 0.03, 0.3),
        "interp": jnp.clip(1.0 * jax.random.uniform(streams_of[3], (NB, K, P_SIZE), jnp.float32) ** steps_of(streams_of[3], (NB, K, P_SIZE), ((0, 128),), -0.2, 0.2), 0.0, 1.0),
        "skeleton": draw_skeleton(jax.random.fold_in(streams_of[7], 71), 0),
        "near_boxes": draw_near_boxes(jax.random.fold_in(streams_of[7], 71), 0),
        "near_count": draw_near_count(jax.random.fold_in(streams_of[7], 71), 0),
    }


WAVENUMBER = 6.0
SMOOTHING = 0.1
SHIFT_SCALE = 0.02
EPSILON = 1e-06
HIGHEST = lax.Precision.HIGHEST

def box_centers(box_index):
    along_band = (box_index // BOX_DEV).astype(jnp.float32)
    across = (box_index % BOX_DEV).astype(jnp.float32)
    return jnp.stack([along_band, across, jnp.zeros_like(along_band)])

def helmholtz_pair(targets, sources):
    spread = SMOOTHING * SMOOTHING
    for axis_index in range(3):
        spread = spread + (targets[axis_index][..., :, None] - sources[axis_index][..., None, :]) ** 2
    distance = jnp.sqrt(spread)
    factor = 1.0 / (4.0 * math.pi * distance)
    return (jnp.cos(WAVENUMBER * distance) * factor, jnp.sin(WAVENUMBER * distance) * factor)

def apply_pair(kernel_re, kernel_im, values):
    real_part = jnp.einsum('tq,cq->ct', kernel_re, values[0], precision=HIGHEST) - jnp.einsum('tq,cq->ct', kernel_im, values[1], precision=HIGHEST)
    imag_part = jnp.einsum('tq,cq->ct', kernel_im, values[0], precision=HIGHEST) + jnp.einsum('tq,cq->ct', kernel_re, values[1], precision=HIGHEST)
    return jnp.stack([real_part, imag_part])

def reference(basis, offsets, weights, interp, skeleton, near_boxes, near_count):
    box_index = jnp.arange(NB, dtype=jnp.int32)
    positions = offsets.reshape(3, NB, P_SIZE) + box_centers(box_index)[:, :, None]
    current = basis[NPREV - 1]
    sources = (current * weights).reshape(2, NC, NB, P_SIZE)
    slot_range = jnp.arange(NEAR, dtype=jnp.int32)

    def near_box(box_id):
        listed = near_boxes[box_id]
        live_slot = (slot_range < near_count[box_id]).astype(jnp.float32)
        source_pos = positions[:, listed, :].reshape(3, NEAR * P_SIZE)
        source_val = (sources[:, :, listed, :] * live_slot[None, None, :, None]).reshape(2, NC, NEAR * P_SIZE)
        kernel_re, kernel_im = helmholtz_pair(positions[:, box_id, :], source_pos)
        return apply_pair(kernel_re, kernel_im, source_val)
    near_field = lax.map(near_box, box_index)
    charges = jnp.einsum('bkq,pcbq->pcbk', interp, sources, precision=HIGHEST).reshape(2, NC, NB * K)
    skel_grid = jnp.take_along_axis(positions, jnp.broadcast_to(skeleton[None], (3, NB, K)), axis=2)
    skel_flat = skel_grid.reshape(3, NB * K)

    def far_box(box_id):
        live_slot = slot_range < near_count[box_id]
        listed = jnp.any((near_boxes[box_id][:, None] == box_index[None, :]) & live_slot[:, None], axis=0)
        far_weight = jnp.repeat(1.0 - listed.astype(jnp.float32), K)
        kernel_re, kernel_im = helmholtz_pair(skel_grid[:, box_id, :], skel_flat)
        return apply_pair(kernel_re * far_weight[None, :], kernel_im * far_weight[None, :], charges)
    potentials = lax.map(far_box, box_index)
    far_field = jnp.einsum('bkq,bpck->bpcq', interp, potentials, precision=HIGHEST)
    applied = 0.5 * current + (near_field + far_field).transpose(1, 2, 0, 3).reshape(2, NC, N)
    coupling = jnp.einsum('kpiq,pjq->kij', basis, applied, precision=HIGHEST) / N
    residual = applied - jnp.einsum('kpiq,kij->pjq', basis, coupling, precision=HIGHEST)
    gram_matrix = jnp.einsum('piq,pjq->ij', residual, residual, precision=HIGHEST) / N
    shift_term = SHIFT_SCALE * jnp.trace(gram_matrix) / NC + EPSILON
    lower_factor = jnp.linalg.cholesky(gram_matrix + shift_term * jnp.eye(NC, dtype=jnp.float32))
    flat_rows = residual.transpose(1, 0, 2).reshape(NC, 2 * N)
    solved = jax.scipy.linalg.solve_triangular(lower_factor, flat_rows, lower=True)
    new_block = solved.reshape(NC, 2, N).transpose(1, 0, 2)
    return (new_block, coupling, lower_factor.T)
```

```python
import functools
import math

import jax
import jax.numpy as jnp
from jax import lax
from jax.experimental import pallas as pl
from jax.experimental.pallas import tpu as pltpu
from jax.sharding import Mesh
from jax.sharding import PartitionSpec as P

BOX_DEV = 4
PTS = 128
SKEL = 32
SLOTS = 27
REACH = 4
WAVENUMBER = 6.0
SMOOTHING = 0.1
SHIFT_SCALE = 0.02
EPSILON = 1e-06
HIGHEST = lax.Precision.HIGHEST
F32 = jnp.float32
BF16 = jnp.bfloat16
INTERPRET = False

GRID = (8, 8, 2)
BOX = ("z", "y", "k")
YK = ("y", "k")
ZX = ("z", "x")

TURNS = WAVENUMBER / (2.0 * math.pi)
SIN_C = (3.1415926401307073, -5.167710083507923, 2.5500775232148563, -0.5982912856211671, 0.07765766030589402)
COS_C = (
    0.9999999997799043,
    -4.934802137078822,
    4.0587091595560825,
    -1.335212003047854,
    0.2349373138047365,
    -0.02439632433202294,
)


def poly(coefs, u):
    r = coefs[-1] * u + coefs[-2]
    for c in coefs[-3::-1]:
        r = r * u + c
    return r


def helmholtz(tx, ty, tz, sx, sy, sz, weight):
    dx = tx - sx
    dy = ty - sy
    dz = tz - sz
    s = SMOOTHING * SMOOTHING + dx * dx + dy * dy + dz * dz
    r = lax.rsqrt(s)
    r = r * (1.5 - (0.5 * s) * (r * r))
    t = (s * r) * TURNS
    f = t - lax.round(t, lax.RoundingMethod.TO_NEAREST_EVEN)
    u = f * f
    sn = f * poly(SIN_C, u)
    cs = poly(COS_C, u)
    two = sn + sn
    w = r * weight
    return (1.0 - two * sn) * w, (two * cs) * w


def split(x):
    hi = x.astype(BF16)
    return hi, (x - hi.astype(F32)).astype(BF16)


def dot(a, b, ca, cb, precision=None):
    return lax.dot_general(
        a, b, (((ca,), (cb,)), ((), ())), precision=precision, preferred_element_type=F32
    )


def rotate(rows):
    parts = []
    for g in range(rows.shape[0] // 32):
        parts.append(-rows[32 * g + 16 : 32 * g + 32])
        parts.append(rows[32 * g : 32 * g + 16])
    return jnp.concatenate(parts, axis=0)


def group_index(dims):
    return (lax.axis_index("z") * dims[1] + lax.axis_index("y")) * dims[2] + lax.axis_index("k")


def call(kernel, out_shape, in_specs, scratch=(), flops=0, name=None):
    vmem = pl.BlockSpec(memory_space=pltpu.VMEM)
    single = not isinstance(out_shape, (tuple, list))
    return pl.pallas_call(
        kernel,
        out_shape=out_shape,
        in_specs=in_specs,
        out_specs=vmem if single else [vmem] * len(out_shape),
        scratch_shapes=list(scratch),
        cost_estimate=pl.CostEstimate(flops=flops, bytes_accessed=1 << 19, transcendentals=0),
        interpret=INTERPRET,
        name=name,
    )


VMEM = pl.BlockSpec(memory_space=pltpu.VMEM)
SMEM = pl.BlockSpec(memory_space=pltpu.SMEM)


def prep_kernel(idx, near, count, cur, weights, offsets, interp, skel, halo, far, info):
    i = idx[0].astype(F32)
    x = idx[1]
    src = cur[...] * weights[...]
    halo[0:32, :] = src
    centre = lax.broadcasted_iota(jnp.int32, (8, 1), 0)
    charges = []
    spots = []
    for b in range(BOX_DEV):
        cols = slice(PTS * b, PTS * b + PTS)
        shift = jnp.where(centre == 0, i, jnp.where(centre == 1, float(b), 0.0))
        pos = jnp.concatenate([offsets[:, cols], jnp.zeros((5, PTS), F32)], axis=0) + shift
        halo[32:40, cols] = pos
        charges.append(dot(src[:, cols], interp[b], 1, 1, HIGHEST))
        q = lax.broadcasted_iota(jnp.int32, (PTS, SKEL), 0)
        pick = (q == skel[b : b + 1, :]).astype(F32)
        spots.append(dot(pos, pick, 1, 0, HIGHEST))
    far[0:32, :] = jnp.concatenate(charges, axis=1)
    far[32:40, :] = jnp.concatenate(spots, axis=1)
    row = lax.broadcasted_iota(jnp.int32, (8, PTS), 0)
    lane = lax.broadcasted_iota(jnp.int32, (8, PTS), 1)
    box_of = BOX_DEV * (idx[0] + row - 1) + lane // SKEL
    listed = jnp.zeros((8, PTS), F32)
    for s in range(SLOTS):
        box = jnp.where(s < count[x], near[x, s], -1000)
        listed = jnp.where(box_of == box, 1.0, listed)
    spot = spots[0]
    for b in range(1, BOX_DEV):
        spot = jnp.where(x == b, spots[b], spot)
    info[...] = jnp.concatenate(
        [
            jnp.concatenate([spot[0:3], jnp.zeros((3, PTS - SKEL), F32)], axis=1),
            1.0 - listed[0:3],
            jnp.zeros((2, PTS), F32),
        ],
        axis=0,
    )


def near_kernel(idx, near, count, prev, own, nxt, cur, out, ext, mult, tpos, acc):
    for e in range(BOX_DEV):
        cols = slice(PTS * e, PTS * e + PTS)
        ext[e] = prev[:, cols]
        ext[BOX_DEV + e] = own[:, cols]
        ext[2 * BOX_DEV + e] = nxt[:, cols]
    stack = jnp.concatenate(
        [own[32:40, PTS * t : PTS * t + PTS] for t in range(BOX_DEV)]
        + [jnp.zeros((PTS - 8 * BOX_DEV, PTS), F32)],
        axis=0,
    )
    turned = stack.T
    base = BOX_DEV * (idx[0] - 1)
    erow = lax.broadcasted_iota(jnp.int32, (16, PTS), 0)
    for t in range(BOX_DEV):
        for c in range(3):
            tpos[t, c] = jnp.broadcast_to(turned[:, 8 * t + c : 8 * t + c + 1], (PTS, PTS))
        m = jnp.zeros((16, PTS), F32)
        for s in range(SLOTS):
            box = jnp.where(s < count[t], near[t, s] - base, -1000)
            m = m + jnp.where(erow == box, 1.0, 0.0)
        mult[t] = m
    acc[...] = jnp.zeros_like(acc)

    def step(d, carry):
        for t in range(BOX_DEV):
            e = t + d
            rows = ext[e, 0:32, :]
            re, im = helmholtz(
                tpos[t, 0],
                tpos[t, 1],
                tpos[t, 2],
                ext[e, 32:33, :],
                ext[e, 33:34, :],
                ext[e, 34:35, :],
                0.25 / math.pi,
            )
            khi, klo = split(jnp.concatenate([re, im], axis=1))
            rhi, rlo = split(jnp.concatenate([rows, rotate(rows)], axis=1))
            both = dot(jnp.concatenate([rhi, rlo], axis=0), khi, 1, 1)
            part = both[0:32] + (both[32:64] + dot(rhi, klo, 1, 1))
            acc[t] += part * mult[t, pl.ds(e, 1), :]
        return carry

    lax.fori_loop(0, 2 * REACH + 1, step, 0)
    for t in range(BOX_DEV):
        out[t] = 0.5 * cur[:, PTS * t : PTS * t + PTS] + acc[t]


def far_kernel(dims, idx, info, gathered, out, tpos, rhi, rlo, weight, acc):
    nz, ny, nk, nx = dims
    targets = ny * nk
    stack = jnp.concatenate([info[d] for d in range(targets)], axis=0)
    if targets * 8 < PTS:
        stack = jnp.concatenate([stack, jnp.zeros((PTS - targets * 8, PTS), F32)], axis=0)
    turned = stack.T
    for d in range(targets):
        for c in range(3):
            tpos[c, SKEL * d : SKEL * d + SKEL, :] = jnp.broadcast_to(
                turned[0:SKEL, 8 * d + c : 8 * d + c + 1], (SKEL, PTS)
            )
    for g in range(nz):
        rows = jnp.concatenate([gathered[nx * g + c, 0:32, :] for c in range(nx)], axis=0)
        hi, lo = split(jnp.concatenate([rows, rotate(rows)], axis=1))
        rhi[g] = hi
        rlo[g] = lo
    acc[...] = jnp.zeros_like(acc)
    per = min(4, targets)

    def step(g, carry):
        sx = gathered[nx * g, 32:33, :]
        sy = gathered[nx * g, 33:34, :]
        sz = gathered[nx * g, 34:35, :]
        source_group = g * targets + idx[1]
        for d in range(targets):
            delta = source_group - (idx[0] + d)
            w = jnp.where(delta == -1, info[d, 3:4, :], 1.0)
            w = jnp.where(delta == 0, info[d, 4:5, :], w)
            w = jnp.where(delta == 1, info[d, 5:6, :], w)
            weight[SKEL * d : SKEL * d + SKEL, :] = jnp.broadcast_to(
                w * (0.25 / math.pi), (SKEL, PTS)
            )
        for n in range(targets // per):
            span = slice(SKEL * per * n, SKEL * per * (n + 1))
            re, im = helmholtz(
                tpos[0, span, :],
                tpos[1, span, :],
                tpos[2, span, :],
                sx,
                sy,
                sz,
                weight[span, :],
            )
            khi, klo = split(jnp.concatenate([re, im], axis=1))
            acc[span, :] += dot(khi, rhi[g], 1, 1) + (
                dot(khi, rlo[g], 1, 1) + dot(klo, rhi[g], 1, 1)
            )
        return carry

    lax.fori_loop(0, nz, step, 0)
    for d in range(targets):
        out[d] = acc[SKEL * d : SKEL * d + SKEL, :]


def halves(rows, nx):
    re = jnp.concatenate([rows[32 * c : 32 * c + 16] for c in range(nx)], axis=0)
    im = jnp.concatenate([rows[32 * c + 16 : 32 * c + 32] for c in range(nx)], axis=0)
    return jnp.concatenate([re, im], axis=1)


def couple_kernel(dims, scale, idx, phi, nearf, interp, basis, applied, stacked, part):
    nx = dims[3]
    total = phi[0]
    for d in range(1, phi.shape[0]):
        total = total + phi[d]
    rows = dot(total, interp[idx[2]], 0, 0, HIGHEST)
    rows = rows + jnp.concatenate([nearf[c] for c in range(nx)], axis=0)
    a2 = halves(rows, nx)
    applied[...] = a2
    blocks = []
    for k in range(4):
        b2 = halves(jnp.concatenate([basis[c, 32 * k : 32 * k + 32, :] for c in range(nx)], axis=0), nx)
        stacked[64 * k : 64 * k + 64, :] = b2
        blocks.append(dot(b2, a2, 1, 1, HIGHEST) * scale)
    left = jnp.concatenate(blocks[0:2], axis=0)
    right = jnp.concatenate(blocks[2:4], axis=0)
    packed = jnp.concatenate([left, right], axis=1)
    n = part.shape[0]
    for d in range(n):
        part[d] = packed[8 * d : 8 * d + 8, :]


def residual_kernel(scale, coup, applied, stacked, residual, part, coupling):
    n = coup.shape[0]
    packed = jnp.concatenate([coup[d] for d in range(n)], axis=0)
    c = jnp.concatenate([packed[:, 0:64], packed[:, 64:128]], axis=0)
    for k in range(4):
        coupling[k] = c[64 * k : 64 * k + 64]
    res = applied[...] - dot(c, stacked[...], 0, 0, HIGHEST)
    residual[...] = res
    gram = dot(res, res, 1, 1, HIGHEST) * scale
    both = jnp.concatenate([gram[0:32], gram[32:64]], axis=1)
    per = 32 // n
    for d in range(n):
        part[d] = jnp.concatenate(
            [both[per * d : per * d + per], jnp.zeros((8 - per, PTS), F32)], axis=0
        )


def finish_kernel(dims, idx, gram, residual, out, factor, inv):
    nx = dims[3]
    n = gram.shape[0]
    per = 32 // n
    both = jnp.concatenate([gram[d, 0:per, :] for d in range(n)], axis=0)
    g = jnp.concatenate([both[:, 0:64], both[:, 64:128]], axis=0)
    row = lax.broadcasted_iota(jnp.int32, (64, 64), 0)
    col = lax.broadcasted_iota(jnp.int32, (64, 64), 1)
    eye = row == col
    diag = jnp.where(eye, g, 0.0)
    trace = jnp.sum(jnp.sum(diag, axis=1, keepdims=True), axis=0, keepdims=True)
    g = g + jnp.where(eye, SHIFT_SCALE * trace / 64.0 + EPSILON, 0.0)
    m = jnp.concatenate([g, eye.astype(F32)], axis=1)
    sub = lax.broadcasted_iota(jnp.int32, (64, 1), 0)
    for j in range(63):
        line = m[j : j + 1, :]
        f = jnp.where(sub > j, m[:, j : j + 1] / line[:, j : j + 1], 0.0)
        m = m - f * line
    pivots = jnp.sum(jnp.where(eye, m[:, 0:64], 0.0), axis=1, keepdims=True)
    root = 1.0 / jnp.sqrt(pivots)
    m = m * root
    factor[...] = jnp.where(row <= col, m[:, 0:64], 0.0)
    inv[...] = m[:, 64:128]
    mine = inv[pl.ds(pl.multiple_of(16 * idx[2], 16), 16), :]
    for b in range(nx):
        rows = dot(mine, residual[b], 1, 0, HIGHEST)
        out[0, :, PTS * b : PTS * b + PTS] = rows[:, 0:PTS]
        out[1, :, PTS * b : PTS * b + PTS] = rows[:, PTS : 2 * PTS]


def share(value, axes, count):
    return lax.all_to_all(
        jnp.broadcast_to(value[None], (count,) + value.shape),
        axes,
        split_axis=0,
        concat_axis=0,
        tiled=True,
    )


def trade(value, axes):
    return lax.all_to_all(value, axes, split_axis=0, concat_axis=0, tiled=True)


def all_sum(part, dims):
    nz, ny, nk, nx = dims
    mine = jnp.sum(trade(part, YK), axis=0)
    mine = jnp.sum(share(mine, ZX, nz * nx), axis=0)
    return share(mine, YK, ny * nk)


def shards(dims, basis, offsets, weights, interp, skeleton, near_boxes, near_count):
    nz, ny, nk, nx = dims
    box_dims = dims[:3]
    groups = nz * ny * nk
    targets = ny * nk
    row_total = groups * BOX_DEV * PTS
    group = group_index(box_dims)
    col = lax.axis_index("x")
    idx_prep = jnp.stack([group, col]).astype(jnp.int32)
    idx_far = jnp.stack(
        [
            lax.axis_index("z") * targets,
            lax.axis_index("y") * nk + lax.axis_index("k"),
            col,
        ]
    ).astype(jnp.int32)
    cur = basis[3].reshape(32, BOX_DEV * PTS)
    shape = lambda *s: jax.ShapeDtypeStruct(s, F32)

    with jax.named_scope("prep"):
        halo, far, info = call(
            prep_kernel,
            (shape(40, BOX_DEV * PTS), shape(40, PTS), shape(8, PTS)),
            [SMEM, SMEM, SMEM] + [VMEM] * 5,
            name="prep",
        )(idx_prep, near_boxes, near_count, cur, weights[None], offsets, interp, skeleton)

    with jax.named_scope("info"):
        info_all = share(info, YK, targets)
    with jax.named_scope("gather"):
        far_all = share(far, ZX, nz * nx)
    with jax.named_scope("halo"):
        prev = lax.ppermute(halo, BOX, [(g, g + 1) for g in range(groups - 1)])
        nxt = lax.ppermute(halo, BOX, [(g + 1, g) for g in range(groups - 1)])
    with jax.named_scope("basis"):
        mixed = basis.reshape(4 * 32, BOX_DEV, PTS).transpose(1, 0, 2)
        basis_rows = trade(mixed, "x")

    with jax.named_scope("near"):
        near_part = call(
            near_kernel,
            shape(BOX_DEV, 32, PTS),
            [SMEM, SMEM, SMEM] + [VMEM] * 4,
            [
                pltpu.VMEM((3 * BOX_DEV, 40, PTS), F32),
                pltpu.VMEM((BOX_DEV, 16, PTS), F32),
                pltpu.VMEM((BOX_DEV, 3, PTS, PTS), F32),
                pltpu.VMEM((BOX_DEV, 32, PTS), F32),
            ],
            flops=36 * 2 * 64 * 256 * 128 * 2,
            name="near",
        )(idx_prep, near_boxes, near_count, prev, halo, nxt, cur)
        near_rows = trade(near_part, "x")

    with jax.named_scope("far"):
        far_part = call(
            functools.partial(far_kernel, dims),
            shape(targets, SKEL, 32 * nx),
            [SMEM, VMEM, VMEM],
            [
                pltpu.VMEM((3, SKEL * targets, PTS), F32),
                pltpu.VMEM((nz, 32 * nx, 2 * PTS), BF16),
                pltpu.VMEM((nz, 32 * nx, 2 * PTS), BF16),
                pltpu.VMEM((SKEL * targets, PTS), F32),
                pltpu.VMEM((SKEL * targets, 32 * nx), F32),
            ],
            flops=3 * 2 * 512 * 2048 * 128,
            name="far",
        )(idx_far, info_all, far_all)
        phi = trade(far_part, YK)

    with jax.named_scope("couple"):
        applied, stacked, part = call(
            functools.partial(couple_kernel, dims, 1.0 / row_total),
            (shape(64, 2 * PTS), shape(256, 2 * PTS), shape(16, 8, PTS)),
            [SMEM] + [VMEM] * 4,
            name="couple",
        )(idx_far, phi, near_rows, interp, basis_rows)
        if targets != 16:
            part = part.reshape(targets, 128 // targets, PTS)
        coup = all_sum(part, dims).reshape(16, 8, PTS)

    with jax.named_scope("residual"):
        residual, part, coupling = call(
            functools.partial(residual_kernel, 1.0 / row_total),
            (shape(64, 2 * PTS), shape(16, 8, PTS), shape(4, 64, 64)),
            [VMEM] * 3,
            name="residual",
        )(coup, applied, stacked)
        if targets != 16:
            part = part.reshape(targets, 128 // targets, PTS)
        residual_all = share(residual, "x", nx)
        gram = all_sum(part, dims).reshape(16, 8, PTS)

    with jax.named_scope("finish"):
        new_block, factor = call(
            functools.partial(finish_kernel, dims),
            (shape(2, 16, BOX_DEV * PTS), shape(64, 64)),
            [SMEM, VMEM, VMEM],
            [pltpu.VMEM((64, 64), F32)],
            name="finish",
        )(idx_far, gram, residual_all)
    return new_block, coupling, factor


def solution(mesh):
    boxes, cols = mesh.devices.shape
    nk = GRID[2]
    ny = GRID[1] if boxes == math.prod(GRID) else 2
    nz = boxes // (ny * nk)
    dims = (nz, ny, nk, cols)
    fine = Mesh(mesh.devices.reshape(dims), ("z", "y", "k", "x"))
    return jax.shard_map(
        functools.partial(shards, dims),
        mesh=fine,
        in_specs=(
            P(None, None, "x", BOX),
            P(None, BOX),
            P(BOX),
            P(BOX, None, None),
            P(BOX, None),
            P(BOX, None),
            P(BOX),
        ),
        out_specs=(P(None, "x", BOX), P(), P()),
        check_vma=False,
    )
```

```python
import functools
import math

import jax
import jax.numpy as jnp
from jax import lax
from jax.experimental import pallas as pl
from jax.experimental.pallas import tpu as pltpu
from jax.sharding import Mesh
from jax.sharding import PartitionSpec as P

BOX_DEV = 4
PTS = 128
SKEL = 32
SLOTS = 27
REACH = 4
WAVENUMBER = 6.0
SMOOTHING = 0.1
SHIFT_SCALE = 0.02
EPSILON = 1e-06
HIGHEST = lax.Precision.HIGHEST
F32 = jnp.float32
BF16 = jnp.bfloat16
INTERPRET = False

GRID = (8, 8, 2)
BOX = ("z", "y", "k")
YK = ("y", "k")
ZX = ("z", "x")

TURNS = WAVENUMBER / (2.0 * math.pi)
SIN_C = (3.1415926401307073, -5.167710083507923, 2.5500775232148563, -0.5982912856211671, 0.07765766030589402)
COS_C = (
    0.9999999997799043,
    -4.934802137078822,
    4.0587091595560825,
    -1.335212003047854,
    0.2349373138047365,
    -0.02439632433202294,
)


def poly(coefs, u):
    r = coefs[-1] * u + coefs[-2]
    for c in coefs[-3::-1]:
        r = r * u + c
    return r


def helmholtz(tx, ty, tz, sx, sy, sz, weight):
    dx = tx - sx
    dy = ty - sy
    dz = tz - sz
    s = SMOOTHING * SMOOTHING + dx * dx + dy * dy + dz * dz
    r = lax.rsqrt(s)
    r = r * (1.5 - (0.5 * s) * (r * r))
    t = (s * r) * TURNS
    f = t - lax.round(t, lax.RoundingMethod.TO_NEAREST_EVEN)
    u = f * f
    sn = f * poly(SIN_C, u)
    cs = poly(COS_C, u)
    two = sn + sn
    w = r * weight
    return (1.0 - two * sn) * w, (two * cs) * w


def split(x):
    hi = x.astype(BF16)
    return hi, (x - hi.astype(F32)).astype(BF16)


def dot(a, b, ca, cb, precision=None):
    return lax.dot_general(
        a, b, (((ca,), (cb,)), ((), ())), precision=precision, preferred_element_type=F32
    )


def rotate(rows):
    parts = []
    for g in range(rows.shape[0] // 32):
        parts.append(-rows[32 * g + 16 : 32 * g + 32])
        parts.append(rows[32 * g : 32 * g + 16])
    return jnp.concatenate(parts, axis=0)


def group_index(dims):
    return (lax.axis_index("z") * dims[1] + lax.axis_index("y")) * dims[2] + lax.axis_index("k")


def call(kernel, out_shape, in_specs, scratch=(), flops=0):
    vmem = pl.BlockSpec(memory_space=pltpu.VMEM)
    single = not isinstance(out_shape, (tuple, list))
    return pl.pallas_call(
        kernel,
        out_shape=out_shape,
        in_specs=in_specs,
        out_specs=vmem if single else [vmem] * len(out_shape),
        scratch_shapes=list(scratch),
        cost_estimate=pl.CostEstimate(flops=flops, bytes_accessed=1 << 19, transcendentals=0),
        interpret=INTERPRET,
    )


VMEM = pl.BlockSpec(memory_space=pltpu.VMEM)
SMEM = pl.BlockSpec(memory_space=pltpu.SMEM)


def centred(offsets, b, group):
    axis = lax.broadcasted_iota(jnp.int32, (8, 1), 0)
    shift = jnp.where(axis == 0, group.astype(F32), jnp.where(axis == 1, float(b), 0.0))
    cols = slice(PTS * b, PTS * b + PTS)
    return jnp.concatenate([offsets[:, cols], jnp.zeros((5, PTS), F32)], axis=0) + shift


def place_kernel(dims, near, count, offsets, skel, info, skelpos):
    group = group_index(dims)
    x = lax.axis_index("x")
    spots = []
    for b in range(BOX_DEV):
        q = lax.broadcasted_iota(jnp.int32, (PTS, SKEL), 0)
        pick = (q == skel[b : b + 1, :]).astype(F32)
        spots.append(dot(centred(offsets, b, group), pick, 1, 0, HIGHEST))
    skelpos[...] = jnp.concatenate(spots, axis=1)
    row = lax.broadcasted_iota(jnp.int32, (8, PTS), 0)
    lane = lax.broadcasted_iota(jnp.int32, (8, PTS), 1)
    box_of = BOX_DEV * (group + row - 1) + lane // SKEL
    listed = jnp.zeros((8, PTS), F32)
    for s in range(SLOTS):
        box = jnp.where(s < count[x], near[x, s], -1000)
        listed = jnp.where(box_of == box, 1.0, listed)
    spot = spots[0]
    for b in range(1, BOX_DEV):
        spot = jnp.where(x == b, spots[b], spot)
    about = jnp.concatenate(
        [
            jnp.concatenate([spot[0:3], jnp.zeros((3, PTS - SKEL), F32)], axis=1),
            1.0 - listed[0:3],
            jnp.zeros((2, PTS), F32),
        ],
        axis=0,
    )
    info[...] = jnp.broadcast_to(about[None], info.shape)


def prep_kernel(dims, cur, weights, offsets, interp, halo, charge):
    group = group_index(dims)
    src = jnp.concatenate([cur[3, 0], cur[3, 1]], axis=0) * weights[...]
    halo[0:32, :] = src
    charges = []
    for b in range(BOX_DEV):
        cols = slice(PTS * b, PTS * b + PTS)
        halo[32:40, cols] = centred(offsets, b, group)
        charges.append(dot(src[:, cols], interp[b], 1, 1, HIGHEST))
    charge[...] = jnp.concatenate(charges, axis=1)


def from_x(r):
    n = lax.axis_size("x")
    return lax.rem(lax.axis_index("x") + n - r, n)


def pack_kernel(skelpos, *refs):
    charges, far = refs[:-1], refs[-1]
    n = 32 * len(charges)
    for r, ref in enumerate(charges):
        at = pl.multiple_of(32 * from_x(r), 32)
        far[0, pl.ds(at, 32), :] = ref[...]
    far[0, n : n + 8, :] = skelpos[...]
    far[1:] = jnp.broadcast_to(far[0][None], (far.shape[0] - 1,) + far.shape[1:])


def near_kernel(dims, near, count, prev, own, nxt, cur, *refs):
    outs, (ext, mult, tpos, acc) = refs[:-4], refs[-4:]
    for e in range(BOX_DEV):
        cols = slice(PTS * e, PTS * e + PTS)
        ext[e] = prev[:, cols]
        ext[BOX_DEV + e] = own[:, cols]
        ext[2 * BOX_DEV + e] = nxt[:, cols]
    stack = jnp.concatenate(
        [own[32:40, PTS * t : PTS * t + PTS] for t in range(BOX_DEV)]
        + [jnp.zeros((PTS - 8 * BOX_DEV, PTS), F32)],
        axis=0,
    )
    turned = stack.T
    base = BOX_DEV * (group_index(dims) - 1)
    erow = lax.broadcasted_iota(jnp.int32, (16, PTS), 0)
    for t in range(BOX_DEV):
        for c in range(3):
            tpos[t, c] = jnp.broadcast_to(turned[:, 8 * t + c : 8 * t + c + 1], (PTS, PTS))
        m = jnp.zeros((16, PTS), F32)
        for s in range(SLOTS):
            box = jnp.where(s < count[t], near[t, s] - base, -1000)
            m = m + jnp.where(erow == box, 1.0, 0.0)
        mult[t] = m
    acc[...] = jnp.zeros_like(acc)

    def step(d, carry):
        for t in range(BOX_DEV):
            e = t + d
            rows = ext[e, 0:32, :]
            re, im = helmholtz(
                tpos[t, 0],
                tpos[t, 1],
                tpos[t, 2],
                ext[e, 32:33, :],
                ext[e, 33:34, :],
                ext[e, 34:35, :],
                0.25 / math.pi,
            )
            khi, klo = split(jnp.concatenate([re, im], axis=1))
            rhi, rlo = split(jnp.concatenate([rows, rotate(rows)], axis=1))
            both = dot(jnp.concatenate([rhi, rlo], axis=0), khi, 1, 1)
            part = both[0:32] + (both[32:64] + dot(rhi, klo, 1, 1))
            acc[t] += part * mult[t, pl.ds(e, 1), :]
        return carry

    lax.fori_loop(0, 2 * REACH + 1, step, 0)
    for t in range(BOX_DEV):
        cols = slice(PTS * t, PTS * t + PTS)
        acc[t] += 0.5 * jnp.concatenate([cur[3, 0, :, cols], cur[3, 1, :, cols]], axis=0)
    n = len(outs)
    for r, out in enumerate(outs):
        out[...] = acc[lax.rem(lax.axis_index("x") + r, n)]


def far_kernel(dims, info, gathered, out, tpos, rhi, rlo, weight, acc):
    nz, ny, nk, nx = dims
    targets = ny * nk
    mine = lax.axis_index("y") * nk + lax.axis_index("k")
    first = lax.axis_index("z") * targets
    stack = jnp.concatenate([info[d] for d in range(targets)], axis=0)
    if targets * 8 < PTS:
        stack = jnp.concatenate([stack, jnp.zeros((PTS - targets * 8, PTS), F32)], axis=0)
    turned = stack.T
    for d in range(targets):
        for c in range(3):
            tpos[c, SKEL * d : SKEL * d + SKEL, :] = jnp.broadcast_to(
                turned[0:SKEL, 8 * d + c : 8 * d + c + 1], (SKEL, PTS)
            )
    for g in range(nz):
        rows = gathered[g, 0 : 32 * nx, :]
        hi, lo = split(jnp.concatenate([rows, rotate(rows)], axis=1))
        rhi[g] = hi
        rlo[g] = lo
    acc[...] = jnp.zeros_like(acc)
    per = min(4, targets)

    def step(g, carry):
        sx = gathered[g, 32 * nx + 0 : 32 * nx + 1, :]
        sy = gathered[g, 32 * nx + 1 : 32 * nx + 2, :]
        sz = gathered[g, 32 * nx + 2 : 32 * nx + 3, :]
        source_group = g * targets + mine
        for d in range(targets):
            delta = source_group - (first + d)
            w = jnp.where(delta == -1, info[d, 3:4, :], 1.0)
            w = jnp.where(delta == 0, info[d, 4:5, :], w)
            w = jnp.where(delta == 1, info[d, 5:6, :], w)
            weight[SKEL * d : SKEL * d + SKEL, :] = jnp.broadcast_to(
                w * (0.25 / math.pi), (SKEL, PTS)
            )
        for n in range(targets // per):
            span = slice(SKEL * per * n, SKEL * per * (n + 1))
            re, im = helmholtz(
                tpos[0, span, :],
                tpos[1, span, :],
                tpos[2, span, :],
                sx,
                sy,
                sz,
                weight[span, :],
            )
            khi, klo = split(jnp.concatenate([re, im], axis=1))
            acc[span, :] += dot(khi, rhi[g], 1, 1) + (
                dot(khi, rlo[g], 1, 1) + dot(klo, rhi[g], 1, 1)
            )
        return carry

    lax.fori_loop(0, nz, step, 0)
    for d in range(targets):
        out[d] = acc[SKEL * d : SKEL * d + SKEL, :]


def halves(rows, nx):
    re = jnp.concatenate([rows[32 * c : 32 * c + 16] for c in range(nx)], axis=0)
    im = jnp.concatenate([rows[32 * c + 16 : 32 * c + 32] for c in range(nx)], axis=0)
    return jnp.concatenate([re, im], axis=1)


def basis_kernel(scale, *refs):
    parts, (ordered, pieces) = refs[:-2], refs[-2:]
    nx = len(parts)
    for r, ref in enumerate(parts):
        c = from_x(r)
        for k in range(4):
            at = pl.ds(pl.multiple_of(16 * (nx * k + c), 16), 16)
            for p in range(2):
                ordered[p, at, :] = ref[32 * k + 16 * p : 32 * k + 16 * p + 16, :]
    cols = pl.ds(pl.multiple_of(PTS * lax.axis_index("x"), PTS), PTS)
    b2 = jnp.concatenate([ordered[0, :, cols], ordered[1, :, cols]], axis=1)
    gram = dot(b2, b2, 1, 1, HIGHEST) * scale
    n = pieces.shape[0]
    per = 256 // n
    for e in range(per):
        pieces[:, e, :] = gram[n * e : n * e + n, 0:PTS]
        pieces[:, per + e, :] = gram[n * e : n * e + n, PTS : 2 * PTS]


def couple_kernel(scale, phi, interp, ordered, gsum, *refs):
    nears, (applied, part, held) = refs[:-3], refs[-3:]
    nx = len(nears)
    for r, ref in enumerate(nears):
        held[from_x(r)] = ref[...]
    total = phi[0]
    for d in range(1, phi.shape[0]):
        total = total + phi[d]
    rows = dot(total, interp[lax.axis_index("x")], 0, 0, HIGHEST)
    rows = rows + jnp.concatenate([held[c] for c in range(nx)], axis=0)
    a2 = halves(rows, nx)
    applied[...] = a2
    cols = pl.ds(pl.multiple_of(PTS * lax.axis_index("x"), PTS), PTS)
    b2 = jnp.concatenate([ordered[0, :, cols], ordered[1, :, cols]], axis=1)
    c = dot(b2, a2, 1, 1, HIGHEST) * scale
    packed = jnp.concatenate([c[0:128], c[128:256]], axis=1)
    own = dot(a2, a2, 1, 1, HIGHEST) * scale
    own = jnp.concatenate([own[0:32], own[32:64]], axis=1)
    g = gsum[0]
    for d in range(1, gsum.shape[0]):
        g = g + gsum[d]
    n = part.shape[0]
    a, b, w = 128 // n, 32 // n, g.shape[0] // n
    for d in range(n):
        part[d] = jnp.concatenate(
            [
                packed[a * d : a * d + a],
                own[b * d : b * d + b],
                g[w * d : w * d + w],
                jnp.zeros((part.shape[1] - a - b - w, PTS), F32),
            ],
            axis=0,
        )


def first_sum_kernel(part, out):
    total = part[0]
    for d in range(1, part.shape[0]):
        total = total + part[d]
    out[...] = jnp.broadcast_to(total[None], out.shape)


def second_sum_kernel(rows, width, part, out):
    n = part.shape[0]
    total = part[0]
    for d in range(1, n):
        total = total + part[d]
    out[:, 0 : part.shape[1], :] = jnp.broadcast_to(
        total[None], (out.shape[0],) + total.shape
    )
    g = [part[:, rows + e, :] for e in range(width)]
    g = jnp.concatenate(g, axis=0)
    out[:, part.shape[1] :, :] = jnp.broadcast_to(g[None], (out.shape[0],) + g.shape)


def finish_kernel(width, summed, ordered, *refs):
    applied, (out, coupling, factor, inv) = refs[:-4], refs[-4:]
    n = summed.shape[0]
    a, b = 128 // n, 32 // n
    packed = jnp.concatenate([summed[d, 0:a, :] for d in range(n)], axis=0)
    c = jnp.concatenate([packed[:, 0:64], packed[:, 64:128]], axis=0)
    for k in range(4):
        coupling[k] = c[64 * k : 64 * k + 64]
    both = jnp.concatenate([summed[d, a : a + b, :] for d in range(n)], axis=0)
    g = jnp.concatenate([both[:, 0:64], both[:, 64:128]], axis=0)
    base = summed.shape[1] - width
    lines = jnp.concatenate([summed[d, base:, :] for d in range(n)], axis=0)
    bb = jnp.concatenate([lines[0:256], lines[256:512]], axis=1)
    gc = dot(bb, c, 1, 0, HIGHEST) - 2.0 * c
    g = g + dot(c, gc, 0, 0, HIGHEST)
    row = lax.broadcasted_iota(jnp.int32, (64, 64), 0)
    col = lax.broadcasted_iota(jnp.int32, (64, 64), 1)
    eye = row == col
    diag = jnp.where(eye, g, 0.0)
    trace = jnp.sum(jnp.sum(diag, axis=1, keepdims=True), axis=0, keepdims=True)
    g = g + jnp.where(eye, SHIFT_SCALE * trace / 64.0 + EPSILON, 0.0)
    m = jnp.concatenate([g, eye.astype(F32)], axis=1)
    sub = lax.broadcasted_iota(jnp.int32, (64, 1), 0)
    for j in range(63):
        line = m[j : j + 1, :]
        f = jnp.where(sub > j, m[:, j : j + 1] / line[:, j : j + 1], 0.0)
        m = m - f * line
    pivots = jnp.sum(jnp.where(eye, m[:, 0:64], 0.0), axis=1, keepdims=True)
    root = 1.0 / jnp.sqrt(pivots)
    m = m * root
    factor[...] = jnp.where(row <= col, m[:, 0:64], 0.0)
    inv[...] = m[:, 64:128]
    mine = inv[pl.ds(pl.multiple_of(16 * lax.axis_index("x"), 16), 16), :]
    back = dot(mine, c, 1, 1, HIGHEST)
    for p in range(2):
        out[p] = -dot(back, ordered[p], 1, 0, HIGHEST)
    for r, ref in enumerate(applied):
        rows = dot(mine, ref[...], 1, 0, HIGHEST)
        cols = pl.ds(pl.multiple_of(PTS * from_x(r), PTS), PTS)
        out[0, :, cols] += rows[:, 0:PTS]
        out[1, :, cols] += rows[:, PTS : 2 * PTS]


def around(blocks):
    n = lax.axis_size("x")
    return [blocks[0]] + [
        lax.ppermute(blocks[r], "x", [(i, (i + r) % n) for i in range(n)]) for r in range(1, n)
    ]


def trade(value, axes):
    return lax.all_to_all(value, axes, split_axis=0, concat_axis=0, tiled=True)


def shards(dims, basis, offsets, weights, interp, skeleton, near_boxes, near_count):
    nz, ny, nk, nx = dims
    groups = nz * ny * nk
    targets = ny * nk
    sources = nz * nx
    points = BOX_DEV * PTS
    scale = 1.0 / (groups * points)
    shape = lambda *s: jax.ShapeDtypeStruct(s, F32)

    info, skelpos = call(
        functools.partial(place_kernel, dims),
        (shape(targets, 8, PTS), shape(8, PTS)),
        [SMEM, SMEM, VMEM, VMEM],
    )(near_boxes, near_count, offsets, skeleton)
    info_all = trade(info, YK)
    halo, charge = call(
        functools.partial(prep_kernel, dims), (shape(40, points), shape(32, PTS)), [VMEM] * 4
    )(basis, weights[None], offsets, interp)
    charges = around([charge] * nx)
    far = call(pack_kernel, shape(nz, 32 * nx + 8, PTS), [VMEM] * (1 + nx))(skelpos, *charges)
    far_all = trade(far, "z")
    prev = lax.ppermute(halo, BOX, [(g, g + 1) for g in range(groups - 1)])
    nxt = lax.ppermute(halo, BOX, [(g + 1, g) for g in range(groups - 1)])
    bases = around([basis.reshape(4 * 32, points)] * nx)

    nears = call(
        functools.partial(near_kernel, dims),
        (shape(32, PTS),) * nx,
        [SMEM, SMEM] + [VMEM] * 4,
        [
            pltpu.VMEM((3 * BOX_DEV, 40, PTS), F32),
            pltpu.VMEM((BOX_DEV, 16, PTS), F32),
            pltpu.VMEM((BOX_DEV, 3, PTS, PTS), F32),
            pltpu.VMEM((BOX_DEV, 32, PTS), F32),
        ],
        flops=36 * 2 * 64 * 256 * 128 * 2,
    )(near_boxes, near_count, prev, halo, nxt, basis)
    nears = around(nears)
    ordered, pieces = call(
        functools.partial(basis_kernel, scale),
        (shape(2, 256, points), shape(sources, 512 // sources, PTS)),
        [VMEM] * nx,
    )(*bases)
    gsum = trade(pieces, ZX)

    far_part = call(
        functools.partial(far_kernel, dims),
        shape(targets, SKEL, 32 * nx),
        [VMEM, VMEM],
        [
            pltpu.VMEM((3, SKEL * targets, PTS), F32),
            pltpu.VMEM((nz, 32 * nx, 2 * PTS), BF16),
            pltpu.VMEM((nz, 32 * nx, 2 * PTS), BF16),
            pltpu.VMEM((SKEL * targets, PTS), F32),
            pltpu.VMEM((SKEL * targets, 32 * nx), F32),
        ],
        flops=3 * 2 * 512 * 2048 * 128,
    )(info_all, far_all)
    phi = trade(far_part, YK)

    used = 128 // targets + 32 // targets
    width = 512 // sources // targets
    tall = -(-(used + width) // 8) * 8
    applied, part = call(
        functools.partial(couple_kernel, scale),
        (shape(64, 2 * PTS), shape(targets, tall, PTS)),
        [VMEM] * (4 + nx),
        [pltpu.VMEM((nx, 32, PTS), F32)],
    )(phi, interp, ordered, gsum, *nears)
    part = trade(part, YK)
    applied = around([applied] * nx)
    part = call(first_sum_kernel, shape(sources, tall, PTS), [VMEM])(part)
    part = trade(part, ZX)
    part = call(
        functools.partial(second_sum_kernel, used, width),
        shape(targets, tall + width * sources, PTS),
        [VMEM],
    )(part)
    summed = trade(part, YK)

    new_block, coupling, factor = call(
        functools.partial(finish_kernel, width * sources),
        (shape(2, 16, points), shape(4, 64, 64), shape(64, 64)),
        [VMEM] * (2 + nx),
        [pltpu.VMEM((64, 64), F32)],
    )(summed, ordered, *applied)
    return new_block, coupling, factor


def solution(mesh):
    boxes, cols = mesh.devices.shape
    nk = GRID[2]
    ny = GRID[1] if boxes == math.prod(GRID) else 2
    nz = boxes // (ny * nk)
    dims = (nz, ny, nk, cols)
    fine = Mesh(mesh.devices.reshape(dims), ("z", "y", "k", "x"))
    return jax.shard_map(
        functools.partial(shards, dims),
        mesh=fine,
        in_specs=(
            P(None, None, "x", BOX),
            P(None, BOX),
            P(BOX),
            P(BOX, None, None),
            P(BOX, None),
            P(BOX, None),
            P(BOX),
        ),
        out_specs=(P(None, "x", BOX), P(), P()),
        check_vma=False,
    )
```

```python
import functools
import math

import jax
import jax.numpy as jnp
from jax import lax
from jax.experimental import pallas as pl
from jax.experimental.pallas import tpu as pltpu
from jax.sharding import Mesh
from jax.sharding import PartitionSpec as P

BOX_DEV = 4
PTS = 128
SKEL = 32
SLOTS = 27
REACH = 4
WAVENUMBER = 6.0
SMOOTHING = 0.1
SHIFT_SCALE = 0.02
EPSILON = 1e-06
HIGHEST = lax.Precision.HIGHEST
F32 = jnp.float32
BF16 = jnp.bfloat16
INTERPRET = False

GRID = (8, 8, 2)
BOX = ("z", "y", "k")
YK = ("y", "k")
ZX = ("z", "x")

TURNS = WAVENUMBER / (2.0 * math.pi)
SIN_C = (3.1415926401307073, -5.167710083507923, 2.5500775232148563, -0.5982912856211671, 0.07765766030589402)
COS_C = (
    0.9999999997799043,
    -4.934802137078822,
    4.0587091595560825,
    -1.335212003047854,
    0.2349373138047365,
    -0.02439632433202294,
)


def poly(coefs, u):
    r = coefs[-1] * u + coefs[-2]
    for c in coefs[-3::-1]:
        r = r * u + c
    return r


def helmholtz(tx, ty, tz, sx, sy, sz, weight):
    dx = tx - sx
    dy = ty - sy
    dz = tz - sz
    s = SMOOTHING * SMOOTHING + dx * dx + dy * dy + dz * dz
    r = lax.rsqrt(s)
    r = r * (1.5 - (0.5 * s) * (r * r))
    t = (s * r) * TURNS
    f = t - lax.round(t, lax.RoundingMethod.TO_NEAREST_EVEN)
    u = f * f
    sn = f * poly(SIN_C, u)
    cs = poly(COS_C, u)
    two = sn + sn
    w = r * weight
    return (1.0 - two * sn) * w, (two * cs) * w


def split(x):
    hi = x.astype(BF16)
    return hi, (x - hi.astype(F32)).astype(BF16)


def dot(a, b, ca, cb, precision=None):
    return lax.dot_general(
        a, b, (((ca,), (cb,)), ((), ())), precision=precision, preferred_element_type=F32
    )


def rotate(rows):
    parts = []
    for g in range(rows.shape[0] // 32):
        parts.append(-rows[32 * g + 16 : 32 * g + 32])
        parts.append(rows[32 * g : 32 * g + 16])
    return jnp.concatenate(parts, axis=0)


def group_index(dims):
    return (lax.axis_index("z") * dims[1] + lax.axis_index("y")) * dims[2] + lax.axis_index("k")


def call(kernel, out_shape, in_specs, scratch=(), flops=0, limit=16 << 20):
    vmem = pl.BlockSpec(memory_space=pltpu.VMEM)
    single = not isinstance(out_shape, (tuple, list))
    return pl.pallas_call(
        kernel,
        out_shape=out_shape,
        in_specs=in_specs,
        out_specs=vmem if single else [vmem] * len(out_shape),
        scratch_shapes=list(scratch),
        cost_estimate=pl.CostEstimate(flops=flops, bytes_accessed=1 << 19, transcendentals=0),
        compiler_params=pltpu.CompilerParams(vmem_limit_bytes=limit),
        interpret=INTERPRET,
    )


VMEM = pl.BlockSpec(memory_space=pltpu.VMEM)
SMEM = pl.BlockSpec(memory_space=pltpu.SMEM)


def centred(offsets, b, group):
    axis = lax.broadcasted_iota(jnp.int32, (8, 1), 0)
    shift = jnp.where(axis == 0, group.astype(F32), jnp.where(axis == 1, float(b), 0.0))
    cols = slice(PTS * b, PTS * b + PTS)
    return jnp.concatenate([offsets[:, cols], jnp.zeros((5, PTS), F32)], axis=0) + shift


def place_kernel(dims, near, count, offsets, skel, info, skelpos):
    group = group_index(dims)
    x = lax.axis_index("x")
    spots = []
    for b in range(BOX_DEV):
        q = lax.broadcasted_iota(jnp.int32, (PTS, SKEL), 0)
        pick = (q == skel[b : b + 1, :]).astype(F32)
        spots.append(dot(centred(offsets, b, group), pick, 1, 0, HIGHEST))
    skelpos[...] = jnp.concatenate(spots, axis=1)
    row = lax.broadcasted_iota(jnp.int32, (8, PTS), 0)
    lane = lax.broadcasted_iota(jnp.int32, (8, PTS), 1)
    box_of = BOX_DEV * (group + row - 1) + lane // SKEL
    listed = jnp.zeros((8, PTS), F32)
    for s in range(SLOTS):
        box = jnp.where(s < count[x], near[x, s], -1000)
        listed = jnp.where(box_of == box, 1.0, listed)
    spot = spots[0]
    for b in range(1, BOX_DEV):
        spot = jnp.where(x == b, spots[b], spot)
    about = jnp.concatenate(
        [
            jnp.concatenate([spot[0:3], jnp.zeros((3, PTS - SKEL), F32)], axis=1),
            1.0 - listed[0:3],
            jnp.zeros((2, PTS), F32),
        ],
        axis=0,
    )
    info[...] = jnp.broadcast_to(about[None], info.shape)


def prep_kernel(dims, cur, weights, offsets, interp, skelpos, halo, far):
    group = group_index(dims)
    src = jnp.concatenate([cur[3, 0], cur[3, 1]], axis=0) * weights[...]
    halo[0:32, :] = src
    charges = []
    for b in range(BOX_DEV):
        cols = slice(PTS * b, PTS * b + PTS)
        halo[32:40, cols] = centred(offsets, b, group)
        charges.append(dot(src[:, cols], interp[b], 1, 1, HIGHEST))
    payload = jnp.concatenate([jnp.concatenate(charges, axis=1), skelpos[...]], axis=0)
    far[...] = jnp.broadcast_to(payload[None], far.shape)


def from_x(r):
    n = lax.axis_size("x")
    return lax.rem(lax.axis_index("x") + n - r, n)


def near_kernel(dims, near, count, prev, own, nxt, cur, *refs):
    outs, (ext, mult, tpos, acc) = refs[:-4], refs[-4:]
    for e in range(BOX_DEV):
        cols = slice(PTS * e, PTS * e + PTS)
        ext[e] = prev[:, cols]
        ext[BOX_DEV + e] = own[:, cols]
        ext[2 * BOX_DEV + e] = nxt[:, cols]
    stack = jnp.concatenate(
        [own[32:40, PTS * t : PTS * t + PTS] for t in range(BOX_DEV)]
        + [jnp.zeros((PTS - 8 * BOX_DEV, PTS), F32)],
        axis=0,
    )
    turned = stack.T
    base = BOX_DEV * (group_index(dims) - 1)
    erow = lax.broadcasted_iota(jnp.int32, (16, PTS), 0)
    for t in range(BOX_DEV):
        for c in range(3):
            tpos[t, c] = jnp.broadcast_to(turned[:, 8 * t + c : 8 * t + c + 1], (PTS, PTS))
        m = jnp.zeros((16, PTS), F32)
        for s in range(SLOTS):
            box = jnp.where(s < count[t], near[t, s] - base, -1000)
            m = m + jnp.where(erow == box, 1.0, 0.0)
        mult[t] = m
    acc[...] = jnp.zeros_like(acc)

    def step(d, carry):
        for t in range(BOX_DEV):
            e = t + d
            rows = ext[e, 0:32, :]
            re, im = helmholtz(
                tpos[t, 0],
                tpos[t, 1],
                tpos[t, 2],
                ext[e, 32:33, :],
                ext[e, 33:34, :],
                ext[e, 34:35, :],
                0.25 / math.pi,
            )
            khi, klo = split(jnp.concatenate([re, im], axis=1))
            rhi, rlo = split(jnp.concatenate([rows, rotate(rows)], axis=1))
            both = dot(jnp.concatenate([rhi, rlo], axis=0), khi, 1, 1)
            part = both[0:32] + (both[32:64] + dot(rhi, klo, 1, 1))
            acc[t] += part * mult[t, pl.ds(e, 1), :]
        return carry

    lax.fori_loop(0, 2 * REACH + 1, step, 0)
    for t in range(BOX_DEV):
        cols = slice(PTS * t, PTS * t + PTS)
        acc[t] += 0.5 * jnp.concatenate([cur[3, 0, :, cols], cur[3, 1, :, cols]], axis=0)
    n = len(outs)
    for r, out in enumerate(outs):
        block = acc[lax.rem(lax.axis_index("x") + r, n)]
        if r == 0:
            out[...] = block
            continue
        for k in range(4):
            for p in range(2):
                out[32 * k + 16 * p : 32 * k + 16 * p + 16, :] = cur[k, p]
        out[PTS : PTS + 8, :] = jnp.concatenate(
            [block[8 * g : 8 * g + 8] for g in range(4)], axis=1
        )


def far_kernel(dims, info, gathered, out, tpos, rhi, rlo, weight, acc):
    nz, ny, nk, nx = dims
    targets = ny * nk
    mine = lax.axis_index("y") * nk + lax.axis_index("k")
    first = lax.axis_index("z") * targets
    stack = jnp.concatenate([info[d] for d in range(targets)], axis=0)
    if targets * 8 < PTS:
        stack = jnp.concatenate([stack, jnp.zeros((PTS - targets * 8, PTS), F32)], axis=0)
    turned = stack.T
    for d in range(targets):
        for c in range(3):
            tpos[c, SKEL * d : SKEL * d + SKEL, :] = jnp.broadcast_to(
                turned[0:SKEL, 8 * d + c : 8 * d + c + 1], (SKEL, PTS)
            )
    for g in range(nz):
        rows = jnp.concatenate([gathered[nx * g + c, 0:32, :] for c in range(nx)], axis=0)
        hi, lo = split(jnp.concatenate([rows, rotate(rows)], axis=1))
        rhi[g] = hi
        rlo[g] = lo
    acc[...] = jnp.zeros_like(acc)
    per = min(4, targets)

    def step(g, carry):
        sx = gathered[nx * g, 32:33, :]
        sy = gathered[nx * g, 33:34, :]
        sz = gathered[nx * g, 34:35, :]
        source_group = g * targets + mine
        for d in range(targets):
            delta = source_group - (first + d)
            w = jnp.where(delta == -1, info[d, 3:4, :], 1.0)
            w = jnp.where(delta == 0, info[d, 4:5, :], w)
            w = jnp.where(delta == 1, info[d, 5:6, :], w)
            weight[SKEL * d : SKEL * d + SKEL, :] = jnp.broadcast_to(
                w * (0.25 / math.pi), (SKEL, PTS)
            )
        for n in range(targets // per):
            span = slice(SKEL * per * n, SKEL * per * (n + 1))
            re, im = helmholtz(
                tpos[0, span, :],
                tpos[1, span, :],
                tpos[2, span, :],
                sx,
                sy,
                sz,
                weight[span, :],
            )
            khi, klo = split(jnp.concatenate([re, im], axis=1))
            acc[span, :] += dot(khi, rhi[g], 1, 1) + (
                dot(khi, rlo[g], 1, 1) + dot(klo, rhi[g], 1, 1)
            )
        return carry

    lax.fori_loop(0, nz, step, 0)
    for d in range(targets):
        out[d] = acc[SKEL * d : SKEL * d + SKEL, :]


def halves(rows, nx):
    re = jnp.concatenate([rows[32 * c : 32 * c + 16] for c in range(nx)], axis=0)
    im = jnp.concatenate([rows[32 * c + 16 : 32 * c + 32] for c in range(nx)], axis=0)
    return jnp.concatenate([re, im], axis=1)


def basis_kernel(scale, first, basis, *refs):
    others, (ordered, nears, blocks) = refs[:-3], refs[-3:]
    nx = 1 + len(others)
    for r, ref in enumerate((basis,) + others):
        c = from_x(r)
        for k in range(4):
            at = pl.ds(pl.multiple_of(16 * (nx * k + c), 16), 16)
            for p in range(2):
                ordered[p, at, :] = ref[32 * k + 16 * p : 32 * k + 16 * p + 16, :]
        block = first[...] if r == 0 else ref[PTS : PTS + 8, :]
        if r > 0:
            block = jnp.concatenate(
                [block[:, PTS * g : PTS * g + PTS] for g in range(4)], axis=0
            )
        nears[pl.ds(pl.multiple_of(32 * c, 32), 32), :] = block
    x = lax.axis_index("x")
    half = lax.rem(x, 2)

    def product(left, right, rows):
        total = None
        for p in range(2):
            a = ordered[p, pl.ds(pl.multiple_of(64 * left, 64), 64), :]
            b = ordered[p, pl.ds(pl.multiple_of(right, 32), rows), :]
            part = dot(a, b, 1, 1, HIGHEST)
            total = part if total is None else total + part
        return total * scale

    blocks[0:64, :] = jnp.concatenate(
        [product(x, 64 * x, 64), product(x, 64 * lax.rem(x + 1, nx), 64)], axis=1
    )
    far = product(half, 64 * (half + 2) + 32 * (x // 2), 32)
    blocks[64:80, :] = jnp.concatenate([far[16 * g : 16 * g + 16] for g in range(4)], axis=1)


def couple_kernel(scale, phi, interp, ordered, nears, blocks, applied, part):
    nx = nears.shape[0] // 32
    total = phi[0]
    for d in range(1, phi.shape[0]):
        total = total + phi[d]
    rows = dot(total, interp[lax.axis_index("x")], 0, 0, HIGHEST) + nears[...]
    a2 = halves(rows, nx)
    applied[...] = a2
    cols = pl.ds(pl.multiple_of(PTS * lax.axis_index("x"), PTS), PTS)
    b2 = jnp.concatenate([ordered[0, :, cols], ordered[1, :, cols]], axis=1)
    c = dot(b2, a2, 1, 1, HIGHEST) * scale
    packed = jnp.concatenate([c[0:128], c[128:256]], axis=1)
    own = dot(a2, a2, 1, 1, HIGHEST) * scale
    n = part.shape[0]
    lead = 128 // n
    for d in range(n):
        part[d, 0:lead, :] = packed[lead * d : lead * d + lead]
    rest = jnp.concatenate(
        [
            jnp.concatenate([own[0:32], own[32:64]], axis=1),
            blocks[...],
            jnp.zeros((16, PTS), F32),
        ],
        axis=0,
    )
    for e in range(part.shape[1] - lead):
        part[:, lead + e, :] = rest[n * e : n * e + n]


def finish_kernel(nx, summed, ordered, *refs):
    applied, (out, coupling, factor, inv) = refs[:-4], refs[-4:]
    n = summed.shape[0]
    lead = 128 // n
    tail = 128 // n
    packed = jnp.concatenate([summed[d, 0:lead, :] for d in range(n)], axis=0)
    c = jnp.concatenate([packed[:, 0:64], packed[:, 64:128]], axis=0)
    for k in range(4):
        coupling[k] = c[64 * k : 64 * k + 64]
    own = None
    de, h = [], []
    for x in range(nx):
        rest = [summed[:, lead + tail * x + e, :] for e in range(112 // n)]
        rest = jnp.concatenate(rest, axis=0)
        own = rest[0:32] if own is None else own + rest[0:32]
        de.append(rest[32:96])
        h.append(
            jnp.concatenate([rest[96:112, 32 * g : 32 * g + 32] for g in range(4)], axis=0)
        )
    g = jnp.concatenate([own[:, 0:64], own[:, 64:128]], axis=0)
    blocks = [c[64 * k : 64 * k + 64] for k in range(4)]
    lines = []
    for k in range(4):
        right = jnp.concatenate([0.5 * blocks[k], blocks[(k + 1) % 4]], axis=0)
        left = de[k]
        if k < 2:
            right = jnp.concatenate([right, blocks[k + 2]], axis=0)
            left = jnp.concatenate([left, h[k], h[k + 2]], axis=1)
        lines.append(dot(left, right, 1, 0, HIGHEST) - blocks[k])
    halfq = dot(c, jnp.concatenate(lines, axis=0), 0, 0, HIGHEST)
    g = g + (halfq + halfq.T)
    row = lax.broadcasted_iota(jnp.int32, (64, 64), 0)
    col = lax.broadcasted_iota(jnp.int32, (64, 64), 1)
    eye = row == col
    diag = jnp.where(eye, g, 0.0)
    trace = jnp.sum(jnp.sum(diag, axis=1, keepdims=True), axis=0, keepdims=True)
    g = g + jnp.where(eye, SHIFT_SCALE * trace / 64.0 + EPSILON, 0.0)
    m = jnp.concatenate([g, eye.astype(F32)], axis=1)
    sub = lax.broadcasted_iota(jnp.int32, (64, 1), 0)
    for j in range(0, 64, 2):
        one = m[j : j + 1, :]
        two = m[j + 1 : j + 2, :]
        p = 1.0 / one[:, j : j + 1]
        f1 = m[:, j : j + 1] * p
        two = two - (two[:, j : j + 1] * p) * one
        f2 = (m[:, j + 1 : j + 2] - f1 * one[:, j + 1 : j + 2]) / two[:, j + 1 : j + 2]
        f1 = jnp.where(sub > j, f1, 0.0)
        f2 = jnp.where(sub > j + 1, f2, 0.0)
        m = m - f1 * one - f2 * two
    pivots = jnp.sum(jnp.where(eye, m[:, 0:64], 0.0), axis=1, keepdims=True)
    m = m * (1.0 / jnp.sqrt(pivots))
    factor[...] = jnp.where(row <= col, m[:, 0:64], 0.0)
    inv[...] = m[:, 64:128]
    mine = inv[pl.ds(pl.multiple_of(16 * lax.axis_index("x"), 16), 16), :]
    back = dot(mine, c, 1, 1, HIGHEST)
    for p in range(2):
        out[p] = -dot(back, ordered[p], 1, 0, HIGHEST)
    for r, ref in enumerate(applied):
        rows = dot(mine, ref[...], 1, 0, HIGHEST)
        cols = pl.ds(pl.multiple_of(PTS * from_x(r), PTS), PTS)
        out[0, :, cols] += rows[:, 0:PTS]
        out[1, :, cols] += rows[:, PTS : 2 * PTS]


def around(blocks):
    n = lax.axis_size("x")
    return [blocks[0]] + [
        lax.ppermute(blocks[r], "x", [(i, (i + r) % n) for i in range(n)]) for r in range(1, n)
    ]


def trade(value, axes):
    return lax.all_to_all(value, axes, split_axis=0, concat_axis=0, tiled=True)


def shards(dims, basis, offsets, weights, interp, skeleton, near_boxes, near_count):
    nz, ny, nk, nx = dims
    groups = nz * ny * nk
    targets = ny * nk
    sources = nz * nx
    points = BOX_DEV * PTS
    scale = 1.0 / (groups * points)
    shape = lambda *s: jax.ShapeDtypeStruct(s, F32)

    info, skelpos = call(
        functools.partial(place_kernel, dims),
        (shape(targets, 8, PTS), shape(8, PTS)),
        [SMEM, SMEM, VMEM, VMEM],
    )(near_boxes, near_count, offsets, skeleton)
    info_all = trade(info, YK)
    halo, far = call(
        functools.partial(prep_kernel, dims),
        (shape(40, points), shape(sources, 40, PTS)),
        [VMEM] * 5,
    )(basis, weights[None], offsets, interp, skelpos)
    prev = lax.ppermute(halo, BOX, [(g, g + 1) for g in range(groups - 1)])
    nxt = lax.ppermute(halo, BOX, [(g + 1, g) for g in range(groups - 1)])
    far_all = trade(far, ZX)

    nears = call(
        functools.partial(near_kernel, dims),
        (shape(32, PTS),) + (shape(PTS + 8, points),) * (nx - 1),
        [SMEM, SMEM] + [VMEM] * 4,
        [
            pltpu.VMEM((3 * BOX_DEV, 40, PTS), F32),
            pltpu.VMEM((BOX_DEV, 16, PTS), F32),
            pltpu.VMEM((BOX_DEV, 3, PTS, PTS), F32),
            pltpu.VMEM((BOX_DEV, 32, PTS), F32),
        ],
        flops=36 * 2 * 64 * 256 * 128 * 2,
    )(near_boxes, near_count, prev, halo, nxt, basis)
    nears = around(nears)
    ordered, near_rows, blocks = call(
        functools.partial(basis_kernel, scale),
        (shape(2, 256, points), shape(32 * nx, PTS), shape(80, PTS)),
        [VMEM] * (1 + nx),
    )(nears[0], basis.reshape(4 * 32, points), *nears[1:])

    far_part = call(
        functools.partial(far_kernel, dims),
        shape(targets, SKEL, 32 * nx),
        [VMEM, VMEM],
        [
            pltpu.VMEM((3, SKEL * targets, PTS), F32),
            pltpu.VMEM((nz, 32 * nx, 2 * PTS), BF16),
            pltpu.VMEM((nz, 32 * nx, 2 * PTS), BF16),
            pltpu.VMEM((SKEL * targets, PTS), F32),
            pltpu.VMEM((SKEL * targets, 32 * nx), F32),
        ],
        flops=3 * 2 * 512 * 2048 * 128,
    )(info_all, far_all)
    phi = trade(far_part, YK)

    lead = 128 // targets
    tall = 2 * lead
    applied, part = call(
        functools.partial(couple_kernel, scale),
        (shape(64, 2 * PTS), shape(targets, tall, PTS)),
        [VMEM] * 5,
    )(phi, interp, ordered, near_rows, blocks)
    part = jnp.sum(trade(part, YK), axis=0)
    applied = around([applied] * nx)
    part = trade(jnp.broadcast_to(part[None], (sources, tall, PTS)), ZX)
    part = jnp.sum(part.reshape(nz, nx, tall, PTS), axis=0)
    part = jnp.concatenate(
        [jnp.sum(part[:, :lead], axis=0), part[:, lead:].reshape(nx * (tall - lead), PTS)],
        axis=0,
    )
    summed = trade(jnp.broadcast_to(part[None], (targets,) + part.shape), YK)

    new_block, coupling, factor = call(
        functools.partial(finish_kernel, nx),
        (shape(2, 16, points), shape(4, 64, 64), shape(64, 64)),
        [VMEM] * (2 + nx),
        [pltpu.VMEM((64, 64), F32)],
    )(summed, ordered, *applied)
    return new_block, coupling, factor


def solution(mesh):
    boxes, cols = mesh.devices.shape
    nk = GRID[2]
    ny = GRID[1] if boxes == math.prod(GRID) else 2
    nz = boxes // (ny * nk)
    dims = (nz, ny, nk, cols)
    fine = Mesh(mesh.devices.reshape(dims), ("z", "y", "k", "x"))
    return jax.shard_map(
        functools.partial(shards, dims),
        mesh=fine,
        in_specs=(
            P(None, None, "x", BOX),
            P(None, BOX),
            P(BOX),
            P(BOX, None, None),
            P(BOX, None),
            P(BOX, None),
            P(BOX),
        ),
        out_specs=(P(None, "x", BOX), P(), P()),
        check_vma=False,
    )
```

```python
import functools
import math

import jax
import jax.numpy as jnp
from jax import lax
from jax.experimental import pallas as pl
from jax.experimental.pallas import tpu as pltpu
from jax.sharding import Mesh
from jax.sharding import PartitionSpec as P

BOX_DEV = 4
PTS = 128
SKEL = 32
SLOTS = 27
REACH = 4
WAVENUMBER = 6.0
SMOOTHING = 0.1
SHIFT_SCALE = 0.02
EPSILON = 1e-06
HIGHEST = lax.Precision.HIGHEST
F32 = jnp.float32
BF16 = jnp.bfloat16
INTERPRET = False

GRID = (8, 8, 2)
BOX = ("z", "y", "k")
YK = ("y", "k")
ZX = ("z", "x")

TURNS = WAVENUMBER / (2.0 * math.pi)
SIN_C = (3.1415926401307073, -5.167710083507923, 2.5500775232148563, -0.5982912856211671, 0.07765766030589402)
COS_C = (
    0.9999999997799043,
    -4.934802137078822,
    4.0587091595560825,
    -1.335212003047854,
    0.2349373138047365,
    -0.02439632433202294,
)


def poly(coefs, u):
    r = coefs[-1] * u + coefs[-2]
    for c in coefs[-3::-1]:
        r = r * u + c
    return r


def helmholtz(tx, ty, tz, sx, sy, sz, weight):
    dx = tx - sx
    dy = ty - sy
    dz = tz - sz
    s = SMOOTHING * SMOOTHING + dx * dx + dy * dy + dz * dz
    r = lax.rsqrt(s)
    r = r * (1.5 - (0.5 * s) * (r * r))
    t = (s * r) * TURNS
    f = t - lax.round(t, lax.RoundingMethod.TO_NEAREST_EVEN)
    u = f * f
    sn = f * poly(SIN_C, u)
    cs = poly(COS_C, u)
    two = sn + sn
    w = r * weight
    return (1.0 - two * sn) * w, (two * cs) * w


def split(x):
    hi = x.astype(BF16)
    return hi, (x - hi.astype(F32)).astype(BF16)


def dot(a, b, ca, cb, precision=None):
    return lax.dot_general(
        a, b, (((ca,), (cb,)), ((), ())), precision=precision, preferred_element_type=F32
    )


def rotate(rows):
    parts = []
    for g in range(rows.shape[0] // 32):
        parts.append(-rows[32 * g + 16 : 32 * g + 32])
        parts.append(rows[32 * g : 32 * g + 16])
    return jnp.concatenate(parts, axis=0)


def group_index(dims):
    return (lax.axis_index("z") * dims[1] + lax.axis_index("y")) * dims[2] + lax.axis_index("k")


def call(kernel, out_shape, in_specs, scratch=(), flops=0, limit=16 << 20):
    vmem = pl.BlockSpec(memory_space=pltpu.VMEM)
    single = not isinstance(out_shape, (tuple, list))
    return pl.pallas_call(
        kernel,
        out_shape=out_shape,
        in_specs=in_specs,
        out_specs=vmem if single else [vmem] * len(out_shape),
        scratch_shapes=list(scratch),
        cost_estimate=pl.CostEstimate(flops=flops, bytes_accessed=1 << 19, transcendentals=0),
        compiler_params=pltpu.CompilerParams(vmem_limit_bytes=limit),
        interpret=INTERPRET,
    )


VMEM = pl.BlockSpec(memory_space=pltpu.VMEM)
SMEM = pl.BlockSpec(memory_space=pltpu.SMEM)


def centred(offsets, b, group):
    axis = lax.broadcasted_iota(jnp.int32, (8, 1), 0)
    shift = jnp.where(axis == 0, group.astype(F32), jnp.where(axis == 1, float(b), 0.0))
    cols = slice(PTS * b, PTS * b + PTS)
    return jnp.concatenate([offsets[:, cols], jnp.zeros((5, PTS), F32)], axis=0) + shift


def place_kernel(dims, near, count, offsets, skel, info, skelpos):
    group = group_index(dims)
    x = lax.axis_index("x")
    spots = []
    for b in range(BOX_DEV):
        q = lax.broadcasted_iota(jnp.int32, (PTS, SKEL), 0)
        pick = (q == skel[b : b + 1, :]).astype(F32)
        spots.append(dot(centred(offsets, b, group), pick, 1, 0, HIGHEST))
    skelpos[...] = jnp.concatenate(spots, axis=1)
    row = lax.broadcasted_iota(jnp.int32, (8, PTS), 0)
    lane = lax.broadcasted_iota(jnp.int32, (8, PTS), 1)
    box_of = BOX_DEV * (group + row - 1) + lane // SKEL
    listed = jnp.zeros((8, PTS), F32)
    for s in range(SLOTS):
        box = jnp.where(s < count[x], near[x, s], -1000)
        listed = jnp.where(box_of == box, 1.0, listed)
    spot = spots[0]
    for b in range(1, BOX_DEV):
        spot = jnp.where(x == b, spots[b], spot)
    about = jnp.concatenate(
        [
            jnp.concatenate([spot[0:3], jnp.zeros((3, PTS - SKEL), F32)], axis=1),
            1.0 - listed[0:3],
            jnp.zeros((2, PTS), F32),
        ],
        axis=0,
    )
    info[...] = jnp.broadcast_to(about[None], info.shape)


def prep_kernel(dims, cur, weights, offsets, interp, skelpos, halo, far):
    group = group_index(dims)
    src = jnp.concatenate([cur[3, 0], cur[3, 1]], axis=0) * weights[...]
    halo[0:32, :] = src
    charges = []
    for b in range(BOX_DEV):
        cols = slice(PTS * b, PTS * b + PTS)
        halo[32:40, cols] = centred(offsets, b, group)
        charges.append(dot(src[:, cols], interp[b], 1, 1, HIGHEST))
    payload = jnp.concatenate([jnp.concatenate(charges, axis=1), skelpos[...]], axis=0)
    far[...] = jnp.broadcast_to(payload[None], far.shape)


def from_x(r):
    n = lax.axis_size("x")
    return lax.rem(lax.axis_index("x") + n - r, n)


def near_kernel(dims, near, count, prev, own, nxt, cur, *refs):
    outs, (ext, mult, tpos, acc) = refs[:-4], refs[-4:]
    for e in range(BOX_DEV):
        cols = slice(PTS * e, PTS * e + PTS)
        ext[e] = prev[:, cols]
        ext[BOX_DEV + e] = own[:, cols]
        ext[2 * BOX_DEV + e] = nxt[:, cols]
    stack = jnp.concatenate(
        [own[32:40, PTS * t : PTS * t + PTS] for t in range(BOX_DEV)]
        + [jnp.zeros((PTS - 8 * BOX_DEV, PTS), F32)],
        axis=0,
    )
    turned = stack.T
    base = BOX_DEV * (group_index(dims) - 1)
    erow = lax.broadcasted_iota(jnp.int32, (16, PTS), 0)
    for t in range(BOX_DEV):
        for c in range(3):
            tpos[t, c] = jnp.broadcast_to(turned[:, 8 * t + c : 8 * t + c + 1], (PTS, PTS))
        m = jnp.zeros((16, PTS), F32)
        for s in range(SLOTS):
            box = jnp.where(s < count[t], near[t, s] - base, -1000)
            m = m + jnp.where(erow == box, 1.0, 0.0)
        mult[t] = m
    acc[...] = jnp.zeros_like(acc)

    def step(d, carry):
        for t in range(BOX_DEV):
            e = t + d
            rows = ext[e, 0:32, :]
            re, im = helmholtz(
                tpos[t, 0],
                tpos[t, 1],
                tpos[t, 2],
                ext[e, 32:33, :],
                ext[e, 33:34, :],
                ext[e, 34:35, :],
                0.25 / math.pi,
            )
            khi, klo = split(jnp.concatenate([re, im], axis=1))
            rhi, rlo = split(jnp.concatenate([rows, rotate(rows)], axis=1))
            both = dot(jnp.concatenate([rhi, rlo], axis=0), khi, 1, 1)
            part = both[0:32] + (both[32:64] + dot(rhi, klo, 1, 1))
            acc[t] += part * mult[t, pl.ds(e, 1), :]
        return carry

    lax.fori_loop(0, 2 * REACH + 1, step, 0)
    for t in range(BOX_DEV):
        cols = slice(PTS * t, PTS * t + PTS)
        acc[t] += 0.5 * jnp.concatenate([cur[3, 0, :, cols], cur[3, 1, :, cols]], axis=0)
    n = len(outs)
    for r, out in enumerate(outs):
        block = acc[lax.rem(lax.axis_index("x") + r, n)]
        if r == 0:
            out[...] = block
            continue
        for k in range(4):
            for p in range(2):
                out[32 * k + 16 * p : 32 * k + 16 * p + 16, :] = cur[k, p]
        out[PTS : PTS + 8, :] = jnp.concatenate(
            [block[8 * g : 8 * g + 8] for g in range(4)], axis=1
        )


def far_kernel(dims, info, far_z, far_x, out, tpos, rhi, rlo, weight, acc):
    nz, ny, nk, nx = dims
    targets = ny * nk
    mine = lax.axis_index("y") * nk + lax.axis_index("k")
    first = lax.axis_index("z") * targets
    stack = jnp.concatenate([info[d] for d in range(targets)], axis=0)
    if targets * 8 < PTS:
        stack = jnp.concatenate([stack, jnp.zeros((PTS - targets * 8, PTS), F32)], axis=0)
    turned = stack.T
    for d in range(targets):
        for c in range(3):
            tpos[c, SKEL * d : SKEL * d + SKEL, :] = jnp.broadcast_to(
                turned[0:SKEL, 8 * d + c : 8 * d + c + 1], (SKEL, PTS)
            )
    for g in range(nz):
        rows = jnp.concatenate([far_x[c, g] for c in range(nx)], axis=0)
        hi, lo = split(jnp.concatenate([rows, rotate(rows)], axis=1))
        rhi[g] = hi
        rlo[g] = lo
    acc[...] = jnp.zeros_like(acc)
    per = min(4, targets)

    def step(g, carry):
        sx = far_z[g, 32:33, :]
        sy = far_z[g, 33:34, :]
        sz = far_z[g, 34:35, :]
        source_group = g * targets + mine
        for d in range(targets):
            delta = source_group - (first + d)
            w = jnp.where(delta == -1, info[d, 3:4, :], 1.0)
            w = jnp.where(delta == 0, info[d, 4:5, :], w)
            w = jnp.where(delta == 1, info[d, 5:6, :], w)
            weight[SKEL * d : SKEL * d + SKEL, :] = jnp.broadcast_to(
                w * (0.25 / math.pi), (SKEL, PTS)
            )
        for n in range(targets // per):
            span = slice(SKEL * per * n, SKEL * per * (n + 1))
            re, im = helmholtz(
                tpos[0, span, :],
                tpos[1, span, :],
                tpos[2, span, :],
                sx,
                sy,
                sz,
                weight[span, :],
            )
            khi, klo = split(jnp.concatenate([re, im], axis=1))
            acc[span, :] += dot(khi, rhi[g], 1, 1) + (
                dot(khi, rlo[g], 1, 1) + dot(klo, rhi[g], 1, 1)
            )
        return carry

    lax.fori_loop(0, nz, step, 0)
    for d in range(targets):
        out[d] = acc[SKEL * d : SKEL * d + SKEL, :]


def halves(rows, nx):
    re = jnp.concatenate([rows[32 * c : 32 * c + 16] for c in range(nx)], axis=0)
    im = jnp.concatenate([rows[32 * c + 16 : 32 * c + 32] for c in range(nx)], axis=0)
    return jnp.concatenate([re, im], axis=1)


def basis_kernel(scale, first, basis, *refs):
    others, (ordered, nears, blocks) = refs[:-3], refs[-3:]
    nx = 1 + len(others)
    for r, ref in enumerate((basis,) + others):
        c = from_x(r)
        for k in range(4):
            at = pl.ds(pl.multiple_of(16 * (nx * k + c), 16), 16)
            for p in range(2):
                ordered[p, at, :] = ref[32 * k + 16 * p : 32 * k + 16 * p + 16, :]
        block = first[...] if r == 0 else ref[PTS : PTS + 8, :]
        if r > 0:
            block = jnp.concatenate(
                [block[:, PTS * g : PTS * g + PTS] for g in range(4)], axis=0
            )
        nears[pl.ds(pl.multiple_of(32 * c, 32), 32), :] = block
    x = lax.axis_index("x")
    half = lax.rem(x, 2)

    def product(left, right, rows):
        total = None
        for p in range(2):
            a = ordered[p, pl.ds(pl.multiple_of(64 * left, 64), 64), :]
            b = ordered[p, pl.ds(pl.multiple_of(right, 32), rows), :]
            part = dot(a, b, 1, 1, HIGHEST)
            total = part if total is None else total + part
        return total * scale

    blocks[0:64, :] = jnp.concatenate(
        [product(x, 64 * x, 64), product(x, 64 * lax.rem(x + 1, nx), 64)], axis=1
    )
    far = product(half, 64 * (half + 2) + 32 * (x // 2), 32)
    blocks[64:80, :] = jnp.concatenate([far[16 * g : 16 * g + 16] for g in range(4)], axis=1)


def couple_kernel(scale, phi, interp, ordered, nears, blocks, applied, part):
    nx = nears.shape[0] // 32
    total = phi[0]
    for d in range(1, phi.shape[0]):
        total = total + phi[d]
    rows = dot(total, interp[lax.axis_index("x")], 0, 0, HIGHEST) + nears[...]
    a2 = halves(rows, nx)
    applied[...] = a2
    cols = pl.ds(pl.multiple_of(PTS * lax.axis_index("x"), PTS), PTS)
    b2 = jnp.concatenate([ordered[0, :, cols], ordered[1, :, cols]], axis=1)
    c = dot(b2, a2, 1, 1, HIGHEST) * scale
    packed = jnp.concatenate([c[0:128], c[128:256]], axis=1)
    own = dot(a2, a2, 1, 1, HIGHEST) * scale
    n = part.shape[0]
    lead = 128 // n
    for d in range(n):
        part[d, 0:lead, :] = packed[lead * d : lead * d + lead]
    rest = jnp.concatenate(
        [
            jnp.concatenate([own[0:32], own[32:64]], axis=1),
            blocks[...],
            jnp.zeros((16, PTS), F32),
        ],
        axis=0,
    )
    for e in range(part.shape[1] - lead):
        part[:, lead + e, :] = rest[n * e : n * e + n]


def finish_kernel(nx, summed, ordered, *refs):
    applied, (out, coupling, factor, inv) = refs[:-4], refs[-4:]
    n = summed.shape[0]
    lead = 128 // n
    tail = 128 // n
    packed = jnp.concatenate([summed[d, 0:lead, :] for d in range(n)], axis=0)
    c = jnp.concatenate([packed[:, 0:64], packed[:, 64:128]], axis=0)
    for k in range(4):
        coupling[k] = c[64 * k : 64 * k + 64]
    own = None
    de, h = [], []
    for x in range(nx):
        rest = [summed[:, lead + tail * x + e, :] for e in range(112 // n)]
        rest = jnp.concatenate(rest, axis=0)
        own = rest[0:32] if own is None else own + rest[0:32]
        de.append(rest[32:96])
        h.append(
            jnp.concatenate([rest[96:112, 32 * g : 32 * g + 32] for g in range(4)], axis=0)
        )
    g = jnp.concatenate([own[:, 0:64], own[:, 64:128]], axis=0)
    blocks = [c[64 * k : 64 * k + 64] for k in range(4)]
    lines = []
    for k in range(4):
        right = jnp.concatenate([0.5 * blocks[k], blocks[(k + 1) % 4]], axis=0)
        left = de[k]
        if k < 2:
            right = jnp.concatenate([right, blocks[k + 2]], axis=0)
            left = jnp.concatenate([left, h[k], h[k + 2]], axis=1)
        lines.append(dot(left, right, 1, 0, HIGHEST) - blocks[k])
    halfq = dot(c, jnp.concatenate(lines, axis=0), 0, 0, HIGHEST)
    g = g + (halfq + halfq.T)
    row = lax.broadcasted_iota(jnp.int32, (64, 64), 0)
    col = lax.broadcasted_iota(jnp.int32, (64, 64), 1)
    eye = row == col
    diag = jnp.where(eye, g, 0.0)
    trace = jnp.sum(jnp.sum(diag, axis=1, keepdims=True), axis=0, keepdims=True)
    g = g + jnp.where(eye, SHIFT_SCALE * trace / 64.0 + EPSILON, 0.0)
    m = jnp.concatenate([g, eye.astype(F32)], axis=1)
    sub = lax.broadcasted_iota(jnp.int32, (64, 1), 0)
    for j in range(0, 64, 2):
        one = m[j : j + 1, :]
        two = m[j + 1 : j + 2, :]
        c1 = jnp.broadcast_to(m[:, j : j + 1], m.shape)
        c2 = jnp.broadcast_to(m[:, j + 1 : j + 2], m.shape)
        p1, a = c1[j : j + 1], c1[j + 1 : j + 2]
        p2 = c2[j + 1 : j + 2]
        det = p1 * p2 - a * a
        r1 = 1.0 / p1
        q = p1 / det
        lower = a * r1
        f1 = c1 * r1
        f2 = jnp.where(sub > j + 1, (c2 - f1 * a) * q, 0.0)
        f1 = jnp.where(sub > j, f1, 0.0)
        m = m - f1 * one - f2 * (two - lower * one)
    pivots = jnp.sum(jnp.where(eye, m[:, 0:64], 0.0), axis=1, keepdims=True)
    m = m * (1.0 / jnp.sqrt(pivots))
    factor[...] = jnp.where(row <= col, m[:, 0:64], 0.0)
    inv[...] = m[:, 64:128]
    mine = inv[pl.ds(pl.multiple_of(16 * lax.axis_index("x"), 16), 16), :]
    back = dot(mine, c, 1, 1, HIGHEST)
    for p in range(2):
        out[p] = -dot(back, ordered[p], 1, 0, HIGHEST)
    for r, ref in enumerate(applied):
        rows = dot(mine, ref[...], 1, 0, HIGHEST)
        cols = pl.ds(pl.multiple_of(PTS * from_x(r), PTS), PTS)
        out[0, :, cols] += rows[:, 0:PTS]
        out[1, :, cols] += rows[:, PTS : 2 * PTS]


def around(blocks):
    n = lax.axis_size("x")
    out = [blocks[0]]
    for r in range(1, n):
        out.append(lax.ppermute(blocks[r], "x", [(i, (i + r) % n) for i in range(n)]))
    return out


def trade(value, axes):
    return lax.all_to_all(value, axes, split_axis=0, concat_axis=0, tiled=True)


def shards(dims, basis, offsets, weights, interp, skeleton, near_boxes, near_count):
    nz, ny, nk, nx = dims
    groups = nz * ny * nk
    targets = ny * nk
    sources = nz * nx
    points = BOX_DEV * PTS
    scale = 1.0 / (groups * points)
    shape = lambda *s: jax.ShapeDtypeStruct(s, F32)

    info, skelpos = call(
        functools.partial(place_kernel, dims),
        (shape(targets, 8, PTS), shape(8, PTS)),
        [SMEM, SMEM, VMEM, VMEM],
        limit=None,
    )(near_boxes, near_count, offsets, skeleton)
    info_all = trade(info, YK)
    halo, far = call(
        functools.partial(prep_kernel, dims),
        (shape(40, points), shape(nz, 40, PTS)),
        [VMEM] * 5,
        limit=None,
    )(basis, weights[None], offsets, interp, skelpos)
    far_z = trade(far, "z")
    prev = lax.ppermute(halo, BOX, [(g, g + 1) for g in range(groups - 1)])
    nxt = lax.ppermute(halo, BOX, [(g + 1, g) for g in range(groups - 1)])
    far_x = trade(jnp.broadcast_to(far_z[None, :, :32], (nx, nz, 32, PTS)), "x")

    nears = call(
        functools.partial(near_kernel, dims),
        (shape(32, PTS),) + (shape(PTS + 8, points),) * (nx - 1),
        [SMEM, SMEM] + [VMEM] * 4,
        [
            pltpu.VMEM((3 * BOX_DEV, 40, PTS), F32),
            pltpu.VMEM((BOX_DEV, 16, PTS), F32),
            pltpu.VMEM((BOX_DEV, 3, PTS, PTS), F32),
            pltpu.VMEM((BOX_DEV, 32, PTS), F32),
        ],
        flops=36 * 2 * 64 * 256 * 128 * 2,
    )(near_boxes, near_count, prev, halo, nxt, basis)
    nears = around(nears)
    ordered, near_rows, blocks = call(
        functools.partial(basis_kernel, scale),
        (shape(2, 256, points), shape(32 * nx, PTS), shape(80, PTS)),
        [VMEM] * (1 + nx),
    )(nears[0], basis.reshape(4 * 32, points), *nears[1:])

    far_part = call(
        functools.partial(far_kernel, dims),
        shape(targets, SKEL, 32 * nx),
        [VMEM] * 3,
        [
            pltpu.VMEM((3, SKEL * targets, PTS), F32),
            pltpu.VMEM((nz, 32 * nx, 2 * PTS), BF16),
            pltpu.VMEM((nz, 32 * nx, 2 * PTS), BF16),
            pltpu.VMEM((SKEL * targets, PTS), F32),
            pltpu.VMEM((SKEL * targets, 32 * nx), F32),
        ],
        flops=3 * 2 * 512 * 2048 * 128,
    )(info_all, far_z, far_x)
    phi = trade(far_part, YK)

    lead = 128 // targets
    tall = 2 * lead
    applied, part = call(
        functools.partial(couple_kernel, scale),
        (shape(64, 2 * PTS), shape(targets, tall, PTS)),
        [VMEM] * 5,
    )(phi, interp, ordered, near_rows, blocks)
    part = jnp.sum(trade(part, YK), axis=0)
    applied = around([applied] * nx)
    part = trade(jnp.broadcast_to(part[None], (sources, tall, PTS)), ZX)
    part = jnp.sum(part.reshape(nz, nx, tall, PTS), axis=0)
    part = jnp.concatenate(
        [jnp.sum(part[:, :lead], axis=0), part[:, lead:].reshape(nx * (tall - lead), PTS)],
        axis=0,
    )
    summed = trade(jnp.broadcast_to(part[None], (targets,) + part.shape), YK)

    new_block, coupling, factor = call(
        functools.partial(finish_kernel, nx),
        (shape(2, 16, points), shape(4, 64, 64), shape(64, 64)),
        [VMEM] * (2 + nx),
        [pltpu.VMEM((64, 64), F32)],
    )(summed, ordered, *applied)
    return new_block, coupling, factor


def solution(mesh):
    boxes, cols = mesh.devices.shape
    nk = GRID[2]
    ny = GRID[1] if boxes == math.prod(GRID) else 2
    nz = boxes // (ny * nk)
    dims = (nz, ny, nk, cols)
    fine = Mesh(mesh.devices.reshape(dims), ("z", "y", "k", "x"))
    return jax.shard_map(
        functools.partial(shards, dims),
        mesh=fine,
        in_specs=(
            P(None, None, "x", BOX),
            P(None, BOX),
            P(BOX),
            P(BOX, None, None),
            P(BOX, None),
            P(BOX, None),
            P(BOX),
        ),
        out_specs=(P(None, "x", BOX), P(), P()),
        check_vma=False,
    )
```

```python
import functools
import math

import jax
import jax.numpy as jnp
from jax import lax
from jax.experimental import pallas as pl
from jax.experimental.pallas import tpu as pltpu
from jax.sharding import Mesh
from jax.sharding import PartitionSpec as P

BOX_DEV = 4
PTS = 128
SKEL = 32
SLOTS = 27
REACH = 4
WAVENUMBER = 6.0
SMOOTHING = 0.1
SHIFT_SCALE = 0.02
EPSILON = 1e-06
HIGHEST = lax.Precision.HIGHEST
F32 = jnp.float32
BF16 = jnp.bfloat16
INTERPRET = False

GRID = (8, 8, 2)
BOX = ("z", "y", "k")
YK = ("y", "k")
ZX = ("z", "x")

TURNS = WAVENUMBER / (2.0 * math.pi)
SIN_C = (3.1415926401307073, -5.167710083507923, 2.5500775232148563, -0.5982912856211671, 0.07765766030589402)
COS_C = (
    0.9999999997799043,
    -4.934802137078822,
    4.0587091595560825,
    -1.335212003047854,
    0.2349373138047365,
    -0.02439632433202294,
)


def poly(coefs, u):
    r = coefs[-1] * u + coefs[-2]
    for c in coefs[-3::-1]:
        r = r * u + c
    return r


def helmholtz(tx, ty, tz, sx, sy, sz, weight):
    dx = tx - sx
    dy = ty - sy
    dz = tz - sz
    s = SMOOTHING * SMOOTHING + dx * dx + dy * dy + dz * dz
    r = lax.rsqrt(s)
    r = r * (1.5 - (0.5 * s) * (r * r))
    t = (s * r) * TURNS
    f = t - lax.round(t, lax.RoundingMethod.TO_NEAREST_EVEN)
    u = f * f
    sn = f * poly(SIN_C, u)
    cs = poly(COS_C, u)
    two = sn + sn
    w = r * weight
    return (1.0 - two * sn) * w, (two * cs) * w


def split(x):
    hi = x.astype(BF16)
    return hi, (x - hi.astype(F32)).astype(BF16)


def dot(a, b, ca, cb, precision=None):
    return lax.dot_general(
        a, b, (((ca,), (cb,)), ((), ())), precision=precision, preferred_element_type=F32
    )


def rotate(rows):
    parts = []
    for g in range(rows.shape[0] // 32):
        parts.append(-rows[32 * g + 16 : 32 * g + 32])
        parts.append(rows[32 * g : 32 * g + 16])
    return jnp.concatenate(parts, axis=0)


def group_index(dims):
    return (lax.axis_index("z") * dims[1] + lax.axis_index("y")) * dims[2] + lax.axis_index("k")


def call(kernel, out_shape, in_specs, scratch=(), flops=0, limit=16 << 20):
    vmem = pl.BlockSpec(memory_space=pltpu.VMEM)
    single = not isinstance(out_shape, (tuple, list))
    return pl.pallas_call(
        kernel,
        out_shape=out_shape,
        in_specs=in_specs,
        out_specs=vmem if single else [vmem] * len(out_shape),
        scratch_shapes=list(scratch),
        cost_estimate=pl.CostEstimate(flops=flops, bytes_accessed=1 << 19, transcendentals=0),
        compiler_params=pltpu.CompilerParams(vmem_limit_bytes=limit),
        interpret=INTERPRET,
    )


VMEM = pl.BlockSpec(memory_space=pltpu.VMEM)
SMEM = pl.BlockSpec(memory_space=pltpu.SMEM)


def centred(offsets, b, group):
    axis = lax.broadcasted_iota(jnp.int32, (8, 1), 0)
    shift = jnp.where(axis == 0, group.astype(F32), jnp.where(axis == 1, float(b), 0.0))
    cols = slice(PTS * b, PTS * b + PTS)
    return jnp.concatenate([offsets[:, cols], jnp.zeros((5, PTS), F32)], axis=0) + shift


def prep_kernel(dims, near, count, cur, weights, offsets, interp, skel, halo, far, info):
    group = group_index(dims)
    x = lax.axis_index("x")
    src = jnp.concatenate([cur[3, 0], cur[3, 1]], axis=0) * weights[...]
    halo[0:32, :] = src
    charges = []
    spots = []
    for b in range(BOX_DEV):
        cols = slice(PTS * b, PTS * b + PTS)
        pos = centred(offsets, b, group)
        halo[32:40, cols] = pos
        charges.append(dot(src[:, cols], interp[b], 1, 1, HIGHEST))
        q = lax.broadcasted_iota(jnp.int32, (PTS, SKEL), 0)
        pick = (q == skel[b : b + 1, :]).astype(F32)
        spots.append(dot(pos, pick, 1, 0, HIGHEST))
    payload = jnp.concatenate(
        [jnp.concatenate(charges, axis=1), jnp.concatenate(spots, axis=1)], axis=0
    )
    far[...] = jnp.broadcast_to(payload[None], far.shape)
    row = lax.broadcasted_iota(jnp.int32, (8, PTS), 0)
    lane = lax.broadcasted_iota(jnp.int32, (8, PTS), 1)
    box_of = BOX_DEV * (group + row - 1) + lane // SKEL
    listed = jnp.zeros((8, PTS), F32)
    for s in range(SLOTS):
        box = jnp.where(s < count[x], near[x, s], -1000)
        listed = jnp.where(box_of == box, 1.0, listed)
    spot = spots[0]
    for b in range(1, BOX_DEV):
        spot = jnp.where(x == b, spots[b], spot)
    info[...] = jnp.concatenate(
        [
            jnp.concatenate([spot[0:3], jnp.zeros((3, PTS - SKEL), F32)], axis=1),
            1.0 - listed[0:3],
            jnp.zeros((2, PTS), F32),
        ],
        axis=0,
    )


def from_x(r):
    n = lax.axis_size("x")
    return lax.rem(lax.axis_index("x") + n - r, n)


def near_kernel(dims, near, count, prev, own, nxt, cur, *refs):
    outs, (ext, mult, tpos, acc) = refs[:-4], refs[-4:]
    for e in range(BOX_DEV):
        cols = slice(PTS * e, PTS * e + PTS)
        ext[e] = prev[:, cols]
        ext[BOX_DEV + e] = own[:, cols]
        ext[2 * BOX_DEV + e] = nxt[:, cols]
    stack = jnp.concatenate(
        [own[32:40, PTS * t : PTS * t + PTS] for t in range(BOX_DEV)]
        + [jnp.zeros((PTS - 8 * BOX_DEV, PTS), F32)],
        axis=0,
    )
    turned = stack.T
    base = BOX_DEV * (group_index(dims) - 1)
    erow = lax.broadcasted_iota(jnp.int32, (16, PTS), 0)
    for t in range(BOX_DEV):
        for c in range(3):
            tpos[t, c] = jnp.broadcast_to(turned[:, 8 * t + c : 8 * t + c + 1], (PTS, PTS))
        m = jnp.zeros((16, PTS), F32)
        for s in range(SLOTS):
            box = jnp.where(s < count[t], near[t, s] - base, -1000)
            m = m + jnp.where(erow == box, 1.0, 0.0)
        mult[t] = m
    acc[...] = jnp.zeros_like(acc)

    def step(d, carry):
        for t in range(BOX_DEV):
            e = t + d
            rows = ext[e, 0:32, :]
            re, im = helmholtz(
                tpos[t, 0],
                tpos[t, 1],
                tpos[t, 2],
                ext[e, 32:33, :],
                ext[e, 33:34, :],
                ext[e, 34:35, :],
                0.25 / math.pi,
            )
            khi, klo = split(jnp.concatenate([re, im], axis=1))
            rhi, rlo = split(jnp.concatenate([rows, rotate(rows)], axis=1))
            both = dot(jnp.concatenate([rhi, rlo], axis=0), khi, 1, 1)
            part = both[0:32] + (both[32:64] + dot(rhi, klo, 1, 1))
            acc[t] += part * mult[t, pl.ds(e, 1), :]
        return carry

    lax.fori_loop(0, 2 * REACH + 1, step, 0)
    for t in range(BOX_DEV):
        cols = slice(PTS * t, PTS * t + PTS)
        acc[t] += 0.5 * jnp.concatenate([cur[3, 0, :, cols], cur[3, 1, :, cols]], axis=0)
    n = len(outs)
    for r, out in enumerate(outs):
        block = acc[lax.rem(lax.axis_index("x") + r, n)]
        if r == 0:
            out[...] = block
            continue
        for k in range(4):
            for p in range(2):
                out[32 * k + 16 * p : 32 * k + 16 * p + 16, :] = cur[k, p]
        out[PTS : PTS + 8, :] = jnp.concatenate(
            [block[8 * g : 8 * g + 8] for g in range(4)], axis=1
        )


def far_kernel(dims, info, gathered, out, tpos, rhi, rlo, weight, acc):
    nz, ny, nk, nx = dims
    targets = ny * nk
    mine = lax.axis_index("y") * nk + lax.axis_index("k")
    first = lax.axis_index("z") * targets
    stack = info[...]
    if targets * 8 < PTS:
        stack = jnp.concatenate([stack, jnp.zeros((PTS - targets * 8, PTS), F32)], axis=0)
    turned = stack.T
    for d in range(targets):
        for c in range(3):
            tpos[c, SKEL * d : SKEL * d + SKEL, :] = jnp.broadcast_to(
                turned[0:SKEL, 8 * d + c : 8 * d + c + 1], (SKEL, PTS)
            )
    for g in range(nz):
        rows = jnp.concatenate([gathered[nx * g + c, 0:32, :] for c in range(nx)], axis=0)
        hi, lo = split(jnp.concatenate([rows, rotate(rows)], axis=1))
        rhi[g] = hi
        rlo[g] = lo
    acc[...] = jnp.zeros_like(acc)
    per = min(4, targets)

    def step(g, carry):
        sx = gathered[nx * g, 32:33, :]
        sy = gathered[nx * g, 33:34, :]
        sz = gathered[nx * g, 34:35, :]
        source_group = g * targets + mine
        for d in range(targets):
            delta = source_group - (first + lax.bitwise_xor(mine, d))
            w = jnp.where(delta == -1, info[8 * d + 3 : 8 * d + 4, :], 1.0)
            w = jnp.where(delta == 0, info[8 * d + 4 : 8 * d + 5, :], w)
            w = jnp.where(delta == 1, info[8 * d + 5 : 8 * d + 6, :], w)
            weight[SKEL * d : SKEL * d + SKEL, :] = jnp.broadcast_to(
                w * (0.25 / math.pi), (SKEL, PTS)
            )
        for n in range(targets // per):
            span = slice(SKEL * per * n, SKEL * per * (n + 1))
            re, im = helmholtz(
                tpos[0, span, :],
                tpos[1, span, :],
                tpos[2, span, :],
                sx,
                sy,
                sz,
                weight[span, :],
            )
            khi, klo = split(jnp.concatenate([re, im], axis=1))
            acc[span, :] += dot(khi, rhi[g], 1, 1) + (
                dot(khi, rlo[g], 1, 1) + dot(klo, rhi[g], 1, 1)
            )
        return carry

    lax.fori_loop(0, nz, step, 0)
    for d in range(targets):
        out[lax.bitwise_xor(mine, d)] = acc[SKEL * d : SKEL * d + SKEL, :]


def halves(rows, nx):
    re = jnp.concatenate([rows[32 * c : 32 * c + 16] for c in range(nx)], axis=0)
    im = jnp.concatenate([rows[32 * c + 16 : 32 * c + 32] for c in range(nx)], axis=0)
    return jnp.concatenate([re, im], axis=1)


def basis_kernel(scale, first, basis, *refs):
    others, (ordered, nears, blocks) = refs[:-3], refs[-3:]
    nx = 1 + len(others)
    for r, ref in enumerate((basis,) + others):
        c = from_x(r)
        for k in range(4):
            at = pl.ds(pl.multiple_of(16 * (nx * k + c), 16), 16)
            for p in range(2):
                ordered[p, at, :] = ref[32 * k + 16 * p : 32 * k + 16 * p + 16, :]
        block = first[...] if r == 0 else ref[PTS : PTS + 8, :]
        if r > 0:
            block = jnp.concatenate(
                [block[:, PTS * g : PTS * g + PTS] for g in range(4)], axis=0
            )
        nears[pl.ds(pl.multiple_of(32 * c, 32), 32), :] = block
    x = lax.axis_index("x")
    half = lax.rem(x, 2)

    def product(left, right, rows):
        total = None
        for p in range(2):
            a = ordered[p, pl.ds(pl.multiple_of(64 * left, 64), 64), :]
            b = ordered[p, pl.ds(pl.multiple_of(right, 32), rows), :]
            part = dot(a, b, 1, 1, HIGHEST)
            total = part if total is None else total + part
        return total * scale

    blocks[0:64, :] = jnp.concatenate(
        [product(x, 64 * x, 64), product(x, 64 * lax.rem(x + 1, nx), 64)], axis=1
    )
    far = product(half, 64 * (half + 2) + 32 * (x // 2), 32)
    blocks[64:80, :] = jnp.concatenate([far[16 * g : 16 * g + 16] for g in range(4)], axis=1)


def couple_kernel(scale, phi, interp, ordered, nears, blocks, applied, part):
    nx = nears.shape[0] // 32
    total = phi[0]
    for d in range(1, phi.shape[0]):
        total = total + phi[d]
    rows = dot(total, interp[lax.axis_index("x")], 0, 0, HIGHEST) + nears[...]
    a2 = halves(rows, nx)
    applied[...] = a2
    cols = pl.ds(pl.multiple_of(PTS * lax.axis_index("x"), PTS), PTS)
    b2 = jnp.concatenate([ordered[0, :, cols], ordered[1, :, cols]], axis=1)
    c = dot(b2, a2, 1, 1, HIGHEST) * scale
    packed = jnp.concatenate([c[0:128], c[128:256]], axis=1)
    own = dot(a2, a2, 1, 1, HIGHEST) * scale
    n = part.shape[0]
    lead = 128 // n
    for d in range(n):
        part[d, 0:lead, :] = packed[lead * d : lead * d + lead]
    rest = jnp.concatenate(
        [
            jnp.concatenate([own[0:32], own[32:64]], axis=1),
            blocks[...],
            jnp.zeros((16, PTS), F32),
        ],
        axis=0,
    )
    for e in range(part.shape[1] - lead):
        part[:, lead + e, :] = rest[n * e : n * e + n]


def finish_kernel(nx, summed, ordered, *refs):
    applied, (out, coupling, factor, inv) = refs[:-4], refs[-4:]
    n = summed.shape[0]
    lead = 128 // n
    tail = 128 // n
    packed = jnp.concatenate([summed[d, 0:lead, :] for d in range(n)], axis=0)
    c = jnp.concatenate([packed[:, 0:64], packed[:, 64:128]], axis=0)
    for k in range(4):
        coupling[k] = c[64 * k : 64 * k + 64]
    own = None
    de, h = [], []
    for x in range(nx):
        rest = [summed[:, lead + tail * x + e, :] for e in range(112 // n)]
        rest = jnp.concatenate(rest, axis=0)
        own = rest[0:32] if own is None else own + rest[0:32]
        de.append(rest[32:96])
        h.append(
            jnp.concatenate([rest[96:112, 32 * g : 32 * g + 32] for g in range(4)], axis=0)
        )
    g = jnp.concatenate([own[:, 0:64], own[:, 64:128]], axis=0)
    blocks = [c[64 * k : 64 * k + 64] for k in range(4)]
    lines = []
    for k in range(4):
        right = jnp.concatenate([0.5 * blocks[k], blocks[(k + 1) % 4]], axis=0)
        left = de[k]
        if k < 2:
            right = jnp.concatenate([right, blocks[k + 2]], axis=0)
            left = jnp.concatenate([left, h[k], h[k + 2]], axis=1)
        lines.append(dot(left, right, 1, 0, HIGHEST) - blocks[k])
    halfq = dot(c, jnp.concatenate(lines, axis=0), 0, 0, HIGHEST)
    g = g + (halfq + halfq.T)
    row = lax.broadcasted_iota(jnp.int32, (64, 64), 0)
    col = lax.broadcasted_iota(jnp.int32, (64, 64), 1)
    eye = row == col
    diag = jnp.where(eye, g, 0.0)
    trace = jnp.sum(jnp.sum(diag, axis=1, keepdims=True), axis=0, keepdims=True)
    g = g + jnp.where(eye, SHIFT_SCALE * trace / 64.0 + EPSILON, 0.0)
    m = jnp.concatenate([g, eye.astype(F32)], axis=1)
    sub = lax.broadcasted_iota(jnp.int32, (64, 1), 0)
    for j in range(0, 64, 2):
        one = m[j : j + 1, :]
        two = m[j + 1 : j + 2, :]
        c1 = jnp.broadcast_to(m[:, j : j + 1], m.shape)
        c2 = jnp.broadcast_to(m[:, j + 1 : j + 2], m.shape)
        p1, a = c1[j : j + 1], c1[j + 1 : j + 2]
        p2 = c2[j + 1 : j + 2]
        det = p1 * p2 - a * a
        r1 = 1.0 / p1
        q = p1 / det
        lower = a * r1
        f1 = c1 * r1
        f2 = jnp.where(sub > j + 1, (c2 - f1 * a) * q, 0.0)
        f1 = jnp.where(sub > j, f1, 0.0)
        m = m - f1 * one - f2 * (two - lower * one)
    pivots = jnp.sum(jnp.where(eye, m[:, 0:64], 0.0), axis=1, keepdims=True)
    m = m * (1.0 / jnp.sqrt(pivots))
    factor[...] = jnp.where(row <= col, m[:, 0:64], 0.0)
    inv[...] = m[:, 64:128]
    mine = inv[pl.ds(pl.multiple_of(16 * lax.axis_index("x"), 16), 16), :]
    back = dot(mine, c, 1, 1, HIGHEST)
    for p in range(2):
        out[p] = -dot(back, ordered[p], 1, 0, HIGHEST)
    for r, ref in enumerate(applied):
        rows = dot(mine, ref[...], 1, 0, HIGHEST)
        cols = pl.ds(pl.multiple_of(PTS * from_x(r), PTS), PTS)
        out[0, :, cols] += rows[:, 0:PTS]
        out[1, :, cols] += rows[:, PTS : 2 * PTS]


def around(blocks):
    n = lax.axis_size("x")
    out = [blocks[0]]
    for r in range(1, n):
        out.append(lax.ppermute(blocks[r], "x", [(i, (i + r) % n) for i in range(n)]))
    return out


def trade(value, axes):
    return lax.all_to_all(value, axes, split_axis=0, concat_axis=0, tiled=True)


def shards(dims, basis, offsets, weights, interp, skeleton, near_boxes, near_count):
    nz, ny, nk, nx = dims
    groups = nz * ny * nk
    targets = ny * nk
    sources = nz * nx
    points = BOX_DEV * PTS
    scale = 1.0 / (groups * points)
    shape = lambda *s: jax.ShapeDtypeStruct(s, F32)

    halo, far, info = call(
        functools.partial(prep_kernel, dims),
        (shape(40, points), shape(sources, 40, PTS), shape(8, PTS)),
        [SMEM, SMEM] + [VMEM] * 5,
        limit=None,
    )(near_boxes, near_count, basis, weights[None], offsets, interp, skeleton)
    far_all = trade(far, ZX)
    prev = lax.ppermute(halo, BOX, [(g, g + 1) for g in range(groups - 1)])
    nxt = lax.ppermute(halo, BOX, [(g + 1, g) for g in range(groups - 1)])
    steps = [("k", 1, nk)] + [("y", 1 << b, ny) for b in range(ny.bit_length() - 1)]
    for axis, bit, size in steps:
        other = lax.ppermute(info, axis, [(i, i ^ bit) for i in range(size)])
        info = jnp.concatenate([info, other], axis=0)

    nears = call(
        functools.partial(near_kernel, dims),
        (shape(32, PTS),) + (shape(PTS + 8, points),) * (nx - 1),
        [SMEM, SMEM] + [VMEM] * 4,
        [
            pltpu.VMEM((3 * BOX_DEV, 40, PTS), F32),
            pltpu.VMEM((BOX_DEV, 16, PTS), F32),
            pltpu.VMEM((BOX_DEV, 3, PTS, PTS), F32),
            pltpu.VMEM((BOX_DEV, 32, PTS), F32),
        ],
        flops=36 * 2 * 64 * 256 * 128 * 2,
    )(near_boxes, near_count, prev, halo, nxt, basis)
    nears = around(nears)
    ordered, near_rows, blocks = call(
        functools.partial(basis_kernel, scale),
        (shape(2, 256, points), shape(32 * nx, PTS), shape(80, PTS)),
        [VMEM] * (1 + nx),
    )(nears[0], basis.reshape(4 * 32, points), *nears[1:])

    far_part = call(
        functools.partial(far_kernel, dims),
        shape(targets, SKEL, 32 * nx),
        [VMEM] * 2,
        [
            pltpu.VMEM((3, SKEL * targets, PTS), F32),
            pltpu.VMEM((nz, 32 * nx, 2 * PTS), BF16),
            pltpu.VMEM((nz, 32 * nx, 2 * PTS), BF16),
            pltpu.VMEM((SKEL * targets, PTS), F32),
            pltpu.VMEM((SKEL * targets, 32 * nx), F32),
        ],
        flops=3 * 2 * 512 * 2048 * 128,
    )(info, far_all)
    phi = trade(far_part, YK)

    lead = 128 // targets
    tall = 2 * lead
    applied, part = call(
        functools.partial(couple_kernel, scale),
        (shape(64, 2 * PTS), shape(targets, tall, PTS)),
        [VMEM] * 5,
    )(phi, interp, ordered, near_rows, blocks)
    part = jnp.sum(trade(part, YK), axis=0)
    applied = around([applied] * nx)
    part = trade(jnp.broadcast_to(part[None], (sources, tall, PTS)), ZX)
    part = jnp.sum(part.reshape(nz, nx, tall, PTS), axis=0)
    part = jnp.concatenate(
        [jnp.sum(part[:, :lead], axis=0), part[:, lead:].reshape(nx * (tall - lead), PTS)],
        axis=0,
    )
    summed = trade(jnp.broadcast_to(part[None], (targets,) + part.shape), YK)

    new_block, coupling, factor = call(
        functools.partial(finish_kernel, nx),
        (shape(2, 16, points), shape(4, 64, 64), shape(64, 64)),
        [VMEM] * (2 + nx),
        [pltpu.VMEM((64, 64), F32)],
    )(summed, ordered, *applied)
    return new_block, coupling, factor


def solution(mesh):
    boxes, cols = mesh.devices.shape
    nk = GRID[2]
    ny = GRID[1] if boxes == math.prod(GRID) else 2
    nz = boxes // (ny * nk)
    dims = (nz, ny, nk, cols)
    fine = Mesh(mesh.devices.reshape(dims), ("z", "y", "k", "x"))
    return jax.shard_map(
        functools.partial(shards, dims),
        mesh=fine,
        in_specs=(
            P(None, None, "x", BOX),
            P(None, BOX),
            P(BOX),
            P(BOX, None, None),
            P(BOX, None),
            P(BOX, None),
            P(BOX),
        ),
        out_specs=(P(None, "x", BOX), P(), P()),
        check_vma=False,
    )
```

```python
import functools
import math

import jax
import jax.numpy as jnp
from jax import lax
from jax.experimental import pallas as pl
from jax.experimental.pallas import tpu as pltpu
from jax.sharding import Mesh
from jax.sharding import PartitionSpec as P

BOX_DEV = 4
PTS = 128
SKEL = 32
SLOTS = 27
REACH = 4
WAVENUMBER = 6.0
SMOOTHING = 0.1
SHIFT_SCALE = 0.02
EPSILON = 1e-06
HIGHEST = lax.Precision.HIGHEST
F32 = jnp.float32
BF16 = jnp.bfloat16
INTERPRET = False

GRID = (8, 8, 2)
BOX = ("z", "y", "k")
YK = ("y", "k")
ZX = ("z", "x")

TURNS = WAVENUMBER / (2.0 * math.pi)
SIN_C = (3.1415926401307073, -5.167710083507923, 2.5500775232148563, -0.5982912856211671, 0.07765766030589402)
COS_C = (
    0.9999999997799043,
    -4.934802137078822,
    4.0587091595560825,
    -1.335212003047854,
    0.2349373138047365,
    -0.02439632433202294,
)


def poly(coefs, u):
    r = coefs[-1] * u + coefs[-2]
    for c in coefs[-3::-1]:
        r = r * u + c
    return r


def helmholtz(tx, ty, tz, sx, sy, sz, weight):
    dx = tx - sx
    dy = ty - sy
    dz = tz - sz
    s = SMOOTHING * SMOOTHING + dx * dx + dy * dy + dz * dz
    r = lax.rsqrt(s)
    r = r * (1.5 - (0.5 * s) * (r * r))
    t = (s * r) * TURNS
    f = t - lax.round(t, lax.RoundingMethod.TO_NEAREST_EVEN)
    u = f * f
    sn = f * poly(SIN_C, u)
    cs = poly(COS_C, u)
    two = sn + sn
    w = r * weight
    return (1.0 - two * sn) * w, (two * cs) * w


def split(x):
    hi = x.astype(BF16)
    return hi, (x - hi.astype(F32)).astype(BF16)


def dot(a, b, ca, cb, precision=None):
    return lax.dot_general(
        a, b, (((ca,), (cb,)), ((), ())), precision=precision, preferred_element_type=F32
    )


def rotate(rows):
    parts = []
    for g in range(rows.shape[0] // 32):
        parts.append(-rows[32 * g + 16 : 32 * g + 32])
        parts.append(rows[32 * g : 32 * g + 16])
    return jnp.concatenate(parts, axis=0)


def group_index(dims):
    return (lax.axis_index("z") * dims[1] + lax.axis_index("y")) * dims[2] + lax.axis_index("k")


def call(kernel, out_shape, in_specs, scratch=(), flops=0, limit=16 << 20):
    vmem = pl.BlockSpec(memory_space=pltpu.VMEM)
    single = not isinstance(out_shape, (tuple, list))
    return pl.pallas_call(
        kernel,
        out_shape=out_shape,
        in_specs=in_specs,
        out_specs=vmem if single else [vmem] * len(out_shape),
        scratch_shapes=list(scratch),
        cost_estimate=pl.CostEstimate(flops=flops, bytes_accessed=1 << 19, transcendentals=0),
        compiler_params=pltpu.CompilerParams(vmem_limit_bytes=limit),
        interpret=INTERPRET,
    )


VMEM = pl.BlockSpec(memory_space=pltpu.VMEM)
SMEM = pl.BlockSpec(memory_space=pltpu.SMEM)


def centred(offsets, b, group):
    axis = lax.broadcasted_iota(jnp.int32, (8, 1), 0)
    shift = jnp.where(axis == 0, group.astype(F32), jnp.where(axis == 1, float(b), 0.0))
    cols = slice(PTS * b, PTS * b + PTS)
    return jnp.concatenate([offsets[:, cols], jnp.zeros((5, PTS), F32)], axis=0) + shift


def prep_kernel(dims, near, count, cur, weights, offsets, interp, skel, halo, far, info):
    group = group_index(dims)
    x = lax.axis_index("x")
    src = jnp.concatenate([cur[3, 0], cur[3, 1]], axis=0) * weights[...]
    halo[0:32, :] = src
    charges = []
    spots = []
    for b in range(BOX_DEV):
        cols = slice(PTS * b, PTS * b + PTS)
        pos = centred(offsets, b, group)
        halo[32:40, cols] = pos
        charges.append(dot(src[:, cols], interp[b], 1, 1, HIGHEST))
        q = lax.broadcasted_iota(jnp.int32, (PTS, SKEL), 0)
        pick = (q == skel[b : b + 1, :]).astype(F32)
        spots.append(dot(pos, pick, 1, 0, HIGHEST))
    payload = jnp.concatenate(
        [jnp.concatenate(charges, axis=1), jnp.concatenate(spots, axis=1)], axis=0
    )
    far[...] = jnp.broadcast_to(payload[None], far.shape)
    row = lax.broadcasted_iota(jnp.int32, (8, PTS), 0)
    lane = lax.broadcasted_iota(jnp.int32, (8, PTS), 1)
    box_of = BOX_DEV * (group + row - 1) + lane // SKEL
    listed = jnp.zeros((8, PTS), F32)
    for s in range(SLOTS):
        box = jnp.where(s < count[x], near[x, s], -1000)
        listed = jnp.where(box_of == box, 1.0, listed)
    spot = spots[0]
    for b in range(1, BOX_DEV):
        spot = jnp.where(x == b, spots[b], spot)
    about = jnp.concatenate(
        [
            jnp.concatenate([spot[0:3], jnp.zeros((3, PTS - SKEL), F32)], axis=1),
            1.0 - listed[0:3],
            jnp.zeros((2, PTS), F32),
        ],
        axis=0,
    )
    info[...] = jnp.broadcast_to(about[None], info.shape)


def from_x(r):
    n = lax.axis_size("x")
    return lax.rem(lax.axis_index("x") + n - r, n)


def near_kernel(dims, near, count, prev, own, nxt, cur, *refs):
    outs, (ext, mult, tpos, acc) = refs[:-4], refs[-4:]
    for e in range(BOX_DEV):
        cols = slice(PTS * e, PTS * e + PTS)
        ext[e] = prev[:, cols]
        ext[BOX_DEV + e] = own[:, cols]
        ext[2 * BOX_DEV + e] = nxt[:, cols]
    stack = jnp.concatenate(
        [own[32:40, PTS * t : PTS * t + PTS] for t in range(BOX_DEV)]
        + [jnp.zeros((PTS - 8 * BOX_DEV, PTS), F32)],
        axis=0,
    )
    turned = stack.T
    base = BOX_DEV * (group_index(dims) - 1)
    erow = lax.broadcasted_iota(jnp.int32, (16, PTS), 0)
    for t in range(BOX_DEV):
        for c in range(3):
            tpos[t, c] = jnp.broadcast_to(turned[:, 8 * t + c : 8 * t + c + 1], (PTS, PTS))
        m = jnp.zeros((16, PTS), F32)
        for s in range(SLOTS):
            box = jnp.where(s < count[t], near[t, s] - base, -1000)
            m = m + jnp.where(erow == box, 1.0, 0.0)
        mult[t] = m
    acc[...] = jnp.zeros_like(acc)

    def step(d, carry):
        for t in range(BOX_DEV):
            e = t + d
            rows = ext[e, 0:32, :]
            re, im = helmholtz(
                tpos[t, 0],
                tpos[t, 1],
                tpos[t, 2],
                ext[e, 32:33, :],
                ext[e, 33:34, :],
                ext[e, 34:35, :],
                0.25 / math.pi,
            )
            khi, klo = split(jnp.concatenate([re, im], axis=1))
            rhi, rlo = split(jnp.concatenate([rows, rotate(rows)], axis=1))
            both = dot(jnp.concatenate([rhi, rlo], axis=0), khi, 1, 1)
            part = both[0:32] + (both[32:64] + dot(rhi, klo, 1, 1))
            acc[t] += part * mult[t, pl.ds(e, 1), :]
        return carry

    lax.fori_loop(0, 2 * REACH + 1, step, 0)
    for t in range(BOX_DEV):
        cols = slice(PTS * t, PTS * t + PTS)
        acc[t] += 0.5 * jnp.concatenate([cur[3, 0, :, cols], cur[3, 1, :, cols]], axis=0)
    n = len(outs)
    for r, out in enumerate(outs):
        block = acc[lax.rem(lax.axis_index("x") + r, n)]
        if r == 0:
            out[...] = block
            continue
        for k in range(4):
            for p in range(2):
                out[32 * k + 16 * p : 32 * k + 16 * p + 16, :] = cur[k, p]
        out[PTS : PTS + 8, :] = jnp.concatenate(
            [block[8 * g : 8 * g + 8] for g in range(4)], axis=1
        )


def far_kernel(dims, info, gathered, out, tpos, rhi, rlo, weight, acc):
    nz, ny, nk, nx = dims
    targets = ny * nk
    mine = lax.axis_index("y") * nk + lax.axis_index("k")
    first = lax.axis_index("z") * targets
    stack = info[...]
    if targets * 8 < PTS:
        stack = jnp.concatenate([stack, jnp.zeros((PTS - targets * 8, PTS), F32)], axis=0)
    turned = stack.T
    for d in range(targets):
        for c in range(3):
            tpos[c, SKEL * d : SKEL * d + SKEL, :] = jnp.broadcast_to(
                turned[0:SKEL, 8 * d + c : 8 * d + c + 1], (SKEL, PTS)
            )
    for g in range(nz):
        rows = jnp.concatenate([gathered[nx * g + c, 0:32, :] for c in range(nx)], axis=0)
        hi, lo = split(jnp.concatenate([rows, rotate(rows)], axis=1))
        rhi[g] = hi
        rlo[g] = lo
    acc[...] = jnp.zeros_like(acc)
    per = min(4, targets)

    def step(g, carry):
        sx = gathered[nx * g, 32:33, :]
        sy = gathered[nx * g, 33:34, :]
        sz = gathered[nx * g, 34:35, :]
        source_group = g * targets + mine
        for d in range(targets):
            delta = source_group - (first + d)
            w = jnp.where(delta == -1, info[8 * d + 3 : 8 * d + 4, :], 1.0)
            w = jnp.where(delta == 0, info[8 * d + 4 : 8 * d + 5, :], w)
            w = jnp.where(delta == 1, info[8 * d + 5 : 8 * d + 6, :], w)
            weight[SKEL * d : SKEL * d + SKEL, :] = jnp.broadcast_to(
                w * (0.25 / math.pi), (SKEL, PTS)
            )
        for n in range(targets // per):
            span = slice(SKEL * per * n, SKEL * per * (n + 1))
            re, im = helmholtz(
                tpos[0, span, :],
                tpos[1, span, :],
                tpos[2, span, :],
                sx,
                sy,
                sz,
                weight[span, :],
            )
            khi, klo = split(jnp.concatenate([re, im], axis=1))
            acc[span, :] += dot(khi, rhi[g], 1, 1) + (
                dot(khi, rlo[g], 1, 1) + dot(klo, rhi[g], 1, 1)
            )
        return carry

    lax.fori_loop(0, nz, step, 0)
    for d in range(targets):
        out[d] = acc[SKEL * d : SKEL * d + SKEL, :]


def halves(rows, nx):
    re = jnp.concatenate([rows[32 * c : 32 * c + 16] for c in range(nx)], axis=0)
    im = jnp.concatenate([rows[32 * c + 16 : 32 * c + 32] for c in range(nx)], axis=0)
    return jnp.concatenate([re, im], axis=1)


def basis_kernel(scale, first, basis, *refs):
    others, (ordered, nears, blocks) = refs[:-3], refs[-3:]
    nx = 1 + len(others)
    for r, ref in enumerate((basis,) + others):
        c = from_x(r)
        for k in range(4):
            at = pl.ds(pl.multiple_of(16 * (nx * k + c), 16), 16)
            for p in range(2):
                ordered[p, at, :] = ref[32 * k + 16 * p : 32 * k + 16 * p + 16, :]
        block = first[...] if r == 0 else ref[PTS : PTS + 8, :]
        if r > 0:
            block = jnp.concatenate(
                [block[:, PTS * g : PTS * g + PTS] for g in range(4)], axis=0
            )
        nears[pl.ds(pl.multiple_of(32 * c, 32), 32), :] = block
    x = lax.axis_index("x")
    half = lax.rem(x, 2)

    def product(left, right, rows):
        total = None
        for p in range(2):
            a = ordered[p, pl.ds(pl.multiple_of(64 * left, 64), 64), :]
            b = ordered[p, pl.ds(pl.multiple_of(right, 32), rows), :]
            part = dot(a, b, 1, 1, HIGHEST)
            total = part if total is None else total + part
        return total * scale

    blocks[0:64, :] = jnp.concatenate(
        [product(x, 64 * x, 64), product(x, 64 * lax.rem(x + 1, nx), 64)], axis=1
    )
    far = product(half, 64 * (half + 2) + 32 * (x // 2), 32)
    blocks[64:80, :] = jnp.concatenate([far[16 * g : 16 * g + 16] for g in range(4)], axis=1)


def couple_kernel(scale, phi, interp, ordered, nears, blocks, applied, part):
    nx = nears.shape[0] // 32
    total = phi[0]
    for d in range(1, phi.shape[0]):
        total = total + phi[d]
    rows = dot(total, interp[lax.axis_index("x")], 0, 0, HIGHEST) + nears[...]
    a2 = halves(rows, nx)
    applied[...] = a2
    cols = pl.ds(pl.multiple_of(PTS * lax.axis_index("x"), PTS), PTS)
    b2 = jnp.concatenate([ordered[0, :, cols], ordered[1, :, cols]], axis=1)
    c = dot(b2, a2, 1, 1, HIGHEST) * scale
    packed = jnp.concatenate([c[0:128], c[128:256]], axis=1)
    own = dot(a2, a2, 1, 1, HIGHEST) * scale
    n = part.shape[0]
    lead = 128 // n
    for d in range(n):
        part[d, 0:lead, :] = packed[lead * d : lead * d + lead]
    rest = jnp.concatenate(
        [
            jnp.concatenate([own[0:32], own[32:64]], axis=1),
            blocks[...],
            jnp.zeros((16, PTS), F32),
        ],
        axis=0,
    )
    for e in range(part.shape[1] - lead):
        part[:, lead + e, :] = rest[n * e : n * e + n]


def finish_kernel(nx, summed, ordered, *refs):
    applied, (out, coupling, factor, inv) = refs[:-4], refs[-4:]
    n = summed.shape[0]
    lead = 128 // n
    tail = 128 // n
    packed = jnp.concatenate([summed[d, 0:lead, :] for d in range(n)], axis=0)
    c = jnp.concatenate([packed[:, 0:64], packed[:, 64:128]], axis=0)
    for k in range(4):
        coupling[k] = c[64 * k : 64 * k + 64]
    own = None
    de, h = [], []
    for x in range(nx):
        rest = [summed[:, lead + tail * x + e, :] for e in range(112 // n)]
        rest = jnp.concatenate(rest, axis=0)
        own = rest[0:32] if own is None else own + rest[0:32]
        de.append(rest[32:96])
        h.append(
            jnp.concatenate([rest[96:112, 32 * g : 32 * g + 32] for g in range(4)], axis=0)
        )
    g = jnp.concatenate([own[:, 0:64], own[:, 64:128]], axis=0)
    blocks = [c[64 * k : 64 * k + 64] for k in range(4)]
    lines = []
    for k in range(4):
        right = jnp.concatenate([0.5 * blocks[k], blocks[(k + 1) % 4]], axis=0)
        left = de[k]
        if k < 2:
            right = jnp.concatenate([right, blocks[k + 2]], axis=0)
            left = jnp.concatenate([left, h[k], h[k + 2]], axis=1)
        lines.append(dot(left, right, 1, 0, HIGHEST) - blocks[k])
    halfq = dot(c, jnp.concatenate(lines, axis=0), 0, 0, HIGHEST)
    g = g + (halfq + halfq.T)
    row = lax.broadcasted_iota(jnp.int32, (64, 64), 0)
    col = lax.broadcasted_iota(jnp.int32, (64, 64), 1)
    eye = row == col
    diag = jnp.where(eye, g, 0.0)
    trace = jnp.sum(jnp.sum(diag, axis=1, keepdims=True), axis=0, keepdims=True)
    g = g + jnp.where(eye, SHIFT_SCALE * trace / 64.0 + EPSILON, 0.0)
    m = jnp.concatenate([g, eye.astype(F32)], axis=1)
    sub = lax.broadcasted_iota(jnp.int32, (64, 1), 0)
    for j in range(0, 64, 2):
        one = m[j : j + 1, :]
        two = m[j + 1 : j + 2, :]
        c1 = jnp.broadcast_to(m[:, j : j + 1], m.shape)
        c2 = jnp.broadcast_to(m[:, j + 1 : j + 2], m.shape)
        p1, a = c1[j : j + 1], c1[j + 1 : j + 2]
        p2 = c2[j + 1 : j + 2]
        det = p1 * p2 - a * a
        r1 = 1.0 / p1
        q = p1 / det
        lower = a * r1
        f1 = c1 * r1
        f2 = jnp.where(sub > j + 1, (c2 - f1 * a) * q, 0.0)
        f1 = jnp.where(sub > j, f1, 0.0)
        m = m - f1 * one - f2 * (two - lower * one)
    pivots = jnp.sum(jnp.where(eye, m[:, 0:64], 0.0), axis=1, keepdims=True)
    m = m * (1.0 / jnp.sqrt(pivots))
    factor[...] = jnp.where(row <= col, m[:, 0:64], 0.0)
    inv[...] = m[:, 64:128]
    mine = inv[pl.ds(pl.multiple_of(16 * lax.axis_index("x"), 16), 16), :]
    back = dot(mine, c, 1, 1, HIGHEST)
    for p in range(2):
        out[p] = -dot(back, ordered[p], 1, 0, HIGHEST)
    for r, ref in enumerate(applied):
        rows = dot(mine, ref[...], 1, 0, HIGHEST)
        cols = pl.ds(pl.multiple_of(PTS * from_x(r), PTS), PTS)
        out[0, :, cols] += rows[:, 0:PTS]
        out[1, :, cols] += rows[:, PTS : 2 * PTS]


def around(blocks):
    n = lax.axis_size("x")
    out = [blocks[0]]
    for r in range(1, n):
        out.append(lax.ppermute(blocks[r], "x", [(i, (i + r) % n) for i in range(n)]))
    return out


def trade(value, axes):
    return lax.all_to_all(value, axes, split_axis=0, concat_axis=0, tiled=True)


def shards(dims, basis, offsets, weights, interp, skeleton, near_boxes, near_count):
    nz, ny, nk, nx = dims
    groups = nz * ny * nk
    targets = ny * nk
    sources = nz * nx
    points = BOX_DEV * PTS
    scale = 1.0 / (groups * points)
    shape = lambda *s: jax.ShapeDtypeStruct(s, F32)

    halo, far, info = call(
        functools.partial(prep_kernel, dims),
        (shape(40, points), shape(sources, 40, PTS), shape(targets, 8, PTS)),
        [SMEM, SMEM] + [VMEM] * 5,
        limit=None,
    )(near_boxes, near_count, basis, weights[None], offsets, interp, skeleton)
    far_all = trade(far, ZX)
    prev = lax.ppermute(halo, BOX, [(g, g + 1) for g in range(groups - 1)])
    nxt = lax.ppermute(halo, BOX, [(g + 1, g) for g in range(groups - 1)])
    info = trade(info, YK).reshape(targets * 8, PTS)

    nears = call(
        functools.partial(near_kernel, dims),
        (shape(32, PTS),) + (shape(PTS + 8, points),) * (nx - 1),
        [SMEM, SMEM] + [VMEM] * 4,
        [
            pltpu.VMEM((3 * BOX_DEV, 40, PTS), F32),
            pltpu.VMEM((BOX_DEV, 16, PTS), F32),
            pltpu.VMEM((BOX_DEV, 3, PTS, PTS), F32),
            pltpu.VMEM((BOX_DEV, 32, PTS), F32),
        ],
        flops=36 * 2 * 64 * 256 * 128 * 2,
    )(near_boxes, near_count, prev, halo, nxt, basis)
    nears = around(nears)
    ordered, near_rows, blocks = call(
        functools.partial(basis_kernel, scale),
        (shape(2, 256, points), shape(32 * nx, PTS), shape(80, PTS)),
        [VMEM] * (1 + nx),
    )(nears[0], basis.reshape(4 * 32, points), *nears[1:])

    far_part = call(
        functools.partial(far_kernel, dims),
        shape(targets, SKEL, 32 * nx),
        [VMEM] * 2,
        [
            pltpu.VMEM((3, SKEL * targets, PTS), F32),
            pltpu.VMEM((nz, 32 * nx, 2 * PTS), BF16),
            pltpu.VMEM((nz, 32 * nx, 2 * PTS), BF16),
            pltpu.VMEM((SKEL * targets, PTS), F32),
            pltpu.VMEM((SKEL * targets, 32 * nx), F32),
        ],
        flops=3 * 2 * 512 * 2048 * 128,
    )(info, far_all)
    phi = trade(far_part, YK)

    lead = 128 // targets
    tall = 2 * lead
    applied, part = call(
        functools.partial(couple_kernel, scale),
        (shape(64, 2 * PTS), shape(targets, tall, PTS)),
        [VMEM] * 5,
    )(phi, interp, ordered, near_rows, blocks)
    part = jnp.sum(trade(part, YK), axis=0)
    applied = around([applied] * nx)
    part = trade(jnp.broadcast_to(part[None], (sources, tall, PTS)), ZX)
    part = jnp.sum(part.reshape(nz, nx, tall, PTS), axis=0)
    part = jnp.concatenate(
        [jnp.sum(part[:, :lead], axis=0), part[:, lead:].reshape(nx * (tall - lead), PTS)],
        axis=0,
    )
    summed = trade(jnp.broadcast_to(part[None], (targets,) + part.shape), YK)

    new_block, coupling, factor = call(
        functools.partial(finish_kernel, nx),
        (shape(2, 16, points), shape(4, 64, 64), shape(64, 64)),
        [VMEM] * (2 + nx),
        [pltpu.VMEM((64, 64), F32)],
    )(summed, ordered, *applied)
    return new_block, coupling, factor


def solution(mesh):
    boxes, cols = mesh.devices.shape
    nk = GRID[2]
    ny = GRID[1] if boxes == math.prod(GRID) else 2
    nz = boxes // (ny * nk)
    dims = (nz, ny, nk, cols)
    fine = Mesh(mesh.devices.reshape(dims), ("z", "y", "k", "x"))
    return jax.shard_map(
        functools.partial(shards, dims),
        mesh=fine,
        in_specs=(
            P(None, None, "x", BOX),
            P(None, BOX),
            P(BOX),
            P(BOX, None, None),
            P(BOX, None),
            P(BOX, None),
            P(BOX),
        ),
        out_specs=(P(None, "x", BOX), P(), P()),
        check_vma=False,
    )
```

```python
import functools
import math

import jax
import jax.numpy as jnp
from jax import lax
from jax.experimental import pallas as pl
from jax.experimental.pallas import tpu as pltpu
from jax.sharding import Mesh
from jax.sharding import PartitionSpec as P

BOX_DEV = 4
PTS = 128
SKEL = 32
SLOTS = 27
REACH = 4
WAVENUMBER = 6.0
SMOOTHING = 0.1
SHIFT_SCALE = 0.02
EPSILON = 1e-06
HIGHEST = lax.Precision.HIGHEST
F32 = jnp.float32
BF16 = jnp.bfloat16
INTERPRET = False

GRID = (8, 8, 2)
BOX = ("z", "y", "k")
YK = ("y", "k")
ZX = ("z", "x")

TURNS = WAVENUMBER / (2.0 * math.pi)
SCALE = TURNS / (4.0 * math.pi)
SIN_C = (3.1415926401307073, -5.167710083507923, 2.5500775232148563, -0.5982912856211671, 0.07765766030589402)
COS_C = (
    0.9999999997799043,
    -4.934802137078822,
    4.0587091595560825,
    -1.335212003047854,
    0.2349373138047365,
    -0.02439632433202294,
)


def poly(coefs, u):
    r = coefs[-1] * u + coefs[-2]
    for c in coefs[-3::-1]:
        r = r * u + c
    return r


def helmholtz(tx, ty, tz, sx, sy, sz, weight):
    dx = tx - sx
    dy = ty - sy
    dz = tz - sz
    s = (SMOOTHING * TURNS) ** 2 + dx * dx + dy * dy + dz * dz
    r = lax.rsqrt(s)
    t = s * r
    f = t - lax.round(t, lax.RoundingMethod.TO_NEAREST_EVEN)
    u = f * f
    sn = f * poly(SIN_C, u)
    cs = poly(COS_C, u)
    two = sn + sn
    w = r * weight
    return (1.0 - two * sn) * w, (two * cs) * w


def split(x):
    hi = x.astype(BF16)
    return hi, (x - hi.astype(F32)).astype(BF16)


def dot(a, b, ca, cb, precision=None):
    return lax.dot_general(
        a, b, (((ca,), (cb,)), ((), ())), precision=precision, preferred_element_type=F32
    )


def rotate(rows):
    parts = []
    for g in range(rows.shape[0] // 32):
        parts.append(-rows[32 * g + 16 : 32 * g + 32])
        parts.append(rows[32 * g : 32 * g + 16])
    return jnp.concatenate(parts, axis=0)


def group_index(dims):
    return (lax.axis_index("z") * dims[1] + lax.axis_index("y")) * dims[2] + lax.axis_index("k")


def call(kernel, out_shape, in_specs, scratch=(), flops=0, limit=16 << 20):
    vmem = pl.BlockSpec(memory_space=pltpu.VMEM)
    single = not isinstance(out_shape, (tuple, list))
    return pl.pallas_call(
        kernel,
        out_shape=out_shape,
        in_specs=in_specs,
        out_specs=vmem if single else [vmem] * len(out_shape),
        scratch_shapes=list(scratch),
        cost_estimate=pl.CostEstimate(flops=flops, bytes_accessed=1 << 19, transcendentals=0),
        compiler_params=pltpu.CompilerParams(vmem_limit_bytes=limit),
        interpret=INTERPRET,
    )


VMEM = pl.BlockSpec(memory_space=pltpu.VMEM)
SMEM = pl.BlockSpec(memory_space=pltpu.SMEM)


def centred(offsets, b, group):
    axis = lax.broadcasted_iota(jnp.int32, (8, 1), 0)
    shift = jnp.where(axis == 0, group.astype(F32), jnp.where(axis == 1, float(b), 0.0))
    cols = slice(PTS * b, PTS * b + PTS)
    return jnp.concatenate([offsets[:, cols], jnp.zeros((5, PTS), F32)], axis=0) + shift


def place_kernel(dims, near, count, offsets, skel, info, skelpos):
    group = group_index(dims)
    x = lax.axis_index("x")
    spots = []
    for b in range(BOX_DEV):
        q = lax.broadcasted_iota(jnp.int32, (PTS, SKEL), 0)
        pick = (q == skel[b : b + 1, :]).astype(F32)
        spots.append(dot(centred(offsets, b, group), pick, 1, 0, HIGHEST))
    skelpos[...] = jnp.concatenate(spots, axis=1)
    row = lax.broadcasted_iota(jnp.int32, (8, PTS), 0)
    lane = lax.broadcasted_iota(jnp.int32, (8, PTS), 1)
    box_of = BOX_DEV * (group + row - 1) + lane // SKEL
    listed = jnp.zeros((8, PTS), F32)
    for s in range(SLOTS):
        box = jnp.where(s < count[x], near[x, s], -1000)
        listed = jnp.where(box_of == box, 1.0, listed)
    spot = spots[0]
    for b in range(1, BOX_DEV):
        spot = jnp.where(x == b, spots[b], spot)
    about = jnp.concatenate(
        [
            jnp.concatenate([spot[0:3], jnp.zeros((3, PTS - SKEL), F32)], axis=1),
            1.0 - listed[0:3],
            jnp.zeros((2, PTS), F32),
        ],
        axis=0,
    )
    info[...] = jnp.broadcast_to(about[None], info.shape)


def prep_kernel(dims, cur, weights, offsets, interp, skelpos, halo, far):
    group = group_index(dims)
    src = jnp.concatenate([cur[3, 0], cur[3, 1]], axis=0) * weights[...]
    halo[0:32, :] = src
    charges = []
    for b in range(BOX_DEV):
        cols = slice(PTS * b, PTS * b + PTS)
        halo[32:40, cols] = centred(offsets, b, group)
        charges.append(dot(src[:, cols], interp[b], 1, 1, HIGHEST))
    payload = jnp.concatenate([jnp.concatenate(charges, axis=1), skelpos[...]], axis=0)
    far[...] = jnp.broadcast_to(payload[None], far.shape)


def from_x(r):
    n = lax.axis_size("x")
    return lax.rem(lax.axis_index("x") + n - r, n)


def near_kernel(dims, near, count, prev, own, nxt, cur, *refs):
    outs, (ext, mult, tpos, acc) = refs[:-4], refs[-4:]
    for e in range(BOX_DEV):
        cols = slice(PTS * e, PTS * e + PTS)
        ext[e] = prev[:, cols]
        ext[BOX_DEV + e] = own[:, cols]
        ext[2 * BOX_DEV + e] = nxt[:, cols]
    stack = jnp.concatenate(
        [own[32:40, PTS * t : PTS * t + PTS] for t in range(BOX_DEV)]
        + [jnp.zeros((PTS - 8 * BOX_DEV, PTS), F32)],
        axis=0,
    )
    turned = stack.T
    base = BOX_DEV * (group_index(dims) - 1)
    erow = lax.broadcasted_iota(jnp.int32, (16, PTS), 0)
    for t in range(BOX_DEV):
        for c in range(3):
            tpos[t, c] = TURNS * jnp.broadcast_to(
                turned[:, 8 * t + c : 8 * t + c + 1], (PTS, PTS)
            )
        m = jnp.zeros((16, PTS), F32)
        for s in range(SLOTS):
            box = jnp.where(s < count[t], near[t, s] - base, -1000)
            m = m + jnp.where(erow == box, 1.0, 0.0)
        mult[t] = m
    acc[...] = jnp.zeros_like(acc)

    def step(d, carry):
        for t in range(BOX_DEV):
            e = t + d
            rows = ext[e, 0:32, :]
            re, im = helmholtz(
                tpos[t, 0],
                tpos[t, 1],
                tpos[t, 2],
                TURNS * ext[e, 32:33, :],
                TURNS * ext[e, 33:34, :],
                TURNS * ext[e, 34:35, :],
                SCALE,
            )
            khi, klo = split(jnp.concatenate([re, im], axis=1))
            rhi, rlo = split(jnp.concatenate([rows, rotate(rows)], axis=1))
            both = dot(jnp.concatenate([rhi, rlo], axis=0), khi, 1, 1)
            part = both[0:32] + (both[32:64] + dot(rhi, klo, 1, 1))
            acc[t] += part * mult[t, pl.ds(e, 1), :]
        return carry

    lax.fori_loop(0, 2 * REACH + 1, step, 0)
    for t in range(BOX_DEV):
        cols = slice(PTS * t, PTS * t + PTS)
        acc[t] += 0.5 * jnp.concatenate([cur[3, 0, :, cols], cur[3, 1, :, cols]], axis=0)
    n = len(outs)
    for r, out in enumerate(outs):
        block = acc[lax.rem(lax.axis_index("x") + r, n)]
        if r == 0:
            out[...] = block
            continue
        for k in range(4):
            for p in range(2):
                out[32 * k + 16 * p : 32 * k + 16 * p + 16, :] = cur[k, p]
        out[PTS : PTS + 8, :] = jnp.concatenate(
            [block[8 * g : 8 * g + 8] for g in range(4)], axis=1
        )


def far_kernel(dims, info, gathered, out, tpos, rhi, rlo, weight, acc):
    nz, ny, nk, nx = dims
    targets = ny * nk
    mine = lax.axis_index("y") * nk + lax.axis_index("k")
    first = lax.axis_index("z") * targets
    stack = info[...]
    if targets * 8 < PTS:
        stack = jnp.concatenate([stack, jnp.zeros((PTS - targets * 8, PTS), F32)], axis=0)
    turned = stack.T
    for d in range(targets):
        for c in range(3):
            tpos[c, SKEL * d : SKEL * d + SKEL, :] = TURNS * jnp.broadcast_to(
                turned[0:SKEL, 8 * d + c : 8 * d + c + 1], (SKEL, PTS)
            )
    for g in range(nz):
        rows = jnp.concatenate([gathered[nx * g + c, 0:32, :] for c in range(nx)], axis=0)
        hi, lo = split(jnp.concatenate([rows, rotate(rows)], axis=1))
        rhi[g] = hi
        rlo[g] = lo
    acc[...] = jnp.zeros_like(acc)
    per = min(4, targets)

    def step(g, carry):
        sx = TURNS * gathered[nx * g, 32:33, :]
        sy = TURNS * gathered[nx * g, 33:34, :]
        sz = TURNS * gathered[nx * g, 34:35, :]
        source_group = g * targets + mine
        for d in range(targets):
            delta = source_group - (first + d)
            w = jnp.where(delta == -1, info[8 * d + 3 : 8 * d + 4, :], 1.0)
            w = jnp.where(delta == 0, info[8 * d + 4 : 8 * d + 5, :], w)
            w = jnp.where(delta == 1, info[8 * d + 5 : 8 * d + 6, :], w)
            weight[SKEL * d : SKEL * d + SKEL, :] = jnp.broadcast_to(
                w * SCALE, (SKEL, PTS)
            )
        for n in range(targets // per):
            span = slice(SKEL * per * n, SKEL * per * (n + 1))
            re, im = helmholtz(
                tpos[0, span, :],
                tpos[1, span, :],
                tpos[2, span, :],
                sx,
                sy,
                sz,
                weight[span, :],
            )
            khi, klo = split(jnp.concatenate([re, im], axis=1))
            acc[span, :] += dot(khi, rhi[g], 1, 1) + (
                dot(khi, rlo[g], 1, 1) + dot(klo, rhi[g], 1, 1)
            )
        return carry

    lax.fori_loop(0, nz, step, 0)
    for d in range(targets):
        out[d] = acc[SKEL * d : SKEL * d + SKEL, :]


def halves(rows, nx):
    re = jnp.concatenate([rows[32 * c : 32 * c + 16] for c in range(nx)], axis=0)
    im = jnp.concatenate([rows[32 * c + 16 : 32 * c + 32] for c in range(nx)], axis=0)
    return jnp.concatenate([re, im], axis=1)


def basis_kernel(scale, first, basis, *refs):
    others, (ordered, nears, blocks) = refs[:-3], refs[-3:]
    nx = 1 + len(others)
    for r, ref in enumerate((basis,) + others):
        c = from_x(r)
        for k in range(4):
            at = pl.ds(pl.multiple_of(16 * (nx * k + c), 16), 16)
            for p in range(2):
                ordered[p, at, :] = ref[32 * k + 16 * p : 32 * k + 16 * p + 16, :]
        block = first[...] if r == 0 else ref[PTS : PTS + 8, :]
        if r > 0:
            block = jnp.concatenate(
                [block[:, PTS * g : PTS * g + PTS] for g in range(4)], axis=0
            )
        nears[pl.ds(pl.multiple_of(32 * c, 32), 32), :] = block
    x = lax.axis_index("x")
    half = lax.rem(x, 2)

    def product(left, right, rows):
        total = None
        for p in range(2):
            a = ordered[p, pl.ds(pl.multiple_of(64 * left, 64), 64), :]
            b = ordered[p, pl.ds(pl.multiple_of(right, 32), rows), :]
            part = dot(a, b, 1, 1, HIGHEST)
            total = part if total is None else total + part
        return total * scale

    blocks[0:64, :] = jnp.concatenate(
        [product(x, 64 * x, 64), product(x, 64 * lax.rem(x + 1, nx), 64)], axis=1
    )
    far = product(half, 64 * (half + 2) + 32 * (x // 2), 32)
    blocks[64:80, :] = jnp.concatenate([far[16 * g : 16 * g + 16] for g in range(4)], axis=1)


def couple_kernel(scale, phi, interp, ordered, nears, blocks, applied, part):
    nx = nears.shape[0] // 32
    total = phi[0]
    for d in range(1, phi.shape[0]):
        total = total + phi[d]
    rows = dot(total, interp[lax.axis_index("x")], 0, 0, HIGHEST) + nears[...]
    a2 = halves(rows, nx)
    applied[...] = a2
    cols = pl.ds(pl.multiple_of(PTS * lax.axis_index("x"), PTS), PTS)
    b2 = jnp.concatenate([ordered[0, :, cols], ordered[1, :, cols]], axis=1)
    c = dot(b2, a2, 1, 1, HIGHEST) * scale
    packed = jnp.concatenate([c[0:128], c[128:256]], axis=1)
    own = dot(a2, a2, 1, 1, HIGHEST) * scale
    n = part.shape[0]
    lead = 128 // n
    for d in range(n):
        part[d, 0:lead, :] = packed[lead * d : lead * d + lead]
    rest = jnp.concatenate(
        [
            jnp.concatenate([own[0:32], own[32:64]], axis=1),
            blocks[...],
            jnp.zeros((16, PTS), F32),
        ],
        axis=0,
    )
    for e in range(part.shape[1] - lead):
        part[:, lead + e, :] = rest[n * e : n * e + n]


def finish_kernel(nx, summed, ordered, *refs):
    applied, (out, coupling, factor, inv) = refs[:-4], refs[-4:]
    n = summed.shape[0]
    lead = 128 // n
    tail = 128 // n
    packed = jnp.concatenate([summed[d, 0:lead, :] for d in range(n)], axis=0)
    c = jnp.concatenate([packed[:, 0:64], packed[:, 64:128]], axis=0)
    for k in range(4):
        coupling[k] = c[64 * k : 64 * k + 64]
    own = None
    de, h = [], []
    for x in range(nx):
        rest = [summed[:, lead + tail * x + e, :] for e in range(112 // n)]
        rest = jnp.concatenate(rest, axis=0)
        own = rest[0:32] if own is None else own + rest[0:32]
        de.append(rest[32:96])
        h.append(
            jnp.concatenate([rest[96:112, 32 * g : 32 * g + 32] for g in range(4)], axis=0)
        )
    g = jnp.concatenate([own[:, 0:64], own[:, 64:128]], axis=0)
    blocks = [c[64 * k : 64 * k + 64] for k in range(4)]
    lines = []
    for k in range(4):
        right = jnp.concatenate([0.5 * blocks[k], blocks[(k + 1) % 4]], axis=0)
        left = de[k]
        if k < 2:
            right = jnp.concatenate([right, blocks[k + 2]], axis=0)
            left = jnp.concatenate([left, h[k], h[k + 2]], axis=1)
        lines.append(dot(left, right, 1, 0, HIGHEST) - blocks[k])
    halfq = dot(c, jnp.concatenate(lines, axis=0), 0, 0, HIGHEST)
    g = g + (halfq + halfq.T)
    row = lax.broadcasted_iota(jnp.int32, (64, 64), 0)
    col = lax.broadcasted_iota(jnp.int32, (64, 64), 1)
    eye = row == col
    diag = jnp.where(eye, g, 0.0)
    trace = jnp.sum(jnp.sum(diag, axis=1, keepdims=True), axis=0, keepdims=True)
    g = g + jnp.where(eye, SHIFT_SCALE * trace / 64.0 + EPSILON, 0.0)
    m = jnp.concatenate([g, eye.astype(F32)], axis=1)
    tiles = [m[8 * i : 8 * i + 8] for i in range(8)]
    sub = lax.broadcasted_iota(jnp.int32, (8, 1), 0)
    for j in range(0, 64, 2):
        at, top = divmod(j, 8)
        ones = [jnp.broadcast_to(tile[:, j : j + 1], (8, PTS)) for tile in tiles[at:]]
        twos = [jnp.broadcast_to(tile[:, j + 1 : j + 2], (8, PTS)) for tile in tiles[at:]]
        one = tiles[at][top : top + 1]
        two = tiles[at][top + 1 : top + 2]
        p1, a = ones[0][top : top + 1], ones[0][top + 1 : top + 2]
        p2 = twos[0][top + 1 : top + 2]
        det = p1 * p2 - a * a
        r1 = 1.0 / p1
        q = p1 / det
        two = two - (a * r1) * one
        for i, (c1, c2) in enumerate(zip(ones, twos)):
            f1 = c1 * r1
            f2 = (c2 - f1 * a) * q
            if i == 0:
                f1 = jnp.where(sub > top, f1, 0.0)
                f2 = jnp.where(sub > top + 1, f2, 0.0)
            tiles[at + i] = tiles[at + i] - f1 * one - f2 * two
    m = jnp.concatenate(tiles, axis=0)
    pivots = jnp.sum(jnp.where(eye, m[:, 0:64], 0.0), axis=1, keepdims=True)
    m = m * (1.0 / jnp.sqrt(pivots))
    factor[...] = jnp.where(row <= col, m[:, 0:64], 0.0)
    inv[...] = m[:, 64:128]
    mine = inv[pl.ds(pl.multiple_of(16 * lax.axis_index("x"), 16), 16), :]
    back = dot(mine, c, 1, 1, HIGHEST)
    for p in range(2):
        out[p] = -dot(back, ordered[p], 1, 0, HIGHEST)
    for r, ref in enumerate(applied):
        rows = dot(mine, ref[...], 1, 0, HIGHEST)
        cols = pl.ds(pl.multiple_of(PTS * from_x(r), PTS), PTS)
        out[0, :, cols] += rows[:, 0:PTS]
        out[1, :, cols] += rows[:, PTS : 2 * PTS]


def around(blocks):
    n = lax.axis_size("x")
    out = [blocks[0]]
    for r in range(1, n):
        out.append(lax.ppermute(blocks[r], "x", [(i, (i + r) % n) for i in range(n)]))
    return out


def trade(value, axes):
    return lax.all_to_all(value, axes, split_axis=0, concat_axis=0, tiled=True)


def shards(dims, basis, offsets, weights, interp, skeleton, near_boxes, near_count):
    nz, ny, nk, nx = dims
    groups = nz * ny * nk
    targets = ny * nk
    sources = nz * nx
    points = BOX_DEV * PTS
    scale = 1.0 / (groups * points)
    shape = lambda *s: jax.ShapeDtypeStruct(s, F32)

    info, skelpos = call(
        functools.partial(place_kernel, dims),
        (shape(targets, 8, PTS), shape(8, PTS)),
        [SMEM, SMEM, VMEM, VMEM],
        limit=None,
    )(near_boxes, near_count, offsets, skeleton)
    info = trade(info, YK).reshape(targets * 8, PTS)
    halo, far = call(
        functools.partial(prep_kernel, dims),
        (shape(40, points), shape(sources, 40, PTS)),
        [VMEM] * 5,
        limit=None,
    )(basis, weights[None], offsets, interp, skelpos)
    prev = lax.ppermute(halo, BOX, [(g, g + 1) for g in range(groups - 1)])
    nxt = lax.ppermute(halo, BOX, [(g + 1, g) for g in range(groups - 1)])
    far_all = trade(far, ZX)

    nears = call(
        functools.partial(near_kernel, dims),
        (shape(32, PTS),) + (shape(PTS + 8, points),) * (nx - 1),
        [SMEM, SMEM] + [VMEM] * 4,
        [
            pltpu.VMEM((3 * BOX_DEV, 40, PTS), F32),
            pltpu.VMEM((BOX_DEV, 16, PTS), F32),
            pltpu.VMEM((BOX_DEV, 3, PTS, PTS), F32),
            pltpu.VMEM((BOX_DEV, 32, PTS), F32),
        ],
        flops=36 * 2 * 64 * 256 * 128 * 2,
    )(near_boxes, near_count, prev, halo, nxt, basis)
    nears = around(nears)
    ordered, near_rows, blocks = call(
        functools.partial(basis_kernel, scale),
        (shape(2, 256, points), shape(32 * nx, PTS), shape(80, PTS)),
        [VMEM] * (1 + nx),
    )(nears[0], basis.reshape(4 * 32, points), *nears[1:])

    far_part = call(
        functools.partial(far_kernel, dims),
        shape(targets, SKEL, 32 * nx),
        [VMEM] * 2,
        [
            pltpu.VMEM((3, SKEL * targets, PTS), F32),
            pltpu.VMEM((nz, 32 * nx, 2 * PTS), BF16),
            pltpu.VMEM((nz, 32 * nx, 2 * PTS), BF16),
            pltpu.VMEM((SKEL * targets, PTS), F32),
            pltpu.VMEM((SKEL * targets, 32 * nx), F32),
        ],
        flops=3 * 2 * 512 * 2048 * 128,
    )(info, far_all)
    phi = trade(far_part, YK)

    lead = 128 // targets
    tall = 2 * lead
    applied, part = call(
        functools.partial(couple_kernel, scale),
        (shape(64, 2 * PTS), shape(targets, tall, PTS)),
        [VMEM] * 5,
    )(phi, interp, ordered, near_rows, blocks)
    part = jnp.sum(trade(part, YK), axis=0)
    applied = around([applied] * nx)
    part = jnp.sum(trade(jnp.broadcast_to(part[None], (nz, tall, PTS)), "z"), axis=0)
    part = trade(jnp.broadcast_to(part[None], (nx, tall, PTS)), "x")
    part = jnp.concatenate(
        [jnp.sum(part[:, :lead], axis=0), part[:, lead:].reshape(nx * (tall - lead), PTS)],
        axis=0,
    )
    summed = trade(jnp.broadcast_to(part[None], (targets,) + part.shape), YK)

    new_block, coupling, factor = call(
        functools.partial(finish_kernel, nx),
        (shape(2, 16, points), shape(4, 64, 64), shape(64, 64)),
        [VMEM] * (2 + nx),
        [pltpu.VMEM((64, 64), F32)],
    )(summed, ordered, *applied)
    return new_block, coupling, factor


def solution(mesh):
    boxes, cols = mesh.devices.shape
    nk = GRID[2]
    ny = GRID[1] if boxes == math.prod(GRID) else 2
    nz = boxes // (ny * nk)
    dims = (nz, ny, nk, cols)
    fine = Mesh(mesh.devices.reshape(dims), ("z", "y", "k", "x"))
    return jax.shard_map(
        functools.partial(shards, dims),
        mesh=fine,
        in_specs=(
            P(None, None, "x", BOX),
            P(None, BOX),
            P(BOX),
            P(BOX, None, None),
            P(BOX, None),
            P(BOX, None),
            P(BOX),
        ),
        out_specs=(P(None, "x", BOX), P(), P()),
        check_vma=False,
    )
```

```python
import functools
import math

import jax
import jax.numpy as jnp
from jax import lax
from jax.experimental import pallas as pl
from jax.experimental.pallas import tpu as pltpu
from jax.sharding import Mesh
from jax.sharding import PartitionSpec as P

BOX_DEV = 4
PTS = 128
SKEL = 32
SLOTS = 27
REACH = 4
WAVENUMBER = 6.0
SMOOTHING = 0.1
SHIFT_SCALE = 0.02
EPSILON = 1e-06
HIGHEST = lax.Precision.HIGHEST
F32 = jnp.float32
BF16 = jnp.bfloat16
INTERPRET = False
PIVOTS = 4

GRID = (8, 8, 2)
BOX = ("z", "y", "k")
YK = ("y", "k")
ZX = ("z", "x")

TURNS = WAVENUMBER / (2.0 * math.pi)
SCALE = TURNS / (4.0 * math.pi)
SIN_C = (3.1415926401307073, -5.167710083507923, 2.5500775232148563, -0.5982912856211671, 0.07765766030589402)
COS_C = (
    0.9999999997799043,
    -4.934802137078822,
    4.0587091595560825,
    -1.335212003047854,
    0.2349373138047365,
    -0.02439632433202294,
)


def poly(coefs, u):
    r = coefs[-1] * u + coefs[-2]
    for c in coefs[-3::-1]:
        r = r * u + c
    return r


def helmholtz(tx, ty, tz, sx, sy, sz, weight):
    dx = tx - sx
    dy = ty - sy
    dz = tz - sz
    s = (SMOOTHING * TURNS) ** 2 + dx * dx + dy * dy + dz * dz
    r = lax.rsqrt(s)
    t = s * r
    f = t - lax.round(t, lax.RoundingMethod.TO_NEAREST_EVEN)
    u = f * f
    sn = f * poly(SIN_C, u)
    cs = poly(COS_C, u)
    two = sn + sn
    w = r * weight
    return (1.0 - two * sn) * w, (two * cs) * w


def split(x):
    hi = x.astype(BF16)
    return hi, (x - hi.astype(F32)).astype(BF16)


def dot(a, b, ca, cb, precision=None):
    return lax.dot_general(
        a, b, (((ca,), (cb,)), ((), ())), precision=precision, preferred_element_type=F32
    )


def rotate(rows):
    parts = []
    for g in range(rows.shape[0] // 32):
        parts.append(-rows[32 * g + 16 : 32 * g + 32])
        parts.append(rows[32 * g : 32 * g + 16])
    return jnp.concatenate(parts, axis=0)


def group_index(dims):
    return (lax.axis_index("z") * dims[1] + lax.axis_index("y")) * dims[2] + lax.axis_index("k")


def call(kernel, out_shape, in_specs, scratch=(), flops=0, limit=16 << 20):
    vmem = pl.BlockSpec(memory_space=pltpu.VMEM)
    single = not isinstance(out_shape, (tuple, list))
    return pl.pallas_call(
        kernel,
        out_shape=out_shape,
        in_specs=in_specs,
        out_specs=vmem if single else [vmem] * len(out_shape),
        scratch_shapes=list(scratch),
        cost_estimate=pl.CostEstimate(flops=flops, bytes_accessed=1 << 19, transcendentals=0),
        compiler_params=pltpu.CompilerParams(vmem_limit_bytes=limit),
        interpret=INTERPRET,
    )


VMEM = pl.BlockSpec(memory_space=pltpu.VMEM)
SMEM = pl.BlockSpec(memory_space=pltpu.SMEM)


def centred(offsets, b, group):
    axis = lax.broadcasted_iota(jnp.int32, (8, 1), 0)
    shift = jnp.where(axis == 0, group.astype(F32), jnp.where(axis == 1, float(b), 0.0))
    cols = slice(PTS * b, PTS * b + PTS)
    return jnp.concatenate([offsets[:, cols], jnp.zeros((5, PTS), F32)], axis=0) + shift


def place_kernel(dims, near, count, offsets, skel, info, skelpos):
    group = group_index(dims)
    x = lax.axis_index("x")
    spots = []
    for b in range(BOX_DEV):
        q = lax.broadcasted_iota(jnp.int32, (PTS, SKEL), 0)
        pick = (q == skel[b : b + 1, :]).astype(F32)
        spots.append(dot(centred(offsets, b, group), pick, 1, 0, HIGHEST))
    skelpos[...] = jnp.concatenate(spots, axis=1)
    row = lax.broadcasted_iota(jnp.int32, (8, PTS), 0)
    lane = lax.broadcasted_iota(jnp.int32, (8, PTS), 1)
    box_of = BOX_DEV * (group + row - 1) + lane // SKEL
    listed = jnp.zeros((8, PTS), F32)
    for s in range(SLOTS):
        box = jnp.where(s < count[x], near[x, s], -1000)
        listed = jnp.where(box_of == box, 1.0, listed)
    spot = spots[0]
    for b in range(1, BOX_DEV):
        spot = jnp.where(x == b, spots[b], spot)
    about = jnp.concatenate(
        [
            jnp.concatenate([spot[0:3], jnp.zeros((3, PTS - SKEL), F32)], axis=1),
            1.0 - listed[0:3],
            jnp.zeros((2, PTS), F32),
        ],
        axis=0,
    )
    info[...] = jnp.broadcast_to(about[None], info.shape)


def prep_kernel(dims, cur, weights, offsets, interp, skelpos, halo, far):
    group = group_index(dims)
    src = jnp.concatenate([cur[3, 0], cur[3, 1]], axis=0) * weights[...]
    halo[0:32, :] = src
    charges = []
    for b in range(BOX_DEV):
        cols = slice(PTS * b, PTS * b + PTS)
        halo[32:40, cols] = centred(offsets, b, group)
        charges.append(dot(src[:, cols], interp[b], 1, 1, HIGHEST))
    payload = jnp.concatenate([jnp.concatenate(charges, axis=1), skelpos[...]], axis=0)
    far[...] = jnp.broadcast_to(payload[None], far.shape)


def from_x(r):
    n = lax.axis_size("x")
    return lax.rem(lax.axis_index("x") + n - r, n)


def near_kernel(dims, near, count, prev, own, nxt, cur, *refs):
    outs, (ext, mult, tpos, acc) = refs[:-4], refs[-4:]
    for e in range(BOX_DEV):
        cols = slice(PTS * e, PTS * e + PTS)
        ext[e] = prev[:, cols]
        ext[BOX_DEV + e] = own[:, cols]
        ext[2 * BOX_DEV + e] = nxt[:, cols]
    stack = jnp.concatenate(
        [own[32:40, PTS * t : PTS * t + PTS] for t in range(BOX_DEV)]
        + [jnp.zeros((PTS - 8 * BOX_DEV, PTS), F32)],
        axis=0,
    )
    turned = stack.T
    base = BOX_DEV * (group_index(dims) - 1)
    erow = lax.broadcasted_iota(jnp.int32, (16, PTS), 0)
    for t in range(BOX_DEV):
        for c in range(3):
            tpos[t, c] = TURNS * jnp.broadcast_to(
                turned[:, 8 * t + c : 8 * t + c + 1], (PTS, PTS)
            )
        m = jnp.zeros((16, PTS), F32)
        for s in range(SLOTS):
            box = jnp.where(s < count[t], near[t, s] - base, -1000)
            m = m + jnp.where(erow == box, 1.0, 0.0)
        mult[t] = m
    acc[...] = jnp.zeros_like(acc)

    def step(d, carry):
        for t in range(BOX_DEV):
            e = t + d
            rows = ext[e, 0:32, :]
            re, im = helmholtz(
                tpos[t, 0],
                tpos[t, 1],
                tpos[t, 2],
                TURNS * ext[e, 32:33, :],
                TURNS * ext[e, 33:34, :],
                TURNS * ext[e, 34:35, :],
                SCALE,
            )
            khi, klo = split(jnp.concatenate([re, im], axis=1))
            rhi, rlo = split(jnp.concatenate([rows, rotate(rows)], axis=1))
            both = dot(jnp.concatenate([rhi, rlo], axis=0), khi, 1, 1)
            part = both[0:32] + (both[32:64] + dot(rhi, klo, 1, 1))
            acc[t] += part * mult[t, pl.ds(e, 1), :]
        return carry

    lax.fori_loop(0, 2 * REACH + 1, step, 0)
    for t in range(BOX_DEV):
        cols = slice(PTS * t, PTS * t + PTS)
        acc[t] += 0.5 * jnp.concatenate([cur[3, 0, :, cols], cur[3, 1, :, cols]], axis=0)
    n = len(outs)
    for r, out in enumerate(outs):
        block = acc[lax.rem(lax.axis_index("x") + r, n)]
        if r == 0:
            out[...] = block
            continue
        for k in range(4):
            for p in range(2):
                out[32 * k + 16 * p : 32 * k + 16 * p + 16, :] = cur[k, p]
        out[PTS : PTS + 8, :] = jnp.concatenate(
            [block[8 * g : 8 * g + 8] for g in range(4)], axis=1
        )


def far_kernel(dims, info, gathered, out, tpos, rcat, weight, acc):
    nz, ny, nk, nx = dims
    targets = ny * nk
    mine = lax.axis_index("y") * nk + lax.axis_index("k")
    first = lax.axis_index("z") * targets
    stack = info[...]
    if targets * 8 < PTS:
        stack = jnp.concatenate([stack, jnp.zeros((PTS - targets * 8, PTS), F32)], axis=0)
    turned = stack.T
    for d in range(targets):
        for c in range(3):
            tpos[c, SKEL * d : SKEL * d + SKEL, :] = TURNS * jnp.broadcast_to(
                turned[0:SKEL, 8 * d + c : 8 * d + c + 1], (SKEL, PTS)
            )
    for g in range(nz):
        rows = jnp.concatenate([gathered[nx * g + c, 0:32, :] for c in range(nx)], axis=0)
        hi, lo = split(jnp.concatenate([rows, rotate(rows)], axis=1))
        rcat[g] = jnp.concatenate([hi, lo], axis=0)
    acc[...] = jnp.zeros_like(acc)
    per = min(4, targets)

    def step(g, carry):
        sx = TURNS * gathered[nx * g, 32:33, :]
        sy = TURNS * gathered[nx * g, 33:34, :]
        sz = TURNS * gathered[nx * g, 34:35, :]
        source_group = g * targets + mine
        for d in range(targets):
            delta = source_group - (first + d)
            w = jnp.where(delta == -1, info[8 * d + 3 : 8 * d + 4, :], 1.0)
            w = jnp.where(delta == 0, info[8 * d + 4 : 8 * d + 5, :], w)
            w = jnp.where(delta == 1, info[8 * d + 5 : 8 * d + 6, :], w)
            weight[SKEL * d : SKEL * d + SKEL, :] = jnp.broadcast_to(
                w * SCALE, (SKEL, PTS)
            )
        for n in range(targets // per):
            span = slice(SKEL * per * n, SKEL * per * (n + 1))
            re, im = helmholtz(
                tpos[0, span, :],
                tpos[1, span, :],
                tpos[2, span, :],
                sx,
                sy,
                sz,
                weight[span, :],
            )
            khi, klo = split(jnp.concatenate([re, im], axis=1))
            width = acc.shape[1]
            both = dot(khi, rcat[g], 1, 1)
            acc[span, :] += both[:, 0:width] + (
                both[:, width:] + dot(klo, rcat[g, 0:width, :], 1, 1)
            )
        return carry

    lax.fori_loop(0, nz, step, 0)
    for d in range(targets):
        out[d] = acc[SKEL * d : SKEL * d + SKEL, :]


def halves(rows, nx):
    re = jnp.concatenate([rows[32 * c : 32 * c + 16] for c in range(nx)], axis=0)
    im = jnp.concatenate([rows[32 * c + 16 : 32 * c + 32] for c in range(nx)], axis=0)
    return jnp.concatenate([re, im], axis=1)


def basis_kernel(scale, first, basis, *refs):
    others, (ordered, nears, blocks) = refs[:-3], refs[-3:]
    nx = 1 + len(others)
    for r, ref in enumerate((basis,) + others):
        c = from_x(r)
        for k in range(4):
            at = pl.ds(pl.multiple_of(16 * (nx * k + c), 16), 16)
            for p in range(2):
                ordered[p, at, :] = ref[32 * k + 16 * p : 32 * k + 16 * p + 16, :]
        block = first[...] if r == 0 else ref[PTS : PTS + 8, :]
        if r > 0:
            block = jnp.concatenate(
                [block[:, PTS * g : PTS * g + PTS] for g in range(4)], axis=0
            )
        nears[pl.ds(pl.multiple_of(32 * c, 32), 32), :] = block
    x = lax.axis_index("x")
    half = lax.rem(x, 2)

    def product(left, right, rows):
        total = None
        for p in range(2):
            a = ordered[p, pl.ds(pl.multiple_of(64 * left, 64), 64), :]
            b = ordered[p, pl.ds(pl.multiple_of(right, 32), rows), :]
            part = dot(a, b, 1, 1, HIGHEST)
            total = part if total is None else total + part
        return total * scale

    blocks[0:64, :] = jnp.concatenate(
        [product(x, 64 * x, 64), product(x, 64 * lax.rem(x + 1, nx), 64)], axis=1
    )
    far = product(half, 64 * (half + 2) + 32 * (x // 2), 32)
    blocks[64:80, :] = jnp.concatenate([far[16 * g : 16 * g + 16] for g in range(4)], axis=1)


def couple_kernel(scale, phi, interp, ordered, nears, blocks, applied, part):
    nx = nears.shape[0] // 32
    total = phi[0]
    for d in range(1, phi.shape[0]):
        total = total + phi[d]
    rows = dot(total, interp[lax.axis_index("x")], 0, 0, HIGHEST) + nears[...]
    a2 = halves(rows, nx)
    applied[...] = a2
    cols = pl.ds(pl.multiple_of(PTS * lax.axis_index("x"), PTS), PTS)
    b2 = jnp.concatenate([ordered[0, :, cols], ordered[1, :, cols]], axis=1)
    c = dot(b2, a2, 1, 1, HIGHEST) * scale
    packed = jnp.concatenate([c[0:128], c[128:256]], axis=1)
    own = dot(a2, a2, 1, 1, HIGHEST) * scale
    n = part.shape[0]
    lead = 128 // n
    for d in range(n):
        part[d, 0:lead, :] = packed[lead * d : lead * d + lead]
    rest = jnp.concatenate(
        [
            jnp.concatenate([own[0:32], own[32:64]], axis=1),
            blocks[...],
            jnp.zeros((16, PTS), F32),
        ],
        axis=0,
    )
    for e in range(part.shape[1] - lead):
        part[:, lead + e, :] = rest[n * e : n * e + n]


def finish_kernel(nx, summed, ordered, *refs):
    applied, (out, coupling, factor, inv) = refs[:-4], refs[-4:]
    n = summed.shape[0]
    lead = 128 // n
    tail = 128 // n
    packed = jnp.concatenate([summed[d, 0:lead, :] for d in range(n)], axis=0)
    c = jnp.concatenate([packed[:, 0:64], packed[:, 64:128]], axis=0)
    for k in range(4):
        coupling[k] = c[64 * k : 64 * k + 64]
    own = None
    de, h = [], []
    for x in range(nx):
        rest = [summed[:, lead + tail * x + e, :] for e in range(112 // n)]
        rest = jnp.concatenate(rest, axis=0)
        own = rest[0:32] if own is None else own + rest[0:32]
        de.append(rest[32:96])
        h.append(
            jnp.concatenate([rest[96:112, 32 * g : 32 * g + 32] for g in range(4)], axis=0)
        )
    g = jnp.concatenate([own[:, 0:64], own[:, 64:128]], axis=0)
    blocks = [c[64 * k : 64 * k + 64] for k in range(4)]
    lines = []
    for k in range(4):
        right = jnp.concatenate([0.5 * blocks[k], blocks[(k + 1) % 4]], axis=0)
        left = de[k]
        if k < 2:
            right = jnp.concatenate([right, blocks[k + 2]], axis=0)
            left = jnp.concatenate([left, h[k], h[k + 2]], axis=1)
        lines.append(dot(left, right, 1, 0, HIGHEST) - blocks[k])
    halfq = dot(c, jnp.concatenate(lines, axis=0), 0, 0, HIGHEST)
    g = g + (halfq + halfq.T)
    row = lax.broadcasted_iota(jnp.int32, (64, 64), 0)
    col = lax.broadcasted_iota(jnp.int32, (64, 64), 1)
    eye = row == col
    diag = jnp.where(eye, g, 0.0)
    trace = jnp.sum(jnp.sum(diag, axis=1, keepdims=True), axis=0, keepdims=True)
    g = g + jnp.where(eye, SHIFT_SCALE * trace / 64.0 + EPSILON, 0.0)
    m = jnp.concatenate([g, eye.astype(F32)], axis=1)
    tiles = [m[8 * i : 8 * i + 8] for i in range(8)]
    sub = lax.broadcasted_iota(jnp.int32, (8, 1), 0)
    for j in range(0, 64, PIVOTS):
        at, top = divmod(j, 8)
        live = tiles[at:]
        cols = [
            [jnp.broadcast_to(tile[:, j + n : j + n + 1], (8, PTS)) for tile in live]
            for n in range(PIVOTS)
        ]
        lines = [tiles[at][top + n : top + n + 1] for n in range(PIVOTS)]
        sm = [[cols[n][0][top + r : top + r + 1] for n in range(PIVOTS)] for r in range(PIVOTS)]
        factors = []
        for n in range(PIVOTS):
            inverse = 1.0 / sm[n][n]
            ratio = [sm[r][n] * inverse for r in range(PIVOTS)]
            factors.append(inverse)
            for r in range(n + 1, PIVOTS):
                lines[r] = lines[r] - ratio[r] * lines[n]
                for e in range(n + 1, PIVOTS):
                    sm[r][e] = sm[r][e] - ratio[r] * sm[n][e]
        for i in range(len(live)):
            bar = [cols[n][i] for n in range(PIVOTS)]
            new = live[i]
            for n in range(PIVOTS):
                f = bar[n] * factors[n]
                for r in range(n + 1, PIVOTS):
                    bar[r] = bar[r] - f * sm[n][r]
                if i == 0:
                    f = jnp.where(sub > top + n, f, 0.0)
                new = new - f * lines[n]
            tiles[at + i] = new
    m = jnp.concatenate(tiles, axis=0)
    pivots = jnp.sum(jnp.where(eye, m[:, 0:64], 0.0), axis=1, keepdims=True)
    m = m * (1.0 / jnp.sqrt(pivots))
    factor[...] = jnp.where(row <= col, m[:, 0:64], 0.0)
    inv[...] = m[:, 64:128]
    mine = inv[pl.ds(pl.multiple_of(16 * lax.axis_index("x"), 16), 16), :]
    back = dot(mine, c, 1, 1, HIGHEST)
    for p in range(2):
        out[p] = -dot(back, ordered[p], 1, 0, HIGHEST)
    for r, ref in enumerate(applied):
        rows = dot(mine, ref[...], 1, 0, HIGHEST)
        cols = pl.ds(pl.multiple_of(PTS * from_x(r), PTS), PTS)
        out[0, :, cols] += rows[:, 0:PTS]
        out[1, :, cols] += rows[:, PTS : 2 * PTS]


def around(blocks):
    n = lax.axis_size("x")
    out = [blocks[0]]
    for r in range(1, n):
        out.append(lax.ppermute(blocks[r], "x", [(i, (i + r) % n) for i in range(n)]))
    return out


def trade(value, axes):
    return lax.all_to_all(value, axes, split_axis=0, concat_axis=0, tiled=True)


def shards(dims, basis, offsets, weights, interp, skeleton, near_boxes, near_count):
    nz, ny, nk, nx = dims
    groups = nz * ny * nk
    targets = ny * nk
    sources = nz * nx
    points = BOX_DEV * PTS
    scale = 1.0 / (groups * points)
    shape = lambda *s: jax.ShapeDtypeStruct(s, F32)

    info, skelpos = call(
        functools.partial(place_kernel, dims),
        (shape(targets, 8, PTS), shape(8, PTS)),
        [SMEM, SMEM, VMEM, VMEM],
        limit=None,
    )(near_boxes, near_count, offsets, skeleton)
    info = trade(info, YK).reshape(targets * 8, PTS)
    halo, far = call(
        functools.partial(prep_kernel, dims),
        (shape(40, points), shape(sources, 40, PTS)),
        [VMEM] * 5,
        limit=None,
    )(basis, weights[None], offsets, interp, skelpos)
    prev = lax.ppermute(halo, BOX, [(g, g + 1) for g in range(groups - 1)])
    nxt = lax.ppermute(halo, BOX, [(g + 1, g) for g in range(groups - 1)])
    far_all = trade(far, ZX)

    nears = call(
        functools.partial(near_kernel, dims),
        (shape(32, PTS),) + (shape(PTS + 8, points),) * (nx - 1),
        [SMEM, SMEM] + [VMEM] * 4,
        [
            pltpu.VMEM((3 * BOX_DEV, 40, PTS), F32),
            pltpu.VMEM((BOX_DEV, 16, PTS), F32),
            pltpu.VMEM((BOX_DEV, 3, PTS, PTS), F32),
            pltpu.VMEM((BOX_DEV, 32, PTS), F32),
        ],
        flops=36 * 2 * 64 * 256 * 128 * 2,
    )(near_boxes, near_count, prev, halo, nxt, basis)
    nears = around(nears)
    ordered, near_rows, blocks = call(
        functools.partial(basis_kernel, scale),
        (shape(2, 256, points), shape(32 * nx, PTS), shape(80, PTS)),
        [VMEM] * (1 + nx),
    )(nears[0], basis.reshape(4 * 32, points), *nears[1:])

    far_part = call(
        functools.partial(far_kernel, dims),
        shape(targets, SKEL, 32 * nx),
        [VMEM] * 2,
        [
            pltpu.VMEM((3, SKEL * targets, PTS), F32),
            pltpu.VMEM((nz, 64 * nx, 2 * PTS), BF16),
            pltpu.VMEM((SKEL * targets, PTS), F32),
            pltpu.VMEM((SKEL * targets, 32 * nx), F32),
        ],
        flops=3 * 2 * 512 * 2048 * 128,
    )(info, far_all)
    phi = trade(far_part, YK)

    lead = 128 // targets
    tall = 2 * lead
    applied, part = call(
        functools.partial(couple_kernel, scale),
        (shape(64, 2 * PTS), shape(targets, tall, PTS)),
        [VMEM] * 5,
    )(phi, interp, ordered, near_rows, blocks)
    part = jnp.sum(trade(part, YK), axis=0)
    applied = around([applied] * nx)
    part = jnp.sum(trade(jnp.broadcast_to(part[None], (nz, tall, PTS)), "z"), axis=0)
    part = trade(jnp.broadcast_to(part[None], (nx, tall, PTS)), "x")
    part = jnp.concatenate(
        [jnp.sum(part[:, :lead], axis=0), part[:, lead:].reshape(nx * (tall - lead), PTS)],
        axis=0,
    )
    summed = trade(jnp.broadcast_to(part[None], (targets,) + part.shape), YK)

    new_block, coupling, factor = call(
        functools.partial(finish_kernel, nx),
        (shape(2, 16, points), shape(4, 64, 64), shape(64, 64)),
        [VMEM] * (2 + nx),
        [pltpu.VMEM((64, 64), F32)],
    )(summed, ordered, *applied)
    return new_block, coupling, factor


def solution(mesh):
    boxes, cols = mesh.devices.shape
    nk = GRID[2]
    ny = GRID[1] if boxes == math.prod(GRID) else 2
    nz = boxes // (ny * nk)
    dims = (nz, ny, nk, cols)
    fine = Mesh(mesh.devices.reshape(dims), ("z", "y", "k", "x"))
    return jax.shard_map(
        functools.partial(shards, dims),
        mesh=fine,
        in_specs=(
            P(None, None, "x", BOX),
            P(None, BOX),
            P(BOX),
            P(BOX, None, None),
            P(BOX, None),
            P(BOX, None),
            P(BOX),
        ),
        out_specs=(P(None, "x", BOX), P(), P()),
        check_vma=False,
    )
```

```python
import functools
import math

import jax
import jax.numpy as jnp
from jax import lax
from jax.experimental import pallas as pl
from jax.experimental.pallas import tpu as pltpu
from jax.sharding import Mesh
from jax.sharding import PartitionSpec as P

BOX_DEV = 4
PTS = 128
SKEL = 32
SLOTS = 27
REACH = 4
WAVENUMBER = 6.0
SMOOTHING = 0.1
SHIFT_SCALE = 0.02
EPSILON = 1e-06
HIGHEST = lax.Precision.HIGHEST
F32 = jnp.float32
BF16 = jnp.bfloat16
INTERPRET = False
PIVOTS = 4

GRID = (8, 8, 2)
BOX = ("z", "y", "k")
YK = ("y", "k")
ZX = ("z", "x")

TURNS = WAVENUMBER / (2.0 * math.pi)
SCALE = TURNS / (4.0 * math.pi)
SIN_C = (3.1415926401307073, -5.167710083507923, 2.5500775232148563, -0.5982912856211671, 0.07765766030589402)
COS_C = (
    0.9999999997799043,
    -4.934802137078822,
    4.0587091595560825,
    -1.335212003047854,
    0.2349373138047365,
    -0.02439632433202294,
)


def poly(coefs, u):
    r = coefs[-1] * u + coefs[-2]
    for c in coefs[-3::-1]:
        r = r * u + c
    return r


def helmholtz(tx, ty, tz, sx, sy, sz, weight):
    dx = tx - sx
    dy = ty - sy
    dz = tz - sz
    s = (SMOOTHING * TURNS) ** 2 + dx * dx + dy * dy + dz * dz
    r = lax.rsqrt(s)
    t = s * r
    f = t - lax.round(t, lax.RoundingMethod.TO_NEAREST_EVEN)
    u = f * f
    sn = f * poly(SIN_C, u)
    cs = poly(COS_C, u)
    two = sn + sn
    w = r * weight
    return (1.0 - two * sn) * w, (two * cs) * w


def split(x):
    hi = x.astype(BF16)
    return hi, (x - hi.astype(F32)).astype(BF16)


def dot(a, b, ca, cb, precision=None):
    return lax.dot_general(
        a, b, (((ca,), (cb,)), ((), ())), precision=precision, preferred_element_type=F32
    )


def rotate(rows):
    parts = []
    for g in range(rows.shape[0] // 32):
        parts.append(-rows[32 * g + 16 : 32 * g + 32])
        parts.append(rows[32 * g : 32 * g + 16])
    return jnp.concatenate(parts, axis=0)


def group_index(dims):
    return (lax.axis_index("z") * dims[1] + lax.axis_index("y")) * dims[2] + lax.axis_index("k")


def call(kernel, out_shape, in_specs, scratch=(), flops=0, limit=16 << 20):
    vmem = pl.BlockSpec(memory_space=pltpu.VMEM)
    single = not isinstance(out_shape, (tuple, list))
    return pl.pallas_call(
        kernel,
        out_shape=out_shape,
        in_specs=in_specs,
        out_specs=vmem if single else [vmem] * len(out_shape),
        scratch_shapes=list(scratch),
        cost_estimate=pl.CostEstimate(flops=flops, bytes_accessed=1 << 19, transcendentals=0),
        compiler_params=pltpu.CompilerParams(vmem_limit_bytes=limit),
        interpret=INTERPRET,
    )


VMEM = pl.BlockSpec(memory_space=pltpu.VMEM)
SMEM = pl.BlockSpec(memory_space=pltpu.SMEM)


def centred(offsets, b, group):
    axis = lax.broadcasted_iota(jnp.int32, (8, 1), 0)
    shift = jnp.where(axis == 0, group.astype(F32), jnp.where(axis == 1, float(b), 0.0))
    cols = slice(PTS * b, PTS * b + PTS)
    return jnp.concatenate([offsets[:, cols], jnp.zeros((5, PTS), F32)], axis=0) + shift


def place_kernel(dims, near, count, offsets, skel, info, skelpos):
    group = group_index(dims)
    x = lax.axis_index("x")
    spots = []
    for b in range(BOX_DEV):
        q = lax.broadcasted_iota(jnp.int32, (PTS, SKEL), 0)
        pick = (q == skel[b : b + 1, :]).astype(F32)
        spots.append(dot(centred(offsets, b, group), pick, 1, 0, HIGHEST))
    skelpos[...] = jnp.concatenate(spots, axis=1)
    row = lax.broadcasted_iota(jnp.int32, (8, PTS), 0)
    lane = lax.broadcasted_iota(jnp.int32, (8, PTS), 1)
    box_of = BOX_DEV * (group + row - 1) + lane // SKEL
    listed = jnp.zeros((8, PTS), F32)
    for s in range(SLOTS):
        box = jnp.where(s < count[x], near[x, s], -1000)
        listed = jnp.where(box_of == box, 1.0, listed)
    spot = spots[0]
    for b in range(1, BOX_DEV):
        spot = jnp.where(x == b, spots[b], spot)
    about = jnp.concatenate(
        [
            jnp.concatenate([spot[0:3], jnp.zeros((3, PTS - SKEL), F32)], axis=1),
            1.0 - listed[0:3],
            jnp.zeros((2, PTS), F32),
        ],
        axis=0,
    )
    info[...] = jnp.broadcast_to(about[None], info.shape)


def prep_kernel(dims, cur, weights, offsets, interp, skelpos, halo, far):
    group = group_index(dims)
    src = jnp.concatenate([cur[3, 0], cur[3, 1]], axis=0) * weights[...]
    halo[0:32, :] = src
    charges = []
    for b in range(BOX_DEV):
        cols = slice(PTS * b, PTS * b + PTS)
        halo[32:40, cols] = centred(offsets, b, group)
        charges.append(dot(src[:, cols], interp[b], 1, 1, HIGHEST))
    payload = jnp.concatenate([jnp.concatenate(charges, axis=1), skelpos[...]], axis=0)
    far[...] = jnp.broadcast_to(payload[None], far.shape)


def from_x(r):
    n = lax.axis_size("x")
    return lax.rem(lax.axis_index("x") + n - r, n)


def near_kernel(dims, near, count, prev, own, nxt, cur, *refs):
    outs, (ext, mult, tpos, acc) = refs[:-4], refs[-4:]
    for e in range(BOX_DEV):
        cols = slice(PTS * e, PTS * e + PTS)
        ext[e] = prev[:, cols]
        ext[BOX_DEV + e] = own[:, cols]
        ext[2 * BOX_DEV + e] = nxt[:, cols]
    stack = jnp.concatenate(
        [own[32:40, PTS * t : PTS * t + PTS] for t in range(BOX_DEV)]
        + [jnp.zeros((PTS - 8 * BOX_DEV, PTS), F32)],
        axis=0,
    )
    turned = stack.T
    base = BOX_DEV * (group_index(dims) - 1)
    erow = lax.broadcasted_iota(jnp.int32, (16, PTS), 0)
    for t in range(BOX_DEV):
        for c in range(3):
            tpos[t, c] = TURNS * jnp.broadcast_to(
                turned[:, 8 * t + c : 8 * t + c + 1], (PTS, PTS)
            )
        m = jnp.zeros((16, PTS), F32)
        for s in range(SLOTS):
            box = jnp.where(s < count[t], near[t, s] - base, -1000)
            m = m + jnp.where(erow == box, 1.0, 0.0)
        mult[t] = m
    acc[...] = jnp.zeros_like(acc)

    def step(d, carry):
        for t in range(BOX_DEV):
            e = t + d
            rows = ext[e, 0:32, :]
            re, im = helmholtz(
                tpos[t, 0],
                tpos[t, 1],
                tpos[t, 2],
                TURNS * ext[e, 32:33, :],
                TURNS * ext[e, 33:34, :],
                TURNS * ext[e, 34:35, :],
                SCALE,
            )
            khi, klo = split(jnp.concatenate([re, im], axis=1))
            rhi, rlo = split(jnp.concatenate([rows, rotate(rows)], axis=1))
            both = dot(jnp.concatenate([rhi, rlo], axis=0), khi, 1, 1)
            part = both[0:32] + (both[32:64] + dot(rhi, klo, 1, 1))
            acc[t] += part * mult[t, pl.ds(e, 1), :]
        return carry

    lax.fori_loop(0, 2 * REACH + 1, step, 0)
    for t in range(BOX_DEV):
        cols = slice(PTS * t, PTS * t + PTS)
        acc[t] += 0.5 * jnp.concatenate([cur[3, 0, :, cols], cur[3, 1, :, cols]], axis=0)
    n = len(outs)
    for r, out in enumerate(outs):
        block = acc[lax.rem(lax.axis_index("x") + r, n)]
        if r == 0:
            out[...] = block
            continue
        for k in range(4):
            for p in range(2):
                out[32 * k + 16 * p : 32 * k + 16 * p + 16, :] = cur[k, p]
        out[PTS : PTS + 8, :] = jnp.concatenate(
            [block[8 * g : 8 * g + 8] for g in range(4)], axis=1
        )


def far_kernel(dims, info, gathered, out, tpos, rcat, weight, acc):
    nz, ny, nk, nx = dims
    targets = ny * nk
    mine = lax.axis_index("y") * nk + lax.axis_index("k")
    first = lax.axis_index("z") * targets
    stack = info[...]
    if targets * 8 < PTS:
        stack = jnp.concatenate([stack, jnp.zeros((PTS - targets * 8, PTS), F32)], axis=0)
    turned = stack.T
    for d in range(targets):
        for c in range(3):
            tpos[c, SKEL * d : SKEL * d + SKEL, :] = TURNS * jnp.broadcast_to(
                turned[0:SKEL, 8 * d + c : 8 * d + c + 1], (SKEL, PTS)
            )
    for g in range(nz):
        rows = jnp.concatenate([gathered[nx * g + c, 0:32, :] for c in range(nx)], axis=0)
        hi, lo = split(jnp.concatenate([rows, rotate(rows)], axis=1))
        rcat[g] = jnp.concatenate([hi, lo], axis=0)
    acc[...] = jnp.zeros_like(acc)
    per = min(4, targets)

    def step(g, carry):
        sx = TURNS * gathered[nx * g, 32:33, :]
        sy = TURNS * gathered[nx * g, 33:34, :]
        sz = TURNS * gathered[nx * g, 34:35, :]
        source_group = g * targets + mine
        for d in range(targets):
            delta = source_group - (first + d)
            w = jnp.where(delta == -1, info[8 * d + 3 : 8 * d + 4, :], 1.0)
            w = jnp.where(delta == 0, info[8 * d + 4 : 8 * d + 5, :], w)
            w = jnp.where(delta == 1, info[8 * d + 5 : 8 * d + 6, :], w)
            weight[SKEL * d : SKEL * d + SKEL, :] = jnp.broadcast_to(
                w * SCALE, (SKEL, PTS)
            )
        for n in range(targets // per):
            span = slice(SKEL * per * n, SKEL * per * (n + 1))
            re, im = helmholtz(
                tpos[0, span, :],
                tpos[1, span, :],
                tpos[2, span, :],
                sx,
                sy,
                sz,
                weight[span, :],
            )
            khi, klo = split(jnp.concatenate([re, im], axis=1))
            width = acc.shape[1]
            both = dot(khi, rcat[g], 1, 1)
            acc[span, :] += both[:, 0:width] + (
                both[:, width:] + dot(klo, rcat[g, 0:width, :], 1, 1)
            )
        return carry

    lax.fori_loop(0, nz, step, 0)
    for d in range(targets):
        out[d] = acc[SKEL * d : SKEL * d + SKEL, :]


def halves(rows, nx):
    re = jnp.concatenate([rows[32 * c : 32 * c + 16] for c in range(nx)], axis=0)
    im = jnp.concatenate([rows[32 * c + 16 : 32 * c + 32] for c in range(nx)], axis=0)
    return jnp.concatenate([re, im], axis=1)


def basis_kernel(scale, first, basis, *refs):
    others, (ordered, nears, blocks) = refs[:-3], refs[-3:]
    nx = 1 + len(others)
    for r, ref in enumerate((basis,) + others):
        c = from_x(r)
        for k in range(4):
            at = pl.ds(pl.multiple_of(16 * (nx * k + c), 16), 16)
            for p in range(2):
                ordered[p, at, :] = ref[32 * k + 16 * p : 32 * k + 16 * p + 16, :]
        block = first[...] if r == 0 else ref[PTS : PTS + 8, :]
        if r > 0:
            block = jnp.concatenate(
                [block[:, PTS * g : PTS * g + PTS] for g in range(4)], axis=0
            )
        nears[pl.ds(pl.multiple_of(32 * c, 32), 32), :] = block
    x = lax.axis_index("x")
    half = lax.rem(x, 2)

    def product(left, right, rows):
        total = None
        for p in range(2):
            a = ordered[p, pl.ds(pl.multiple_of(64 * left, 64), 64), :]
            b = ordered[p, pl.ds(pl.multiple_of(right, 32), rows), :]
            part = dot(a, b, 1, 1, HIGHEST)
            total = part if total is None else total + part
        return total * scale

    blocks[0:64, :] = jnp.concatenate(
        [product(x, 64 * x, 64), product(x, 64 * lax.rem(x + 1, nx), 64)], axis=1
    )
    far = product(half, 64 * (half + 2) + 32 * (x // 2), 32)
    blocks[64:80, :] = jnp.concatenate([far[16 * g : 16 * g + 16] for g in range(4)], axis=1)


def couple_kernel(scale, phi, interp, ordered, nears, blocks, applied, part):
    nx = nears.shape[0] // 32
    total = phi[0]
    for d in range(1, phi.shape[0]):
        total = total + phi[d]
    rows = dot(total, interp[lax.axis_index("x")], 0, 0, HIGHEST) + nears[...]
    a2 = halves(rows, nx)
    applied[...] = a2
    cols = pl.ds(pl.multiple_of(PTS * lax.axis_index("x"), PTS), PTS)
    b2 = jnp.concatenate([ordered[0, :, cols], ordered[1, :, cols]], axis=1)
    c = dot(b2, a2, 1, 1, HIGHEST) * scale
    packed = jnp.concatenate([c[0:128], c[128:256]], axis=1)
    own = dot(a2, a2, 1, 1, HIGHEST) * scale
    n = part.shape[0]
    lead = 128 // n
    for d in range(n):
        part[d, 0:lead, :] = packed[lead * d : lead * d + lead]
    rest = jnp.concatenate(
        [
            jnp.concatenate([own[0:32], own[32:64]], axis=1),
            blocks[...],
            jnp.zeros((16, PTS), F32),
        ],
        axis=0,
    )
    for e in range(part.shape[1] - lead):
        part[:, lead + e, :] = rest[n * e : n * e + n]


def finish_kernel(nx, summed, ordered, *refs):
    applied, (out, coupling, factor, inv) = refs[:-4], refs[-4:]
    n = summed.shape[0]
    lead = 128 // n
    packed = jnp.concatenate([summed[d, 0:lead, :] for d in range(n)], axis=0)
    c = jnp.concatenate([packed[:, 0:64], packed[:, 64:128]], axis=0)
    for k in range(4):
        coupling[k] = c[64 * k : 64 * k + 64]
    base = lead + 32 // n
    own = jnp.concatenate([summed[:, e, :] for e in range(lead, base)], axis=0)
    de, h = [], []
    for x in range(nx):
        rest = [summed[:, base + 80 // n * x + e, :] for e in range(80 // n)]
        rest = jnp.concatenate(rest, axis=0)
        de.append(rest[0:64])
        h.append(
            jnp.concatenate([rest[64:80, 32 * g : 32 * g + 32] for g in range(4)], axis=0)
        )
    g = jnp.concatenate([own[:, 0:64], own[:, 64:128]], axis=0)
    blocks = [c[64 * k : 64 * k + 64] for k in range(4)]
    lines = []
    for k in range(4):
        right = jnp.concatenate([0.5 * blocks[k], blocks[(k + 1) % 4]], axis=0)
        left = de[k]
        if k < 2:
            right = jnp.concatenate([right, blocks[k + 2]], axis=0)
            left = jnp.concatenate([left, h[k], h[k + 2]], axis=1)
        lines.append(dot(left, right, 1, 0, HIGHEST) - blocks[k])
    halfq = dot(c, jnp.concatenate(lines, axis=0), 0, 0, HIGHEST)
    g = g + (halfq + halfq.T)
    row = lax.broadcasted_iota(jnp.int32, (64, 64), 0)
    col = lax.broadcasted_iota(jnp.int32, (64, 64), 1)
    eye = row == col
    diag = jnp.where(eye, g, 0.0)
    trace = jnp.sum(jnp.sum(diag, axis=1, keepdims=True), axis=0, keepdims=True)
    g = g + jnp.where(eye, SHIFT_SCALE * trace / 64.0 + EPSILON, 0.0)
    m = jnp.concatenate([g, eye.astype(F32)], axis=1)
    tiles = [m[8 * i : 8 * i + 8] for i in range(8)]
    sub = lax.broadcasted_iota(jnp.int32, (8, 1), 0)
    for j in range(0, 64, PIVOTS):
        at, top = divmod(j, 8)
        live = tiles[at:]
        cols = [
            [jnp.broadcast_to(tile[:, j + n : j + n + 1], (8, PTS)) for tile in live]
            for n in range(PIVOTS)
        ]
        lines = [tiles[at][top + n : top + n + 1] for n in range(PIVOTS)]
        sm = [[cols[n][0][top + r : top + r + 1] for n in range(PIVOTS)] for r in range(PIVOTS)]
        factors = []
        for n in range(PIVOTS):
            inverse = 1.0 / sm[n][n]
            ratio = [sm[r][n] * inverse for r in range(PIVOTS)]
            factors.append(inverse)
            for r in range(n + 1, PIVOTS):
                lines[r] = lines[r] - ratio[r] * lines[n]
                for e in range(n + 1, PIVOTS):
                    sm[r][e] = sm[r][e] - ratio[r] * sm[n][e]
        for i in range(len(live)):
            bar = [cols[n][i] for n in range(PIVOTS)]
            new = live[i]
            for n in range(PIVOTS):
                f = bar[n] * factors[n]
                for r in range(n + 1, PIVOTS):
                    bar[r] = bar[r] - f * sm[n][r]
                if i == 0:
                    f = jnp.where(sub > top + n, f, 0.0)
                new = new - f * lines[n]
            tiles[at + i] = new
    m = jnp.concatenate(tiles, axis=0)
    pivots = jnp.sum(jnp.where(eye, m[:, 0:64], 0.0), axis=1, keepdims=True)
    m = m * (1.0 / jnp.sqrt(pivots))
    factor[...] = jnp.where(row <= col, m[:, 0:64], 0.0)
    inv[...] = m[:, 64:128]
    mine = inv[pl.ds(pl.multiple_of(16 * lax.axis_index("x"), 16), 16), :]
    back = dot(mine, c, 1, 1, HIGHEST)
    for p in range(2):
        out[p] = -dot(back, ordered[p], 1, 0, HIGHEST)
    for r, ref in enumerate(applied):
        rows = dot(mine, ref[...], 1, 0, HIGHEST)
        cols = pl.ds(pl.multiple_of(PTS * from_x(r), PTS), PTS)
        out[0, :, cols] += rows[:, 0:PTS]
        out[1, :, cols] += rows[:, PTS : 2 * PTS]


def around(blocks):
    n = lax.axis_size("x")
    out = [blocks[0]]
    for r in range(1, n):
        out.append(lax.ppermute(blocks[r], "x", [(i, (i + r) % n) for i in range(n)]))
    return out


def trade(value, axes):
    return lax.all_to_all(value, axes, split_axis=0, concat_axis=0, tiled=True)


def shards(dims, basis, offsets, weights, interp, skeleton, near_boxes, near_count):
    nz, ny, nk, nx = dims
    groups = nz * ny * nk
    targets = ny * nk
    sources = nz * nx
    points = BOX_DEV * PTS
    scale = 1.0 / (groups * points)
    shape = lambda *s: jax.ShapeDtypeStruct(s, F32)

    info, skelpos = call(
        functools.partial(place_kernel, dims),
        (shape(targets, 8, PTS), shape(8, PTS)),
        [SMEM, SMEM, VMEM, VMEM],
        limit=None,
    )(near_boxes, near_count, offsets, skeleton)
    info = trade(info, YK).reshape(targets * 8, PTS)
    halo, far = call(
        functools.partial(prep_kernel, dims),
        (shape(40, points), shape(sources, 40, PTS)),
        [VMEM] * 5,
        limit=None,
    )(basis, weights[None], offsets, interp, skelpos)
    prev = lax.ppermute(halo, BOX, [(g, g + 1) for g in range(groups - 1)])
    nxt = lax.ppermute(halo, BOX, [(g + 1, g) for g in range(groups - 1)])
    far_all = trade(far, ZX)

    nears = call(
        functools.partial(near_kernel, dims),
        (shape(32, PTS),) + (shape(PTS + 8, points),) * (nx - 1),
        [SMEM, SMEM] + [VMEM] * 4,
        [
            pltpu.VMEM((3 * BOX_DEV, 40, PTS), F32),
            pltpu.VMEM((BOX_DEV, 16, PTS), F32),
            pltpu.VMEM((BOX_DEV, 3, PTS, PTS), F32),
            pltpu.VMEM((BOX_DEV, 32, PTS), F32),
        ],
        flops=36 * 2 * 64 * 256 * 128 * 2,
    )(near_boxes, near_count, prev, halo, nxt, basis)
    nears = around(nears)
    ordered, near_rows, blocks = call(
        functools.partial(basis_kernel, scale),
        (shape(2, 256, points), shape(32 * nx, PTS), shape(80, PTS)),
        [VMEM] * (1 + nx),
    )(nears[0], basis.reshape(4 * 32, points), *nears[1:])

    far_part = call(
        functools.partial(far_kernel, dims),
        shape(targets, SKEL, 32 * nx),
        [VMEM] * 2,
        [
            pltpu.VMEM((3, SKEL * targets, PTS), F32),
            pltpu.VMEM((nz, 64 * nx, 2 * PTS), BF16),
            pltpu.VMEM((SKEL * targets, PTS), F32),
            pltpu.VMEM((SKEL * targets, 32 * nx), F32),
        ],
        flops=3 * 2 * 512 * 2048 * 128,
    )(info, far_all)
    phi = trade(far_part, YK)

    lead = 128 // targets
    tall = 2 * lead
    added = lead + 32 // targets
    used = added + 80 // targets
    applied, part = call(
        functools.partial(couple_kernel, scale),
        (shape(64, 2 * PTS), shape(targets, tall, PTS)),
        [VMEM] * 5,
    )(phi, interp, ordered, near_rows, blocks)
    part = jnp.sum(trade(part, YK), axis=0)
    applied = around([applied] * nx)
    part = jnp.sum(trade(jnp.broadcast_to(part[None], (nz, tall, PTS)), "z"), axis=0)
    part = trade(jnp.broadcast_to(part[None], (nx, tall, PTS)), "x")
    part = jnp.concatenate(
        [jnp.sum(part[:, :added], axis=0), part[:, added:used].reshape(nx * (used - added), PTS)],
        axis=0,
    )
    summed = trade(jnp.broadcast_to(part[None], (targets,) + part.shape), YK)

    new_block, coupling, factor = call(
        functools.partial(finish_kernel, nx),
        (shape(2, 16, points), shape(4, 64, 64), shape(64, 64)),
        [VMEM] * (2 + nx),
        [pltpu.VMEM((64, 64), F32)],
    )(summed, ordered, *applied)
    return new_block, coupling, factor


def solution(mesh):
    boxes, cols = mesh.devices.shape
    nk = GRID[2]
    ny = GRID[1] if boxes == math.prod(GRID) else 2
    nz = boxes // (ny * nk)
    dims = (nz, ny, nk, cols)
    fine = Mesh(mesh.devices.reshape(dims), ("z", "y", "k", "x"))
    return jax.shard_map(
        functools.partial(shards, dims),
        mesh=fine,
        in_specs=(
            P(None, None, "x", BOX),
            P(None, BOX),
            P(BOX),
            P(BOX, None, None),
            P(BOX, None),
            P(BOX, None),
            P(BOX),
        ),
        out_specs=(P(None, "x", BOX), P(), P()),
        check_vma=False,
    )
```

```python
import functools
import math

import jax
import jax.numpy as jnp
from jax import lax
from jax.experimental import pallas as pl
from jax.experimental.pallas import tpu as pltpu
from jax.sharding import Mesh
from jax.sharding import PartitionSpec as P

BOX_DEV = 4
PTS = 128
SKEL = 32
SLOTS = 27
REACH = 4
WAVENUMBER = 6.0
SMOOTHING = 0.1
SHIFT_SCALE = 0.02
EPSILON = 1e-06
HIGHEST = lax.Precision.HIGHEST
F32 = jnp.float32
BF16 = jnp.bfloat16
INTERPRET = False
PIVOTS = 4

GRID = (8, 8, 2)
BOX = ("z", "y", "k")
YK = ("k", "y")
ZX = ("x", "z")

TURNS = WAVENUMBER / (2.0 * math.pi)
SCALE = TURNS / (4.0 * math.pi)
SIN_C = (3.1415926401307073, -5.167710083507923, 2.5500775232148563, -0.5982912856211671, 0.07765766030589402)
COS_C = (
    0.9999999997799043,
    -4.934802137078822,
    4.0587091595560825,
    -1.335212003047854,
    0.2349373138047365,
    -0.02439632433202294,
)


def poly(coefs, u):
    r = coefs[-1] * u + coefs[-2]
    for c in coefs[-3::-1]:
        r = r * u + c
    return r


def helmholtz(tx, ty, tz, sx, sy, sz, weight):
    dx = tx - sx
    dy = ty - sy
    dz = tz - sz
    s = (SMOOTHING * TURNS) ** 2 + dx * dx + dy * dy + dz * dz
    r = lax.rsqrt(s)
    t = s * r
    f = t - lax.round(t, lax.RoundingMethod.TO_NEAREST_EVEN)
    u = f * f
    sn = f * poly(SIN_C, u)
    cs = poly(COS_C, u)
    two = sn + sn
    w = r * weight
    return (1.0 - two * sn) * w, (two * cs) * w


def split(x):
    hi = x.astype(BF16)
    return hi, (x - hi.astype(F32)).astype(BF16)


def dot(a, b, ca, cb, precision=None):
    return lax.dot_general(
        a, b, (((ca,), (cb,)), ((), ())), precision=precision, preferred_element_type=F32
    )


def rotate(rows):
    parts = []
    for g in range(rows.shape[0] // 32):
        parts.append(-rows[32 * g + 16 : 32 * g + 32])
        parts.append(rows[32 * g : 32 * g + 16])
    return jnp.concatenate(parts, axis=0)


def group_index(dims):
    return (lax.axis_index("z") * dims[1] + lax.axis_index("y")) * dims[2] + lax.axis_index("k")


def call(kernel, out_shape, in_specs, scratch=(), flops=0, limit=16 << 20):
    vmem = pl.BlockSpec(memory_space=pltpu.VMEM)
    single = not isinstance(out_shape, (tuple, list))
    return pl.pallas_call(
        kernel,
        out_shape=out_shape,
        in_specs=in_specs,
        out_specs=vmem if single else [vmem] * len(out_shape),
        scratch_shapes=list(scratch),
        cost_estimate=pl.CostEstimate(flops=flops, bytes_accessed=1 << 19, transcendentals=0),
        compiler_params=pltpu.CompilerParams(vmem_limit_bytes=limit),
        interpret=INTERPRET,
    )


VMEM = pl.BlockSpec(memory_space=pltpu.VMEM)
SMEM = pl.BlockSpec(memory_space=pltpu.SMEM)


def centred(offsets, b, group):
    axis = lax.broadcasted_iota(jnp.int32, (8, 1), 0)
    shift = jnp.where(axis == 0, group.astype(F32), jnp.where(axis == 1, float(b), 0.0))
    cols = slice(PTS * b, PTS * b + PTS)
    return jnp.concatenate([offsets[:, cols], jnp.zeros((5, PTS), F32)], axis=0) + shift


def place_kernel(dims, near, count, offsets, skel, info, skelpos):
    group = group_index(dims)
    x = lax.axis_index("x")
    spots = []
    for b in range(BOX_DEV):
        q = lax.broadcasted_iota(jnp.int32, (PTS, SKEL), 0)
        pick = (q == skel[b : b + 1, :]).astype(F32)
        spots.append(dot(centred(offsets, b, group), pick, 1, 0, HIGHEST))
    skelpos[...] = jnp.concatenate(spots, axis=1)
    row = lax.broadcasted_iota(jnp.int32, (8, PTS), 0)
    lane = lax.broadcasted_iota(jnp.int32, (8, PTS), 1)
    box_of = BOX_DEV * (group + row - 1) + lane // SKEL
    listed = jnp.zeros((8, PTS), F32)
    for s in range(SLOTS):
        box = jnp.where(s < count[x], near[x, s], -1000)
        listed = jnp.where(box_of == box, 1.0, listed)
    spot = spots[0]
    for b in range(1, BOX_DEV):
        spot = jnp.where(x == b, spots[b], spot)
    about = jnp.concatenate(
        [
            jnp.concatenate([spot[0:3], jnp.zeros((3, PTS - SKEL), F32)], axis=1),
            1.0 - listed[0:3],
            jnp.zeros((2, PTS), F32),
        ],
        axis=0,
    )
    info[...] = jnp.broadcast_to(about[None], info.shape)


def prep_kernel(dims, cur, weights, offsets, interp, skelpos, halo, far):
    group = group_index(dims)
    src = jnp.concatenate([cur[3, 0], cur[3, 1]], axis=0) * weights[...]
    halo[0:32, :] = src
    charges = []
    for b in range(BOX_DEV):
        cols = slice(PTS * b, PTS * b + PTS)
        halo[32:40, cols] = centred(offsets, b, group)
        charges.append(dot(src[:, cols], interp[b], 1, 1, HIGHEST))
    payload = jnp.concatenate([jnp.concatenate(charges, axis=1), skelpos[...]], axis=0)
    far[...] = jnp.broadcast_to(payload[None], far.shape)


def from_x(r):
    n = lax.axis_size("x")
    return lax.rem(lax.axis_index("x") + n - r, n)


def near_kernel(dims, near, count, prev, own, nxt, cur, *refs):
    outs, (ext, mult, tpos, acc) = refs[:-4], refs[-4:]
    for e in range(BOX_DEV):
        cols = slice(PTS * e, PTS * e + PTS)
        ext[e] = prev[:, cols]
        ext[BOX_DEV + e] = own[:, cols]
        ext[2 * BOX_DEV + e] = nxt[:, cols]
    stack = jnp.concatenate(
        [own[32:40, PTS * t : PTS * t + PTS] for t in range(BOX_DEV)]
        + [jnp.zeros((PTS - 8 * BOX_DEV, PTS), F32)],
        axis=0,
    )
    turned = stack.T
    base = BOX_DEV * (group_index(dims) - 1)
    erow = lax.broadcasted_iota(jnp.int32, (16, PTS), 0)
    for t in range(BOX_DEV):
        for c in range(3):
            tpos[t, c] = TURNS * jnp.broadcast_to(
                turned[:, 8 * t + c : 8 * t + c + 1], (PTS, PTS)
            )
        m = jnp.zeros((16, PTS), F32)
        for s in range(SLOTS):
            box = jnp.where(s < count[t], near[t, s] - base, -1000)
            m = m + jnp.where(erow == box, 1.0, 0.0)
        mult[t] = m
    acc[...] = jnp.zeros_like(acc)

    def step(d, carry):
        for t in range(BOX_DEV):
            e = t + d
            rows = ext[e, 0:32, :]
            re, im = helmholtz(
                tpos[t, 0],
                tpos[t, 1],
                tpos[t, 2],
                TURNS * ext[e, 32:33, :],
                TURNS * ext[e, 33:34, :],
                TURNS * ext[e, 34:35, :],
                SCALE,
            )
            khi, klo = split(jnp.concatenate([re, im], axis=1))
            rhi, rlo = split(jnp.concatenate([rows, rotate(rows)], axis=1))
            both = dot(jnp.concatenate([rhi, rlo], axis=0), khi, 1, 1)
            part = both[0:32] + (both[32:64] + dot(rhi, klo, 1, 1))
            acc[t] += part * mult[t, pl.ds(e, 1), :]
        return carry

    lax.fori_loop(0, 2 * REACH + 1, step, 0)
    for t in range(BOX_DEV):
        cols = slice(PTS * t, PTS * t + PTS)
        acc[t] += 0.5 * jnp.concatenate([cur[3, 0, :, cols], cur[3, 1, :, cols]], axis=0)
    n = len(outs)
    for r, out in enumerate(outs):
        block = acc[lax.rem(lax.axis_index("x") + r, n)]
        if r == 0:
            out[...] = block
            continue
        for k in range(4):
            for p in range(2):
                out[32 * k + 16 * p : 32 * k + 16 * p + 16, :] = cur[k, p]
        out[PTS : PTS + 8, :] = jnp.concatenate(
            [block[8 * g : 8 * g + 8] for g in range(4)], axis=1
        )


def far_kernel(dims, info, gathered, out, tpos, rcat, weight, acc):
    nz, ny, nk, nx = dims
    targets = ny * nk
    mine = lax.axis_index("y") * nk + lax.axis_index("k")
    first = lax.axis_index("z") * targets
    stack = info[...]
    if targets * 8 < PTS:
        stack = jnp.concatenate([stack, jnp.zeros((PTS - targets * 8, PTS), F32)], axis=0)
    turned = stack.T
    for d in range(targets):
        for c in range(3):
            tpos[c, SKEL * d : SKEL * d + SKEL, :] = TURNS * jnp.broadcast_to(
                turned[0:SKEL, 8 * d + c : 8 * d + c + 1], (SKEL, PTS)
            )
    for g in range(nz):
        rows = jnp.concatenate([gathered[nz * c + g, 0:32, :] for c in range(nx)], axis=0)
        hi, lo = split(jnp.concatenate([rows, rotate(rows)], axis=1))
        rcat[g] = jnp.concatenate([hi, lo], axis=0)
    acc[...] = jnp.zeros_like(acc)
    per = min(4, targets)

    def step(g, carry):
        sx = TURNS * gathered[g, 32:33, :]
        sy = TURNS * gathered[g, 33:34, :]
        sz = TURNS * gathered[g, 34:35, :]
        source_group = g * targets + mine
        for d in range(targets):
            delta = source_group - (first + d % ny * nk + d // ny)
            w = jnp.where(delta == -1, info[8 * d + 3 : 8 * d + 4, :], 1.0)
            w = jnp.where(delta == 0, info[8 * d + 4 : 8 * d + 5, :], w)
            w = jnp.where(delta == 1, info[8 * d + 5 : 8 * d + 6, :], w)
            weight[SKEL * d : SKEL * d + SKEL, :] = jnp.broadcast_to(
                w * SCALE, (SKEL, PTS)
            )
        for n in range(targets // per):
            span = slice(SKEL * per * n, SKEL * per * (n + 1))
            re, im = helmholtz(
                tpos[0, span, :],
                tpos[1, span, :],
                tpos[2, span, :],
                sx,
                sy,
                sz,
                weight[span, :],
            )
            khi, klo = split(jnp.concatenate([re, im], axis=1))
            width = acc.shape[1]
            both = dot(khi, rcat[g], 1, 1)
            acc[span, :] += both[:, 0:width] + (
                both[:, width:] + dot(klo, rcat[g, 0:width, :], 1, 1)
            )
        return carry

    lax.fori_loop(0, nz, step, 0)
    for d in range(targets):
        out[d] = acc[SKEL * d : SKEL * d + SKEL, :]


def halves(rows, nx):
    re = jnp.concatenate([rows[32 * c : 32 * c + 16] for c in range(nx)], axis=0)
    im = jnp.concatenate([rows[32 * c + 16 : 32 * c + 32] for c in range(nx)], axis=0)
    return jnp.concatenate([re, im], axis=1)


def basis_kernel(scale, first, basis, *refs):
    others, (ordered, nears, blocks) = refs[:-3], refs[-3:]
    nx = 1 + len(others)
    for r, ref in enumerate((basis,) + others):
        c = from_x(r)
        for k in range(4):
            at = pl.ds(pl.multiple_of(16 * (nx * k + c), 16), 16)
            for p in range(2):
                ordered[p, at, :] = ref[32 * k + 16 * p : 32 * k + 16 * p + 16, :]
        block = first[...] if r == 0 else ref[PTS : PTS + 8, :]
        if r > 0:
            block = jnp.concatenate(
                [block[:, PTS * g : PTS * g + PTS] for g in range(4)], axis=0
            )
        nears[pl.ds(pl.multiple_of(32 * c, 32), 32), :] = block
    x = lax.axis_index("x")
    half = lax.rem(x, 2)

    def product(left, right, rows):
        total = None
        for p in range(2):
            a = ordered[p, pl.ds(pl.multiple_of(64 * left, 64), 64), :]
            b = ordered[p, pl.ds(pl.multiple_of(right, 32), rows), :]
            part = dot(a, b, 1, 1, HIGHEST)
            total = part if total is None else total + part
        return total * scale

    blocks[0:64, :] = jnp.concatenate(
        [product(x, 64 * x, 64), product(x, 64 * lax.rem(x + 1, nx), 64)], axis=1
    )
    far = product(half, 64 * (half + 2) + 32 * (x // 2), 32)
    blocks[64:80, :] = jnp.concatenate([far[16 * g : 16 * g + 16] for g in range(4)], axis=1)


def couple_kernel(scale, phi, interp, ordered, nears, blocks, applied, part):
    nx = nears.shape[0] // 32
    total = phi[0]
    for d in range(1, phi.shape[0]):
        total = total + phi[d]
    rows = dot(total, interp[lax.axis_index("x")], 0, 0, HIGHEST) + nears[...]
    a2 = halves(rows, nx)
    applied[...] = a2
    cols = pl.ds(pl.multiple_of(PTS * lax.axis_index("x"), PTS), PTS)
    b2 = jnp.concatenate([ordered[0, :, cols], ordered[1, :, cols]], axis=1)
    c = dot(b2, a2, 1, 1, HIGHEST) * scale
    packed = jnp.concatenate([c[0:128], c[128:256]], axis=1)
    own = dot(a2, a2, 1, 1, HIGHEST) * scale
    n = part.shape[0]
    lead = 128 // n
    for d in range(n):
        part[d, 0:lead, :] = packed[lead * d : lead * d + lead]
    rest = jnp.concatenate(
        [
            jnp.concatenate([own[0:32], own[32:64]], axis=1),
            blocks[...],
            jnp.zeros((16, PTS), F32),
        ],
        axis=0,
    )
    for e in range(part.shape[1] - lead):
        part[:, lead + e, :] = rest[n * e : n * e + n]


def finish_kernel(nx, summed, ordered, *refs):
    applied, (out, coupling, factor, inv) = refs[:-4], refs[-4:]
    n = summed.shape[0]
    lead = 128 // n
    packed = jnp.concatenate([summed[d, 0:lead, :] for d in range(n)], axis=0)
    c = jnp.concatenate([packed[:, 0:64], packed[:, 64:128]], axis=0)
    for k in range(4):
        coupling[k] = c[64 * k : 64 * k + 64]
    base = lead + 32 // n
    own = jnp.concatenate([summed[:, e, :] for e in range(lead, base)], axis=0)
    de, h = [], []
    for x in range(nx):
        rest = [summed[:, base + 80 // n * x + e, :] for e in range(80 // n)]
        rest = jnp.concatenate(rest, axis=0)
        de.append(rest[0:64])
        h.append(
            jnp.concatenate([rest[64:80, 32 * g : 32 * g + 32] for g in range(4)], axis=0)
        )
    g = jnp.concatenate([own[:, 0:64], own[:, 64:128]], axis=0)
    blocks = [c[64 * k : 64 * k + 64] for k in range(4)]
    lines = []
    for k in range(4):
        right = jnp.concatenate([0.5 * blocks[k], blocks[(k + 1) % 4]], axis=0)
        left = de[k]
        if k < 2:
            right = jnp.concatenate([right, blocks[k + 2]], axis=0)
            left = jnp.concatenate([left, h[k], h[k + 2]], axis=1)
        lines.append(dot(left, right, 1, 0, HIGHEST) - blocks[k])
    halfq = dot(c, jnp.concatenate(lines, axis=0), 0, 0, HIGHEST)
    g = g + (halfq + halfq.T)
    row = lax.broadcasted_iota(jnp.int32, (64, 64), 0)
    col = lax.broadcasted_iota(jnp.int32, (64, 64), 1)
    eye = row == col
    diag = jnp.where(eye, g, 0.0)
    trace = jnp.sum(jnp.sum(diag, axis=1, keepdims=True), axis=0, keepdims=True)
    g = g + jnp.where(eye, SHIFT_SCALE * trace / 64.0 + EPSILON, 0.0)
    m = jnp.concatenate([g, eye.astype(F32)], axis=1)
    tiles = [m[8 * i : 8 * i + 8] for i in range(8)]
    sub = lax.broadcasted_iota(jnp.int32, (8, 1), 0)
    for j in range(0, 64, PIVOTS):
        at, top = divmod(j, 8)
        live = tiles[at:]
        cols = [
            [jnp.broadcast_to(tile[:, j + n : j + n + 1], (8, PTS)) for tile in live]
            for n in range(PIVOTS)
        ]
        lines = [tiles[at][top + n : top + n + 1] for n in range(PIVOTS)]
        sm = [[cols[n][0][top + r : top + r + 1] for n in range(PIVOTS)] for r in range(PIVOTS)]
        factors = []
        for n in range(PIVOTS):
            inverse = 1.0 / sm[n][n]
            ratio = [sm[r][n] * inverse for r in range(PIVOTS)]
            factors.append(inverse)
            for r in range(n + 1, PIVOTS):
                lines[r] = lines[r] - ratio[r] * lines[n]
                for e in range(n + 1, PIVOTS):
                    sm[r][e] = sm[r][e] - ratio[r] * sm[n][e]
        for i in range(len(live)):
            bar = [cols[n][i] for n in range(PIVOTS)]
            new = live[i]
            for n in range(PIVOTS):
                f = bar[n] * factors[n]
                for r in range(n + 1, PIVOTS):
                    bar[r] = bar[r] - f * sm[n][r]
                if i == 0:
                    f = jnp.where(sub > top + n, f, 0.0)
                new = new - f * lines[n]
            tiles[at + i] = new
    m = jnp.concatenate(tiles, axis=0)
    pivots = jnp.sum(jnp.where(eye, m[:, 0:64], 0.0), axis=1, keepdims=True)
    m = m * (1.0 / jnp.sqrt(pivots))
    factor[...] = jnp.where(row <= col, m[:, 0:64], 0.0)
    inv[...] = m[:, 64:128]
    mine = inv[pl.ds(pl.multiple_of(16 * lax.axis_index("x"), 16), 16), :]
    back = dot(mine, c, 1, 1, HIGHEST)
    for p in range(2):
        out[p] = -dot(back, ordered[p], 1, 0, HIGHEST)
    for r, ref in enumerate(applied):
        rows = dot(mine, ref[...], 1, 0, HIGHEST)
        cols = pl.ds(pl.multiple_of(PTS * from_x(r), PTS), PTS)
        out[0, :, cols] += rows[:, 0:PTS]
        out[1, :, cols] += rows[:, PTS : 2 * PTS]


def around(blocks):
    n = lax.axis_size("x")
    out = [blocks[0]]
    for r in range(1, n):
        out.append(lax.ppermute(blocks[r], "x", [(i, (i + r) % n) for i in range(n)]))
    return out


def trade(value, axes):
    return lax.all_to_all(value, axes, split_axis=0, concat_axis=0, tiled=True)


def shards(dims, basis, offsets, weights, interp, skeleton, near_boxes, near_count):
    nz, ny, nk, nx = dims
    groups = nz * ny * nk
    targets = ny * nk
    sources = nz * nx
    points = BOX_DEV * PTS
    scale = 1.0 / (groups * points)
    shape = lambda *s: jax.ShapeDtypeStruct(s, F32)

    info, skelpos = call(
        functools.partial(place_kernel, dims),
        (shape(targets, 8, PTS), shape(8, PTS)),
        [SMEM, SMEM, VMEM, VMEM],
        limit=None,
    )(near_boxes, near_count, offsets, skeleton)
    info = trade(info, YK).reshape(targets * 8, PTS)
    halo, far = call(
        functools.partial(prep_kernel, dims),
        (shape(40, points), shape(sources, 40, PTS)),
        [VMEM] * 5,
        limit=None,
    )(basis, weights[None], offsets, interp, skelpos)
    prev = lax.ppermute(halo, BOX, [(g, g + 1) for g in range(groups - 1)])
    nxt = lax.ppermute(halo, BOX, [(g + 1, g) for g in range(groups - 1)])
    far_all = trade(far, ZX)

    nears = call(
        functools.partial(near_kernel, dims),
        (shape(32, PTS),) + (shape(PTS + 8, points),) * (nx - 1),
        [SMEM, SMEM] + [VMEM] * 4,
        [
            pltpu.VMEM((3 * BOX_DEV, 40, PTS), F32),
            pltpu.VMEM((BOX_DEV, 16, PTS), F32),
            pltpu.VMEM((BOX_DEV, 3, PTS, PTS), F32),
            pltpu.VMEM((BOX_DEV, 32, PTS), F32),
        ],
        flops=36 * 2 * 64 * 256 * 128 * 2,
    )(near_boxes, near_count, prev, halo, nxt, basis)
    nears = around(nears)
    ordered, near_rows, blocks = call(
        functools.partial(basis_kernel, scale),
        (shape(2, 256, points), shape(32 * nx, PTS), shape(80, PTS)),
        [VMEM] * (1 + nx),
    )(nears[0], basis.reshape(4 * 32, points), *nears[1:])

    far_part = call(
        functools.partial(far_kernel, dims),
        shape(targets, SKEL, 32 * nx),
        [VMEM] * 2,
        [
            pltpu.VMEM((3, SKEL * targets, PTS), F32),
            pltpu.VMEM((nz, 64 * nx, 2 * PTS), BF16),
            pltpu.VMEM((SKEL * targets, PTS), F32),
            pltpu.VMEM((SKEL * targets, 32 * nx), F32),
        ],
        flops=3 * 2 * 512 * 2048 * 128,
    )(info, far_all)
    phi = trade(far_part, YK)

    lead = 128 // targets
    tall = 2 * lead
    added = lead + 32 // targets
    used = added + 80 // targets
    applied, part = call(
        functools.partial(couple_kernel, scale),
        (shape(64, 2 * PTS), shape(targets, tall, PTS)),
        [VMEM] * 5,
    )(phi, interp, ordered, near_rows, blocks)
    part = jnp.sum(trade(part, YK), axis=0)
    applied = around([applied] * nx)
    part = jnp.sum(trade(jnp.broadcast_to(part[None], (nz, tall, PTS)), "z"), axis=0)
    part = trade(jnp.broadcast_to(part[None], (nx, tall, PTS)), "x")
    part = jnp.concatenate(
        [jnp.sum(part[:, :added], axis=0), part[:, added:used].reshape(nx * (used - added), PTS)],
        axis=0,
    )
    summed = trade(jnp.broadcast_to(part[None], (targets,) + part.shape), YK)

    new_block, coupling, factor = call(
        functools.partial(finish_kernel, nx),
        (shape(2, 16, points), shape(4, 64, 64), shape(64, 64)),
        [VMEM] * (2 + nx),
        [pltpu.VMEM((64, 64), F32)],
    )(summed, ordered, *applied)
    return new_block, coupling, factor


def solution(mesh):
    boxes, cols = mesh.devices.shape
    nk = GRID[2]
    ny = GRID[1] if boxes == math.prod(GRID) else 2
    nz = boxes // (ny * nk)
    dims = (nz, ny, nk, cols)
    fine = Mesh(mesh.devices.reshape(dims), ("z", "y", "k", "x"))
    return jax.shard_map(
        functools.partial(shards, dims),
        mesh=fine,
        in_specs=(
            P(None, None, "x", BOX),
            P(None, BOX),
            P(BOX),
            P(BOX, None, None),
            P(BOX, None),
            P(BOX, None),
            P(BOX),
        ),
        out_specs=(P(None, "x", BOX), P(), P()),
        check_vma=False,
    )
```
